32 devices in a mesh: row: 4 (over x, core), col: 8 (over z, y).
Axes of the slice: x: 2, y: 2, z: 4, core: 2. Of those that a mesh axis runs over, the one named last changes fastest.
Arguments:
- block_input: bfloat16 [2, 1152, 4096], P(None, 'col', 'row'), may hold values from -6 to 6
- text_tokens: bfloat16 [2, 480, 1152], P(None, 'row', 'col'), may hold values from -6 to 6
- text_length: int32 [2, 4], P(None, 'row'), may hold values from 1 to 120, as said below
- time_index: int32 [2, 4], P(None, 'row'), may hold values from 0 to 1023
- shift_table: float32 [6, 1152], P(None, 'col'), may hold values from -6 to 6
- time_table: float32 [6, 1152, 1024], P(None, 'col'), may hold values from -6 to 6
- query_weight: bfloat16 [1152, 1152], P('row', 'col'), may hold values from -0.1875 to 0.1875
- key_weight: bfloat16 [1152, 1152], P('row', 'col'), may hold values from -0.1875 to 0.1875
- value_weight: bfloat16 [1152, 1152], P('row', 'col'), may hold values from -0.1875 to 0.1875
- query_bias: float32 [1152], P('col'), may hold values from -4 to 4
- value_bias: float32 [1152], P('col'), may hold values from -4 to 4
- out_weight: bfloat16 [1152, 1152], P('col', 'row'), may hold values from -0.75 to 0.75
- out_bias: float32 [1152], P('col'), may hold values from -4 to 4
- cross_query: bfloat16 [1152, 1152], P('row', 'col'), may hold values from -0.1875 to 0.1875
- cross_key: bfloat16 [1152, 1152], P('row', 'col'), may hold values from -0.1875 to 0.1875
- cross_value: bfloat16 [1152, 1152], P('row', 'col'), may hold values from -0.1875 to 0.1875
- cross_query_bias: float32 [1152], P('col'), may hold values from -4 to 4
- cross_value_bias: float32 [1152], P('col'), may hold values from -4 to 4
- cross_out: bfloat16 [1152, 1152], P('col', 'row'), may hold values from -0.5 to 0.5
- cross_out_bias: float32 [1152], P('col'), may hold values from -4 to 4
- up_weight: bfloat16 [1152, 4608], P('row', 'col'), may hold values from -0.1875 to 0.1875
- up_bias: float32 [4608], P('col'), may hold values from -4 to 4
- down_weight: bfloat16 [4608, 1152], P('col', 'row'), may hold values from -0.09375 to 0.09375
- down_bias: float32 [1152], P('col'), may hold values from -4 to 4
- out_grad: bfloat16 [2, 1152, 4096], P(None, 'col', 'row'), may hold values from -6 to 6
Outputs:
- block_output: float32 [2, 1152, 4096], P(None, 'col', 'row')
- grad_input: float32 [2, 1152, 4096], P(None, 'col', 'row')
- grad_text: float32 [2, 480, 1152], P(None, 'row', 'col')
- grad_shift_table: float32 [6, 1152], P(None, 'col')
- grad_time_table: float32 [6, 1152, 1024], P(None, 'col')
- grad_query_weight: float32 [1152, 1152], P('row', 'col')
- grad_key_weight: float32 [1152, 1152], P('row', 'col')
- grad_value_weight: float32 [1152, 1152], P('row', 'col')
- grad_query_bias: float32 [1152], P('col')
- grad_value_bias: float32 [1152], P('col')
- grad_out_weight: float32 [1152, 1152], P('col', 'row')
- grad_out_bias: float32 [1152], P('col')
- grad_cross_query: float32 [1152, 1152], P('row', 'col')
- grad_cross_key: float32 [1152, 1152], P('row', 'col')
- grad_cross_value: float32 [1152, 1152], P('row', 'col')
- grad_cross_query_bias: float32 [1152], P('col')
- grad_cross_value_bias: float32 [1152], P('col')
- grad_cross_out: float32 [1152, 1152], P('col', 'row')
- grad_cross_out_bias: float32 [1152], P('col')
- grad_up_weight: float32 [1152, 4608], P('row', 'col')
- grad_up_bias: float32 [4608], P('col')
- grad_down_weight: float32 [4608, 1152], P('col', 'row')
- grad_down_bias: float32 [1152], P('col')
The draws below stay inside these ranges and needn't reach their ends.
Inputs may be any that keep to these rules, and one draw needn't show every extreme that they name: Caption keys at positions text_length and beyond are masked; in each micro-batch one latent has all 120 text tokens and another has one.
All inputs are finite; a program needn't handle non-finite values.
Results may differ from the reference program's by a relative error of at most 0.02.
Values may be sent and summed in bfloat16 or wider, within the bound.
A program may use at most 192 MiB of HBM per device.

```python
import jax
import jax.numpy as jnp
from jax import lax

D = 1152
HEADS = 16
FF = 4608
NSTEP = 1024
TXT = 120
LENGTH = 1024
MICRO = 2
HD = 72
LAT_MB = 4
TOKENS = 4096
TEXTS = 480


def draw_text_length(key, part):
    lengths = jax.random.randint(key, (MICRO, LAT_MB), 1, TXT + 1)
    column_ids = jnp.arange(LAT_MB, dtype=jnp.int32)[None, :]
    top_place = jax.random.randint(jax.random.fold_in(key, 1), (MICRO, 1), 0, LAT_MB)
    offset_place = jax.random.randint(jax.random.fold_in(key, 2), (MICRO, 1), 0, LAT_MB - 1)
    bottom_place = (top_place + 1 + offset_place) % LAT_MB
    lengths = jnp.where(column_ids == top_place, TXT, lengths)
    lengths = jnp.where(column_ids == bottom_place, 1, lengths)
    return lengths.astype(jnp.int32)


def with_ends(values, stream_key, low, high):
    longest = values.shape.index(max(values.shape))
    spots = []
    for shift in (0, 1):
        where = [jax.random.randint(jax.random.fold_in(stream_key, axis), (), 0, length) for axis, length in enumerate(values.shape)]
        where[longest] = (where[longest] + shift) % values.shape[longest]
        spots.append(tuple(where))
    return values.at[spots[0]].set(low).at[spots[1]].set(high)


def level_of(rng, extent, split, least, high):
    def one(axis_at, parts):
        heights = jax.random.uniform(jax.random.fold_in(jax.random.fold_in(rng, 6), axis_at), (parts,), jnp.float32, least / len(split), high / len(split))
        return jnp.repeat(jnp.exp(heights), extent[axis_at] // parts).reshape((-1,) + (1,) * (len(extent) - axis_at - 1))

    loudness = one(*split[0])
    for cut in split[1:]:
        loudness = loudness * one(*cut)
    return loudness


def normal_values(key, shape, scale, most, cuts=(), held_as=jnp.bfloat16):
    values = jax.random.normal(key, shape, jnp.float32) * scale
    if len(cuts) > 0:
        values = level_of(key, shape, cuts, -0.22, 0.18) * values
    return jnp.clip(values, min=-most, max=most).astype(held_as)


def setup_inputs(seed: int = 0) -> dict:
    arg_keys = jax.random.split(jax.random.key(seed), 26)
    return {
        "block_input": normal_values(arg_keys[0], (MICRO, D, TOKENS), 1.0, 6.0, ((1, 8), (2, 4))),
        "text_tokens": normal_values(arg_keys[1], (MICRO, TEXTS, D), 1.0, 6.0, ((1, 4), (2, 8))),
        "text_length": draw_text_length(jax.random.fold_in(arg_keys[25], 71), 0),
        "time_index": with_ends(jax.random.randint(arg_keys[3], (MICRO, LAT_MB), 0, NSTEP), jax.random.fold_in(arg_keys[3], 1), 0, NSTEP - 1).astype(jnp.int32),
        "shift_table": normal_values(arg_keys[4], (6, D), 0.4, 6.0, ((1, 8),), jnp.float32),
        "time_table": normal_values(arg_keys[5], (6, D, NSTEP), 0.4, 6.0, ((1, 8),), jnp.float32),
        "query_weight": normal_values(arg_keys[6], (D, D), D ** -0.5, 0.1875, ((0, 4), (1, 8))),
        "key_weight": normal_values(arg_keys[7], (D, D), D ** -0.5, 0.1875, ((0, 4), (1, 8))),
        "value_weight": normal_values(arg_keys[8], (D, D), D ** -0.5, 0.1875, ((0, 4), (1, 8))),
        "query_bias": normal_values(arg_keys[9], (D,), 0.3, 4.0, ((0, 8),), jnp.float32),
        "value_bias": normal_values(arg_keys[10], (D,), 0.3, 4.0, ((0, 8),), jnp.float32),
        "out_weight": normal_values(arg_keys[11], (D, D), (D // 16) ** -0.5, 0.75, ((0, 8), (1, 4))),
        "out_bias": normal_values(arg_keys[12], (D,), 0.3, 4.0, ((0, 8),), jnp.float32),
        "cross_query": normal_values(arg_keys[13], (D, D), D ** -0.5, 0.1875, ((0, 4), (1, 8))),
        "cross_key": normal_values(arg_keys[14], (D, D), D ** -0.5, 0.1875, ((0, 4), (1, 8))),
        "cross_value": normal_values(arg_keys[15], (D, D), D ** -0.5, 0.1875, ((0, 4), (1, 8))),
        "cross_query_bias": normal_values(arg_keys[16], (D,), 0.3, 4.0, ((0, 8),), jnp.float32),
        "cross_value_bias": normal_values(arg_keys[17], (D,), 0.3, 4.0, ((0, 8),), jnp.float32),
        "cross_out": normal_values(arg_keys[18], (D, D), (D // 8) ** -0.5, 0.5, ((0, 8), (1, 4))),
        "cross_out_bias": normal_values(arg_keys[19], (D,), 0.3, 4.0, ((0, 8),), jnp.float32),
        "up_weight": normal_values(arg_keys[20], (D, FF), D ** -0.5, 0.1875, ((0, 4), (1, 8))),
        "up_bias": normal_values(arg_keys[21], (FF,), 0.3, 4.0, ((0, 8),), jnp.float32),
        "down_weight": normal_values(arg_keys[22], (FF, D), FF ** -0.5, 0.09375, ((0, 8), (1, 4))),
        "down_bias": normal_values(arg_keys[23], (D,), 0.3, 4.0, ((0, 8),), jnp.float32),
        "out_grad": normal_values(arg_keys[24], (MICRO, D, TOKENS), 1.0, 6.0, ((1, 8), (2, 4))),
    }


@jax.custom_vjp
def low(v):
    return lax.optimization_barrier(v.astype(jnp.bfloat16)).astype(jnp.float32)

@jax.custom_vjp
def low_back(v):
    return v

def low_keep(v):
    return (low(v), None)

def low_pass(kept, grad):
    return (grad,)

def back_keep(v):
    return (v, None)

def back_low(kept, grad):
    return (low(grad),)
low.defvjp(low_keep, low_pass)
low_back.defvjp(back_keep, back_low)
NORM_EPS = 1e-06
MASK_FILL = -1e+30

def round_both(value):
    return low(low_back(value))

def product(first_op, second_op):
    return jnp.dot(first_op, second_op, precision=lax.Precision.HIGHEST, preferred_element_type=jnp.float32)

def layer_norm(value):
    average = lax.optimization_barrier(jnp.mean(value, axis=-1, keepdims=True))
    centered = value - average
    variance = lax.optimization_barrier(jnp.mean(centered * centered, axis=-1, keepdims=True))
    return centered * lax.rsqrt(variance + NORM_EPS)

def attend(queries, key_rows, values_in, key_valid):
    q_heads = queries.reshape(queries.shape[0], HEADS, HD)
    k_heads = key_rows.reshape(key_rows.shape[0], HEADS, HD)
    v_heads = values_in.reshape(values_in.shape[0], HEADS, HD)
    scores = low_back(jnp.einsum('qhd,khd->hqk', q_heads, k_heads, precision=lax.Precision.HIGHEST)) * HD ** (-0.5)
    if key_valid is not None:
        scores = jnp.where(key_valid[None, None, :], scores, MASK_FILL)
    attn_probs = jax.nn.softmax(scores, axis=-1)
    attn_out = jnp.einsum('hqk,khd->qhd', low(attn_probs), v_heads, precision=lax.Precision.HIGHEST)
    return round_both(attn_out.reshape(queries.shape[0], D))

def forward(param_set, latent_x, caption, length_l, step_l):
    shift_table, time_table, query_weight, key_weight, value_weight, query_bias, value_bias, out_weight, out_bias, cross_query, cross_key, cross_value, cross_query_bias, cross_value_bias, cross_out, cross_out_bias, up_weight, up_bias, down_weight, down_bias = param_set
    modulation = shift_table + time_table[:, :, step_l]
    attn_in = low(layer_norm(latent_x) * (1.0 + modulation[1]) + modulation[0])
    queries = round_both(product(attn_in, query_weight) + query_bias)
    key_rows = round_both(product(attn_in, key_weight))
    values_s = round_both(product(attn_in, value_weight) + value_bias)
    attn_out = attend(queries, key_rows, values_s, None)
    attn_branch = low_back(product(attn_out, out_weight)) + out_bias
    after_attn = latent_x + modulation[2] * attn_branch
    cross_in = low(after_attn)
    cross_q = round_both(product(cross_in, cross_query) + cross_query_bias)
    cross_k = round_both(product(caption, cross_key))
    cross_v = round_both(product(caption, cross_value) + cross_value_bias)
    key_valid = jnp.arange(TXT, dtype=jnp.int32) < length_l
    cross_att = attend(cross_q, cross_k, cross_v, key_valid)
    after_cross = after_attn + low_back(product(cross_att, cross_out)) + cross_out_bias
    mlp_in = low(layer_norm(after_cross) * (1.0 + modulation[4]) + modulation[3])
    hidden_pre = low_back(product(mlp_in, up_weight) + up_bias)
    hidden_act = low(jax.nn.gelu(hidden_pre, approximate=True))
    mlp_branch = low_back(product(hidden_act, down_weight)) + down_bias
    return after_cross + modulation[5] * mlp_branch

def reference(block_input, text_tokens, text_length, time_index, shift_table, time_table, query_weight, key_weight, value_weight, query_bias, value_bias, out_weight, out_bias, cross_query, cross_key, cross_value, cross_query_bias, cross_value_bias, cross_out, cross_out_bias, up_weight, up_bias, down_weight, down_bias, out_grad):
    params = tuple((weight.astype(jnp.float32) for weight in (shift_table, time_table, query_weight, key_weight, value_weight, query_bias, value_bias, out_weight, out_bias, cross_query, cross_key, cross_value, cross_query_bias, cross_value_bias, cross_out, cross_out_bias, up_weight, up_bias, down_weight, down_bias)))
    inputs_x = jnp.transpose(block_input.astype(jnp.float32), (0, 2, 1)).reshape(MICRO * LAT_MB, LENGTH, D)
    captions = text_tokens.astype(jnp.float32).reshape(MICRO * LAT_MB, TXT, D)
    cotangents = jnp.transpose(out_grad.astype(jnp.float32), (0, 2, 1)).reshape(MICRO * LAT_MB, LENGTH, D)
    lengths = text_length.reshape(MICRO * LAT_MB).astype(jnp.int32)
    steps_all = time_index.reshape(MICRO * LAT_MB).astype(jnp.int32)

    def latent_step(totals, inputs_l):
        latent_x, caption, cotangent, length_l, step_l = inputs_l

        def forward_l(param_set, x_in, text_in):
            return forward(param_set, x_in, text_in, length_l, step_l)
        result, pullback = jax.vjp(forward_l, params, latent_x, caption)
        grad_params, grad_latent, grad_caption = pullback(cotangent)
        totals = jax.tree.map(lambda earlier, added: earlier + added, totals, grad_params)
        return (totals, (result, grad_latent, grad_caption))
    zero_set = tuple((jnp.zeros(weight.shape, jnp.float32) for weight in params))
    totals, (results, grad_xs, grad_caps) = lax.scan(latent_step, zero_set, (inputs_x, captions, cotangents, lengths, steps_all))
    g_shift, g_time, g_query, g_key, g_value, g_qbias, g_vbias, g_out, g_obias, g_cquery, g_ckey, g_cvalue, g_cqbias, g_cvbias, g_cout, g_cobias, g_up, g_upbias, g_down, g_downbias = totals
    results = jnp.transpose(results.reshape(MICRO, LAT_MB * LENGTH, D), (0, 2, 1))
    grad_xs = jnp.transpose(grad_xs.reshape(MICRO, LAT_MB * LENGTH, D), (0, 2, 1))
    return (results, grad_xs, grad_caps.reshape(MICRO, LAT_MB * TXT, D), g_shift, g_time, g_query, g_key, g_value, g_qbias, g_vbias, g_out, g_obias, g_cquery, g_ckey, g_cvalue, g_cqbias, g_cvbias, g_cout, g_cobias, g_up, g_upbias, g_down, g_downbias)
```

```python
import jax
import jax.numpy as jnp
from jax import lax
from jax.sharding import PartitionSpec as P

D = 1152
HEADS = 16
HD = 72

NORM_EPS = 1e-06
MASK_FILL = -1e30
BF = jnp.bfloat16
F32 = jnp.float32


def dot_nn(a, b):
    return lax.dot_general(a, b, (((1,), (0,)), ((), ())), preferred_element_type=F32)


def dot_tn(a, b):
    return lax.dot_general(a, b, (((0,), (0,)), ((), ())), preferred_element_type=F32)


def dot_nt(a, b):
    return lax.dot_general(a, b, (((1,), (1,)), ((), ())), preferred_element_type=F32)


def after(value, *deps):
    return lax.optimization_barrier((value,) + deps)[0]


def bit_reverse(value, bits):
    out = 0
    for b in range(bits):
        out = out | (((value >> b) & 1) << (bits - 1 - b))
    return out


def row_swap(value, rows, bit):
    return lax.ppermute(value, "row", [(i, i ^ bit) for i in range(rows)])


def col_swap(value, cols, mask):
    return lax.ppermute(value, "col", [(i, i ^ mask) for i in range(cols)])


def layer_norm(resid):
    mean = jnp.mean(resid, axis=0, keepdims=True)
    centered = resid - mean
    var = jnp.mean(centered * centered, axis=0, keepdims=True)
    inv = lax.rsqrt(var + NORM_EPS)
    return centered * inv, inv


def norm_backward(grad, normed, inv, scale):
    dn = grad * (1.0 + scale)
    first = jnp.mean(dn, axis=0, keepdims=True)
    second = jnp.mean(dn * normed, axis=0, keepdims=True)
    back = (dn - first - normed * second) * inv
    return back, jnp.sum(grad, axis=1), jnp.sum(grad * normed, axis=1)


def attend_forward(q_t, k_t, v_t, valid):
    heads = q_t.shape[0] // HD
    q3, k3, v3 = (a.reshape(heads, HD, a.shape[1]) for a in (q_t, k_t, v_t))
    s = jnp.einsum("hdk,hdq->hkq", k3, q3, preferred_element_type=F32) * HD ** -0.5
    if valid is not None:
        s = jnp.where(valid[None, :, None], s, MASK_FILL)
    top = jnp.max(s, axis=1, keepdims=True)
    lse = top + jnp.log(jnp.sum(jnp.exp(s - top), axis=1, keepdims=True))
    p = jnp.exp(s - lse).astype(BF)
    out = jnp.einsum("hdk,hkq->hdq", v3, p, preferred_element_type=F32)
    return out.reshape(q_t.shape).astype(BF), lse


def attend_backward(q_t, k_t, v_t, valid, lse, do_t):
    heads = q_t.shape[0] // HD
    q3, k3, v3, do3 = (a.reshape(heads, HD, a.shape[1]) for a in (q_t, k_t, v_t, do_t))
    s = jnp.einsum("hdk,hdq->hkq", k3, q3, preferred_element_type=F32) * HD ** -0.5
    if valid is not None:
        s = jnp.where(valid[None, :, None], s, MASK_FILL)
    p = jnp.exp(s - lse)
    dv = jnp.einsum("hdq,hkq->hdk", do3, p.astype(BF), preferred_element_type=F32)
    dp = jnp.einsum("hdk,hdq->hkq", v3, do3, preferred_element_type=F32)
    ds = p * (dp - jnp.sum(dp * p, axis=1, keepdims=True))
    ds = (ds * HD ** -0.5).astype(BF)
    dq = jnp.einsum("hdk,hkq->hdq", k3, ds, preferred_element_type=F32)
    dk = jnp.einsum("hdq,hkq->hdk", q3, ds, preferred_element_type=F32)
    return dq.reshape(q_t.shape).astype(BF), dk.reshape(k_t.shape).astype(BF), dv.reshape(k_t.shape).astype(BF)


def shards(
    block_input,
    text_tokens,
    text_length,
    time_index,
    shift_table,
    time_table,
    query_weight,
    key_weight,
    value_weight,
    query_bias,
    value_bias,
    out_weight,
    out_bias,
    cross_query,
    cross_key,
    cross_value,
    cross_query_bias,
    cross_value_bias,
    cross_out,
    cross_out_bias,
    up_weight,
    up_bias,
    down_weight,
    down_bias,
    out_grad,
):
    rows, cols = lax.axis_size("row"), lax.axis_size("col")
    r, c = lax.axis_index("row"), lax.axis_index("col")
    row_bits = rows.bit_length() - 1
    half = cols // 2
    feat = block_input.shape[1]
    chunk = D // rows
    width = 2 * block_input.shape[2] // cols
    texts = text_tokens.shape[1]
    steps = time_table.shape[2]
    ups = up_bias.shape[0]
    core, low_z, micro = r & 1, (c >> 1) & 1, c // half
    home_row = (r - core) | low_z
    at_home = core == low_z
    r_rev = bit_reverse(r, row_bits)

    kv_masks = [1 << b for b in range(2, cols.bit_length() - 2)]
    swap_pairs = []
    for i in range(rows):
        for j in range(cols):
            swap_pairs.append(
                (i * cols + j, ((i & ~1) | ((j >> 1) & 1)) * cols + ((j & ~2) | ((i & 1) << 1)))
            )

    def place_swap(value):
        return lax.ppermute(value, ("row", "col"), swap_pairs)

    def to_local(value):
        parts = value.reshape((rows, chunk) + value.shape[1:])
        picked = [
            lax.dynamic_index_in_dim(parts, r ^ bit_reverse(i, row_bits), 0, keepdims=False)
            for i in range(rows)
        ]
        return jnp.concatenate(picked, axis=0)

    def to_natural(value):
        parts = value.reshape((rows, chunk) + value.shape[1:])
        picked = [
            lax.dynamic_index_in_dim(parts, r_rev ^ bit_reverse(i, row_bits), 0, keepdims=False)
            for i in range(rows)
        ]
        return jnp.concatenate(picked, axis=0)

    def tokens_in(value):
        blocks = value.reshape(2, feat, half, width).transpose(0, 2, 1, 3).reshape(cols, feat, width)
        blocks = lax.all_to_all(blocks, "col", 0, 0, tiled=True)
        return to_local(place_swap(blocks.reshape(D, width)))

    def tokens_out(value):
        blocks = place_swap(to_natural(value.astype(BF))).reshape(cols, feat, width)
        blocks = lax.all_to_all(blocks, "col", 0, 0, tiled=True)
        blocks = blocks.reshape(2, half, feat, width).transpose(0, 2, 1, 3)
        return blocks.reshape(2, feat, half * width).astype(F32)

    def gather_pair(value):
        return jnp.concatenate([value, col_swap(value, cols, 1)], axis=1)

    def reduce_pair(value):
        own, other = value[:, :width], value[:, width:]
        return own + col_swap(other.astype(BF), cols, 1).astype(F32)

    def gather_keys(value):
        parts = [value]
        parts = parts + [row_swap(p, rows, 1) for p in parts]
        for mask in kv_masks:
            parts = parts + [col_swap(p, cols, mask) for p in parts]
        return jnp.concatenate(parts, axis=1)

    def reduce_keys(value):
        for mask in reversed(kv_masks):
            h = value.shape[1] // 2
            value = (value[:, :h].astype(F32) + col_swap(value[:, h:], cols, mask).astype(F32)).astype(BF)
        h = value.shape[1] // 2
        return (value[:, :h].astype(F32) + row_swap(value[:, h:], rows, 1).astype(F32)).astype(BF)

    row_order = [1 << b for b in reversed(range(row_bits))]

    def gather_weights(shards_w, gate):
        sizes = [w.shape[1] for w in shards_w]
        flat = jnp.concatenate(shards_w, axis=1) if len(shards_w) > 1 else shards_w[0]
        if gate is not None:
            flat = after(flat, gate)
        near = [flat] + [col_swap(flat, cols, e << 1) for e in range(1, half)]
        z_gate = near[-1]
        pieces, start = [], 0
        for size in sizes:
            pieces += [p[:, start : start + size] for p in near]
            start += size
        parts = [jnp.concatenate(pieces, axis=1)]
        for bit in row_order:
            parts = parts + [row_swap(p, rows, bit) for p in parts]
        full = jnp.concatenate(parts, axis=0)
        out, start = [], 0
        for size in sizes:
            out.append(full[:, start : start + size * half])
            start += size * half
        return full, out, z_gate

    def reduce_weights(left, right, sizes):
        end = D
        received = []
        for bit in reversed(row_order):
            start = end // 2
            part = dot_nt(left[start:end], right)
            for piece in received:
                part = part + piece[start:end].astype(F32)
            received.append(row_swap(part.astype(BF), rows, bit))
            end = start
        own = dot_nt(left[:end], right)
        for piece in received:
            own = own + piece[:end].astype(F32)
        groups, start = [], 0
        for size in sizes:
            groups.append([own[:, start + e * size : start + (e + 1) * size] for e in range(half)])
            start += size * half
        total = jnp.concatenate([g[0] for g in groups], axis=1) if len(groups) > 1 else groups[0][0]
        for e in range(1, half):
            sent = [g[e].astype(BF) for g in groups]
            sent = jnp.concatenate(sent, axis=1) if len(sent) > 1 else sent[0]
            total = total + col_swap(sent, cols, e << 1).astype(F32)
        out, start = [], 0
        for size in sizes:
            out.append(total[:, start : start + size])
            start += size
        return out

    qkv_w, _, gate_one = gather_weights([query_weight, key_weight, value_weight], None)
    _, (out_w, cq_w, ck_w, cv_w, cout_w), gate_two = gather_weights(
        [out_weight.T, cross_query, cross_key, cross_value, cross_out.T], gate_one
    )
    up_w, _, gate_three = gather_weights([up_weight], gate_two)
    down_w, _, _ = gather_weights([down_weight.T], gate_three)

    lengths_steps = lax.all_gather(jnp.stack([text_length[:, 0], time_index[:, 0]]), "row")
    length = lengths_steps[home_row, 0, micro]
    step_all = lengths_steps[:, 1, :].T.reshape(2 * rows)
    step_ids = jnp.arange(steps, dtype=jnp.int32)
    onehot = (time_index[:, 0][:, None] == step_ids[None, :]).astype(F32)
    modulation = lax.dot_general(
        onehot,
        time_table.reshape(6 * feat, steps),
        (((1,), (1,)), ((), ())),
        precision=lax.Precision.HIGHEST,
        preferred_element_type=F32,
    ).reshape(2, 6, feat) + shift_table[None]
    small = jnp.concatenate(
        [
            modulation.reshape(12, feat),
            out_bias[None],
            cross_out_bias[None],
            down_bias[None],
            query_bias[None],
            value_bias[None],
            cross_query_bias[None],
            cross_value_bias[None],
            up_bias.reshape(ups // feat, feat),
        ],
        axis=0,
    )
    small = lax.all_gather(small, "col")
    mods = small[:, :12].transpose(1, 0, 2).reshape(2, 6, D)
    mods = lax.dynamic_index_in_dim(mods, micro, 0, keepdims=False)
    mods = jnp.where(at_home, mods, row_swap(mods, rows, 1))
    model_rows = jnp.concatenate([mods, small[:, 12:15].transpose(1, 0, 2).reshape(3, D)], axis=0)
    model_rows = to_local(model_rows.T)
    shift_a, scale_a, gate_a, shift_m, scale_m, gate_m, out_b, cout_b, down_b = (
        model_rows[:, i : i + 1] for i in range(9)
    )
    col_rows = [
        lax.dynamic_index_in_dim(small, c ^ (e << 1), 0, keepdims=False)[15:] for e in range(half)
    ]
    col_rows = jnp.stack(col_rows, axis=1)
    q_b, v_b, cq_b, cv_b = (col_rows[i].reshape(half * feat, 1) for i in range(4))
    up_b = col_rows[4:].transpose(1, 0, 2).reshape(half * ups, 1)

    text_blocks = text_tokens.transpose(0, 2, 1)
    text_t = lax.all_to_all(jnp.repeat(text_blocks, half, axis=0), "col", 0, 0, tiled=True).reshape(D, texts)
    text_t = to_local(jnp.where(at_home, text_t, row_swap(text_t, rows, 1)))
    valid = jnp.arange(texts, dtype=jnp.int32) < length

    resid = tokens_in(block_input).astype(F32)
    cot = tokens_in(out_grad).astype(F32)
    normed_a, inv_a = layer_norm(resid)
    attn_full = gather_pair((normed_a * (1.0 + scale_a) + shift_a).astype(BF))
    heads_w = half * feat
    qkv_bias = jnp.concatenate([q_b, jnp.zeros_like(q_b), v_b], axis=0)
    qkv = (dot_tn(qkv_w, attn_full) + qkv_bias).astype(BF)
    q_t = qkv[:heads_w]
    kv_t = gather_keys(qkv[heads_w:])
    k_t, v_t = kv_t[:heads_w], kv_t[heads_w:]
    att, lse = attend_forward(q_t, k_t, v_t, None)
    branch_a = reduce_pair(dot_nn(out_w, att)) + out_b
    after_attn = resid + gate_a * branch_a
    cross_full = gather_pair(after_attn.astype(BF))
    cq_t = (dot_tn(cq_w, cross_full) + cq_b).astype(BF)
    ck_t = dot_tn(ck_w, text_t).astype(BF)
    cv_t = (dot_tn(cv_w, text_t) + cv_b).astype(BF)
    catt, clse = attend_forward(cq_t, ck_t, cv_t, valid)
    after_cross = after_attn + reduce_pair(dot_nn(cout_w, catt)) + cout_b
    normed_m, inv_m = layer_norm(after_cross)
    mlp_full = gather_pair((normed_m * (1.0 + scale_m) + shift_m).astype(BF))
    hidden_pre = dot_tn(up_w, mlp_full) + up_b
    hidden_val, gelu_pull = jax.vjp(lambda v: jax.nn.gelu(v, approximate=True), hidden_pre)
    hidden = hidden_val.astype(BF)
    branch_m = reduce_pair(dot_nn(down_w, hidden)) + down_b
    block_output = tokens_out(after_cross + gate_m * branch_m)

    grad_mlp = gate_m * cot
    low_full = gather_pair(grad_mlp.astype(BF))
    g_down_b = jnp.sum(grad_mlp, axis=1)
    g_gate_m = jnp.sum(cot * branch_m, axis=1)
    grad_pre = gelu_pull(dot_tn(down_w, low_full))[0].astype(BF)
    (g_down,) = reduce_weights(low_full, hidden, [ups])
    back_in = reduce_pair(dot_nn(up_w, grad_pre))
    (g_up,) = reduce_weights(mlp_full, grad_pre, [ups])
    g_up_b = jnp.sum(grad_pre.astype(F32), axis=1)
    back_m, g_shift_m, g_scale_m = norm_backward(back_in, normed_m, inv_m, scale_m)
    grad_cross = cot + back_m
    g_cout_b = jnp.sum(grad_cross, axis=1)
    low_cross = gather_pair(grad_cross.astype(BF))
    dcatt = dot_tn(cout_w, low_cross).astype(BF)
    dcq, dck, dcv = attend_backward(cq_t, ck_t, cv_t, valid, clse, dcatt)
    g_cq_b = jnp.sum(dcq.astype(F32), axis=1)
    g_cv_b = jnp.sum(dcv.astype(F32), axis=1)
    grad_res = grad_cross + reduce_pair(dot_nn(cq_w, dcq))
    grad_text = to_natural(dot_nn(ck_w, dck) + dot_nn(cv_w, dcv)).astype(BF)
    grad_text = grad_text.astype(F32) + row_swap(grad_text, rows, 1).astype(F32)
    grad_text = jnp.where(at_home, grad_text, 0.0).astype(BF).reshape(cols, feat, texts)
    grad_text = lax.all_to_all(grad_text, "col", 0, 0, tiled=True)
    grad_text = jnp.sum(grad_text.reshape(2, half, feat, texts).astype(F32), axis=1).transpose(0, 2, 1)
    (g_cout,) = reduce_weights(low_cross, catt, [feat])
    (g_cq,) = reduce_weights(cross_full, dcq, [feat])
    g_ck, g_cv = reduce_weights(text_t, jnp.concatenate([dck, dcv], axis=0), [feat, feat])
    g_gate_a = jnp.sum(grad_res * branch_a, axis=1)
    grad_attn = gate_a * grad_res
    g_out_b = jnp.sum(grad_attn, axis=1)
    low_attn = gather_pair(grad_attn.astype(BF))
    datt = dot_tn(out_w, low_attn).astype(BF)
    dq, dk, dv = attend_backward(q_t, k_t, v_t, None, lse, datt)
    (g_out,) = reduce_weights(low_attn, att, [feat])
    dkv = reduce_keys(jnp.concatenate([dk, dv], axis=0))
    dqkv = jnp.concatenate([dq, dkv], axis=0)
    g_q, g_k, g_v = reduce_weights(attn_full, dqkv, [feat, feat, feat])
    g_q_b = jnp.sum(dq.astype(F32), axis=1)
    g_v_b = jnp.sum(dkv[heads_w:].astype(F32), axis=1)
    back_a, g_shift_a, g_scale_a = norm_backward(
        reduce_pair(dot_nn(qkv_w, dqkv)), normed_a, inv_a, scale_a
    )
    grad_input = tokens_out(grad_res + back_a)

    model_g = jnp.stack(
        [g_shift_a, g_scale_a, g_gate_a, g_shift_m, g_scale_m, g_gate_m, g_out_b, g_cout_b, g_down_b], axis=1
    )
    model_g = to_natural(model_g).T.reshape(9, cols, feat).transpose(1, 0, 2)
    per_col = ups // feat
    col_g = jnp.concatenate(
        [g.reshape(half, 1, feat) for g in (g_q_b, g_v_b, g_cq_b, g_cv_b)] + [g_up_b.reshape(half, per_col, feat)],
        axis=1,
    )
    side = c & 1
    blocks = []
    for j in range(cols):
        part = lax.dynamic_index_in_dim(col_g, (j >> 1) ^ (c >> 1), 0, keepdims=False)
        blocks.append(jnp.where(side == (j & 1), part, 0.0))
    small_g = jnp.concatenate([model_g, jnp.stack(blocks)], axis=1)
    small_g = lax.all_to_all(small_g, "col", 0, 0, tiled=True)
    mod_g = small_g[:, :6].reshape(2, cols // 8, 2, 2, 6, feat).sum(axis=(1, 3))
    bias_g = small_g[:, 6:].sum(axis=0)
    small_g = lax.all_gather(jnp.concatenate([mod_g.reshape(24, feat), bias_g], axis=0), "row")
    mod_g = small_g[:, :24].reshape(rows // 2, 2, 2, 2, 6, feat).sum(axis=1)
    mod_g = mod_g.transpose(1, 0, 2, 3, 4).reshape(2 * rows, 6, feat)
    bias_g = small_g[:, 24:].sum(axis=0)
    g_shift = mod_g.sum(axis=0)
    onehot_all = (step_all[:, None] == step_ids[None, :]).astype(F32)
    g_time = lax.dot_general(
        mod_g.reshape(2 * rows, 6 * feat),
        onehot_all,
        (((0,), (0,)), ((), ())),
        precision=lax.Precision.HIGHEST,
        preferred_element_type=F32,
    ).reshape(6, feat, steps)
    g_out_b, g_cout_b, g_down_b, g_q_b, g_v_b, g_cq_b, g_cv_b = (bias_g[i] for i in range(7))
    g_up_b = bias_g[7:].reshape(ups)
    return (
        block_output,
        grad_input,
        grad_text,
        g_shift,
        g_time,
        g_q,
        g_k,
        g_v,
        g_q_b,
        g_v_b,
        g_out.T,
        g_out_b,
        g_cq,
        g_ck,
        g_cv,
        g_cq_b,
        g_cv_b,
        g_cout.T,
        g_cout_b,
        g_up,
        g_up_b,
        g_down.T,
        g_down_b,
    )


def solution(mesh):
    return jax.shard_map(
        shards,
        mesh=mesh,
        in_specs=(
            P(None, "col", "row"),
            P(None, "row", "col"),
            P(None, "row"),
            P(None, "row"),
            P(None, "col"),
            P(None, "col", None),
            P("row", "col"),
            P("row", "col"),
            P("row", "col"),
            P("col"),
            P("col"),
            P("col", "row"),
            P("col"),
            P("row", "col"),
            P("row", "col"),
            P("row", "col"),
            P("col"),
            P("col"),
            P("col", "row"),
            P("col"),
            P("row", "col"),
            P("col"),
            P("col", "row"),
            P("col"),
            P(None, "col", "row"),
        ),
        out_specs=(
            P(None, "col", "row"),
            P(None, "col", "row"),
            P(None, "row", "col"),
            P(None, "col"),
            P(None, "col", None),
            P("row", "col"),
            P("row", "col"),
            P("row", "col"),
            P("col"),
            P("col"),
            P("col", "row"),
            P("col"),
            P("row", "col"),
            P("row", "col"),
            P("row", "col"),
            P("col"),
            P("col"),
            P("col", "row"),
            P("col"),
            P("row", "col"),
            P("col"),
            P("col", "row"),
            P("col"),
        ),
        check_vma=False,
    )
```

```python
import functools

import jax
import jax.numpy as jnp
from jax import lax
from jax.experimental import pallas as pl
from jax.experimental.pallas import tpu as pltpu
from jax.sharding import PartitionSpec as P

D = 1152
HEADS = 16
HD = 72

NORM_EPS = 1e-06
MASK_FILL = -1e30
BF = jnp.bfloat16
F32 = jnp.float32
LOG_SCALE = HD ** -0.5 * 1.4426950408889634


def dot_nn(a, b):
    return lax.dot_general(a, b, (((1,), (0,)), ((), ())), preferred_element_type=F32)


def dot_tn(a, b):
    return lax.dot_general(a, b, (((0,), (0,)), ((), ())), preferred_element_type=F32)


def dot_nt(a, b):
    return lax.dot_general(a, b, (((1,), (1,)), ((), ())), preferred_element_type=F32)


def after(value, *deps):
    return lax.optimization_barrier((value,) + deps)[0]


def bit_reverse(value, bits):
    out = 0
    for b in range(bits):
        out = out | (((value >> b) & 1) << (bits - 1 - b))
    return out


def row_swap(value, rows, bit):
    return lax.ppermute(value, "row", [(i, i ^ bit) for i in range(rows)])


def col_swap(value, cols, mask):
    return lax.ppermute(value, "col", [(i, i ^ mask) for i in range(cols)])


def layer_norm(resid):
    mean = jnp.mean(resid, axis=0, keepdims=True)
    centered = resid - mean
    var = jnp.mean(centered * centered, axis=0, keepdims=True)
    inv = lax.rsqrt(var + NORM_EPS)
    return centered * inv, inv


def norm_backward(grad, normed, inv, scale):
    dn = grad * (1.0 + scale)
    first = jnp.mean(dn, axis=0, keepdims=True)
    second = jnp.mean(dn * normed, axis=0, keepdims=True)
    back = (dn - first - normed * second) * inv
    return back, jnp.sum(grad, axis=1), jnp.sum(grad * normed, axis=1)


def dot_at(a, b, a_dim, b_dim):
    return lax.dot_general(a, b, (((a_dim,), (b_dim,)), ((), ())), preferred_element_type=F32)


def masked_scores(scores, len_ref):
    if len_ref is None:
        return scores
    return jnp.where(lax.broadcasted_iota(jnp.int32, scores.shape, 1) < len_ref[0], scores, MASK_FILL)


def forward_kernel(*refs):
    len_ref = refs[0] if len(refs) == 6 else None
    q_ref, k_ref, v_ref, out_ref, lse_ref = refs[-5:]
    for h in range(q_ref.shape[0] // HD):
        head = slice(HD * h, HD * h + HD)
        scores = masked_scores(dot_at(q_ref[head, :], k_ref[head, :], 0, 0), len_ref)
        top = jnp.max(scores, axis=1, keepdims=True)
        probs = jnp.exp2((scores - top) * LOG_SCALE)
        total = jnp.sum(probs, axis=1, keepdims=True)
        out = dot_at(probs.astype(BF), v_ref[head, :], 1, 1) / total
        out_ref[head, :] = out.T.astype(BF)
        lse_ref[0, :, h : h + 1] = top * LOG_SCALE + jnp.log2(total)


def backward_kernel(*refs):
    len_ref = refs[0] if len(refs) == 9 else None
    q_ref, k_ref, v_ref, lse_ref, do_ref, dq_ref, dk_ref, dv_ref = refs[-8:]
    for h in range(q_ref.shape[0] // HD):
        head = slice(HD * h, HD * h + HD)
        q, k, v, do = q_ref[head, :], k_ref[head, :], v_ref[head, :], do_ref[head, :]
        scores = masked_scores(dot_at(q, k, 0, 0), len_ref)
        probs = jnp.exp2(scores * LOG_SCALE - lse_ref[0, :, h : h + 1])
        dv_ref[head, :] = dot_at(do, probs.astype(BF), 1, 0).astype(BF)
        dp = dot_at(do, v, 0, 0)
        ds = probs * (dp - jnp.sum(dp * probs, axis=1, keepdims=True)) * HD ** -0.5
        ds = ds.astype(BF)
        dq_ref[head, :] = dot_at(ds, k, 1, 1).T.astype(BF)
        dk_ref[head, :] = dot_at(q, ds, 1, 0).astype(BF)


def attend_call(kernel, args, length, outs, group):
    def spec(a):
        if len(a.shape) == 3:
            return pl.BlockSpec((1,) + a.shape[1:], lambda i: (i, 0, 0))
        return pl.BlockSpec((group, a.shape[1]), lambda i: (i, 0))

    specs = [spec(a) for a in args]
    if length is not None:
        specs, args = [pl.BlockSpec(memory_space=pltpu.SMEM)] + specs, [length] + args
    return pl.pallas_call(
        kernel,
        grid=(outs[0].shape[0] // group,),
        in_specs=specs,
        out_specs=[spec(o) for o in outs],
        out_shape=outs,
        compiler_params=pltpu.CompilerParams(vmem_limit_bytes=50 * 2**20),
    )(*args)


def attend_forward(q_t, k_t, v_t, length):
    group = HD * (2 if q_t.shape[0] % (2 * HD) == 0 else 1)
    outs = [
        jax.ShapeDtypeStruct(q_t.shape, BF),
        jax.ShapeDtypeStruct((q_t.shape[0] // group, q_t.shape[1], group // HD), F32),
    ]
    return attend_call(forward_kernel, [q_t, k_t, v_t], length, outs, group)


def attend_backward(q_t, k_t, v_t, length, lse, do_t):
    group = HD * lse.shape[2]
    outs = [jax.ShapeDtypeStruct(a.shape, BF) for a in (q_t, k_t, v_t)]
    return attend_call(backward_kernel, [q_t, k_t, v_t, lse, do_t], length, outs, group)


def shards(
    block_input,
    text_tokens,
    text_length,
    time_index,
    shift_table,
    time_table,
    query_weight,
    key_weight,
    value_weight,
    query_bias,
    value_bias,
    out_weight,
    out_bias,
    cross_query,
    cross_key,
    cross_value,
    cross_query_bias,
    cross_value_bias,
    cross_out,
    cross_out_bias,
    up_weight,
    up_bias,
    down_weight,
    down_bias,
    out_grad,
):
    rows, cols = lax.axis_size("row"), lax.axis_size("col")
    r, c = lax.axis_index("row"), lax.axis_index("col")
    row_bits = rows.bit_length() - 1
    half = cols // 2
    feat = block_input.shape[1]
    chunk = D // rows
    width = 2 * block_input.shape[2] // cols
    texts = text_tokens.shape[1]
    steps = time_table.shape[2]
    ups = up_bias.shape[0]
    core, low_z, micro = r & 1, (c >> 1) & 1, c // half
    at_home = core == low_z
    r_rev = bit_reverse(r, row_bits)

    kv_masks = [1 << b for b in range(2, cols.bit_length() - 2)]
    swap_pairs = []
    for i in range(rows):
        for j in range(cols):
            swap_pairs.append(
                (i * cols + j, ((i & ~1) | ((j >> 1) & 1)) * cols + ((j & ~2) | ((i & 1) << 1)))
            )

    def place_swap(value):
        return lax.ppermute(value, ("row", "col"), swap_pairs)

    def to_local(value):
        parts = value.reshape((rows, chunk) + value.shape[1:])
        picked = [
            lax.dynamic_index_in_dim(parts, r ^ bit_reverse(i, row_bits), 0, keepdims=False)
            for i in range(rows)
        ]
        return jnp.concatenate(picked, axis=0)

    def to_natural(value):
        parts = value.reshape((rows, chunk) + value.shape[1:])
        picked = [
            lax.dynamic_index_in_dim(parts, r_rev ^ bit_reverse(i, row_bits), 0, keepdims=False)
            for i in range(rows)
        ]
        return jnp.concatenate(picked, axis=0)

    def tokens_in(value):
        blocks = value.reshape(2, feat, half, width).transpose(0, 2, 1, 3).reshape(cols, feat, width)
        blocks = lax.all_to_all(blocks, "col", 0, 0, tiled=True)
        return to_local(place_swap(blocks.reshape(D, width)))

    def tokens_out(value):
        blocks = place_swap(to_natural(value.astype(BF))).reshape(cols, feat, width)
        blocks = lax.all_to_all(blocks, "col", 0, 0, tiled=True)
        blocks = blocks.reshape(2, half, feat, width).transpose(0, 2, 1, 3)
        return blocks.reshape(2, feat, half * width).astype(F32)

    def gather_pair(value):
        return jnp.concatenate([value, col_swap(value, cols, 1)], axis=1)

    def reduce_pair(value):
        own, other = value[:, :width], value[:, width:]
        return own + col_swap(other.astype(BF), cols, 1).astype(F32)

    def gather_keys(value):
        parts = [value]
        parts = parts + [row_swap(p, rows, 1) for p in parts]
        for mask in kv_masks:
            parts = parts + [col_swap(p, cols, mask) for p in parts]
        return jnp.concatenate(parts, axis=1)

    def reduce_keys(value):
        for mask in reversed(kv_masks):
            h = value.shape[1] // 2
            value = (value[:, :h].astype(F32) + col_swap(value[:, h:], cols, mask).astype(F32)).astype(BF)
        h = value.shape[1] // 2
        return (value[:, :h].astype(F32) + row_swap(value[:, h:], rows, 1).astype(F32)).astype(BF)

    row_order = [1 << b for b in reversed(range(row_bits))]

    def gather_weights(shards_w, gate):
        sizes = [w.shape[1] for w in shards_w]
        flat = jnp.concatenate(shards_w, axis=1) if len(shards_w) > 1 else shards_w[0]
        if gate is not None:
            flat = after(flat, gate)
        near = [flat] + [col_swap(flat, cols, e << 1) for e in range(1, half)]
        z_gate = near[-1]
        pieces, start = [], 0
        for size in sizes:
            pieces += [p[:, start : start + size] for p in near]
            start += size
        parts = [jnp.concatenate(pieces, axis=1)]
        for bit in row_order:
            parts = parts + [row_swap(p, rows, bit) for p in parts]
        full = jnp.concatenate(parts, axis=0)
        out, start = [], 0
        for size in sizes:
            out.append(full[:, start : start + size * half])
            start += size * half
        return full, out, z_gate

    def reduce_weights(left, right, sizes):
        end = D
        received = []
        for bit in reversed(row_order):
            start = end // 2
            part = dot_nt(left[start:end], right)
            for piece in received:
                part = part + piece[start:end].astype(F32)
            received.append(row_swap(part.astype(BF), rows, bit))
            end = start
        own = dot_nt(left[:end], right)
        for piece in received:
            own = own + piece[:end].astype(F32)
        groups, start = [], 0
        for size in sizes:
            groups.append([own[:, start + e * size : start + (e + 1) * size] for e in range(half)])
            start += size * half
        total = jnp.concatenate([g[0] for g in groups], axis=1) if len(groups) > 1 else groups[0][0]
        for e in range(1, half):
            sent = [g[e].astype(BF) for g in groups]
            sent = jnp.concatenate(sent, axis=1) if len(sent) > 1 else sent[0]
            total = total + col_swap(sent, cols, e << 1).astype(F32)
        out, start = [], 0
        for size in sizes:
            out.append(total[:, start : start + size])
            start += size
        return out

    qkv_w, _, gate_one = gather_weights([query_weight, key_weight, value_weight], None)
    _, (out_w, cq_w, ck_w, cv_w, cout_w), gate_two = gather_weights(
        [out_weight.T, cross_query, cross_key, cross_value, cross_out.T], gate_one
    )
    up_w, _, gate_three = gather_weights([up_weight], gate_two)
    down_w, _, _ = gather_weights([down_weight.T], gate_three)

    step_ids = jnp.arange(steps, dtype=jnp.int32)
    onehot = (time_index[:, 0][:, None] == step_ids[None, :]).astype(F32)
    modulation = lax.dot_general(
        onehot,
        time_table.reshape(6 * feat, steps),
        (((1,), (1,)), ((), ())),
        precision=lax.Precision.HIGHEST,
        preferred_element_type=F32,
    ).reshape(2, 6, feat) + shift_table[None]
    same = [
        jnp.broadcast_to(b.reshape(1, -1, feat), (2, b.shape[0] // feat, feat))
        for b in (out_bias, cross_out_bias, down_bias, query_bias, value_bias, cross_query_bias, cross_value_bias, up_bias)
    ]
    lengths = jnp.broadcast_to(text_length.astype(F32)[:, :, None], (2, 1, feat))
    small = jnp.concatenate([modulation, lengths] + same, axis=1).transpose(0, 2, 1)
    small_high = lax.reduce_precision(small, 8, 7)
    small_rest = small - small_high
    small_mid = lax.reduce_precision(small_rest, 8, 7)
    small_low = small_rest - small_mid
    extra = jnp.concatenate(
        [text_tokens.transpose(0, 2, 1)] + [p.astype(BF) for p in (small_high, small_mid, small_low)], axis=2
    )
    blocks = block_input.reshape(2, feat, half, width).transpose(0, 2, 1, 3).reshape(cols, feat, width)
    blocks = jnp.concatenate([blocks, jnp.repeat(extra, half, axis=0)], axis=2)
    blocks = lax.all_to_all(blocks, "col", 0, 0, tiled=True).reshape(D, -1)
    arrived = place_swap(blocks)
    arrived_local = to_local(arrived)
    small_n = small.shape[2]

    def small_of(value):
        parts = [value[:, width + texts + i * small_n : width + texts + (i + 1) * small_n].astype(F32) for i in range(3)]
        return parts[0] + parts[1] + parts[2]

    model_rows = small_of(arrived_local)
    shift_a, scale_a, gate_a, shift_m, scale_m, gate_m, length_row, out_b, cout_b, down_b = (
        model_rows[:, i : i + 1] for i in range(10)
    )
    length = length_row[0].astype(jnp.int32)
    col_rows = small_of(arrived).reshape(cols, feat, small_n)
    col_rows = jnp.concatenate(
        [
            lax.dynamic_index_in_dim(col_rows, c ^ (e << 1), 0, keepdims=False)[:, 10:].T.reshape(-1, 1, feat)
            for e in range(half)
        ],
        axis=1,
    )
    q_b, v_b, cq_b, cv_b = (col_rows[i].reshape(half * feat, 1) for i in range(4))
    up_b = col_rows[4:].transpose(1, 0, 2).reshape(half * ups, 1)
    text_t = arrived_local[:, width : width + texts]

    resid = arrived_local[:, :width].astype(F32)
    cot = tokens_in(out_grad).astype(F32)
    normed_a, inv_a = layer_norm(resid)
    attn_full = gather_pair((normed_a * (1.0 + scale_a) + shift_a).astype(BF))
    heads_w = half * feat
    qkv_bias = jnp.concatenate([q_b, jnp.zeros_like(q_b), v_b], axis=0)
    qkv = (dot_tn(qkv_w, attn_full) + qkv_bias).astype(BF)
    q_t = qkv[:heads_w]
    kv_t = gather_keys(qkv[heads_w:])
    k_t, v_t = kv_t[:heads_w], kv_t[heads_w:]
    att, lse = attend_forward(q_t, k_t, v_t, None)
    branch_a = reduce_pair(dot_nn(out_w, att)) + out_b
    after_attn = resid + gate_a * branch_a
    cross_full = gather_pair(after_attn.astype(BF))
    cq_t = (dot_tn(cq_w, cross_full) + cq_b).astype(BF)
    ck_t = dot_tn(ck_w, text_t).astype(BF)
    cv_t = (dot_tn(cv_w, text_t) + cv_b).astype(BF)
    catt, clse = attend_forward(cq_t, ck_t, cv_t, length)
    after_cross = after_attn + reduce_pair(dot_nn(cout_w, catt)) + cout_b
    normed_m, inv_m = layer_norm(after_cross)
    mlp_full = gather_pair((normed_m * (1.0 + scale_m) + shift_m).astype(BF))
    hidden_pre = dot_tn(up_w, mlp_full) + up_b
    hidden_val, gelu_pull = jax.vjp(lambda v: jax.nn.gelu(v, approximate=True), hidden_pre)
    hidden = hidden_val.astype(BF)
    branch_m = reduce_pair(dot_nn(down_w, hidden)) + down_b
    block_output = tokens_out(after_cross + gate_m * branch_m)

    grad_mlp = gate_m * cot
    low_full = gather_pair(grad_mlp.astype(BF))
    g_down_b = jnp.sum(grad_mlp, axis=1)
    g_gate_m = jnp.sum(cot * branch_m, axis=1)
    grad_pre = gelu_pull(dot_tn(down_w, low_full))[0].astype(BF)
    (g_down,) = reduce_weights(low_full, hidden, [ups])
    back_in = reduce_pair(dot_nn(up_w, grad_pre))
    (g_up,) = reduce_weights(mlp_full, grad_pre, [ups])
    g_up_b = jnp.sum(grad_pre.astype(F32), axis=1)
    back_m, g_shift_m, g_scale_m = norm_backward(back_in, normed_m, inv_m, scale_m)
    grad_cross = cot + back_m
    g_cout_b = jnp.sum(grad_cross, axis=1)
    low_cross = gather_pair(grad_cross.astype(BF))
    dcatt = dot_tn(cout_w, low_cross).astype(BF)
    dcq, dck, dcv = attend_backward(cq_t, ck_t, cv_t, length, clse, dcatt)
    g_cq_b = jnp.sum(dcq.astype(F32), axis=1)
    g_cv_b = jnp.sum(dcv.astype(F32), axis=1)
    grad_res = grad_cross + reduce_pair(dot_nn(cq_w, dcq))
    grad_text = to_natural(dot_nn(ck_w, dck) + dot_nn(cv_w, dcv)).astype(BF)
    grad_text = grad_text.astype(F32) + row_swap(grad_text, rows, 1).astype(F32)
    grad_text = jnp.where(at_home, grad_text, 0.0).astype(BF).reshape(cols, feat, texts)
    grad_text = lax.all_to_all(grad_text, "col", 0, 0, tiled=True)
    grad_text = jnp.sum(grad_text.reshape(2, half, feat, texts).astype(F32), axis=1).transpose(0, 2, 1)
    (g_cout,) = reduce_weights(low_cross, catt, [feat])
    (g_cq,) = reduce_weights(cross_full, dcq, [feat])
    g_ck, g_cv = reduce_weights(text_t, jnp.concatenate([dck, dcv], axis=0), [feat, feat])
    g_gate_a = jnp.sum(grad_res * branch_a, axis=1)
    grad_attn = gate_a * grad_res
    g_out_b = jnp.sum(grad_attn, axis=1)
    low_attn = gather_pair(grad_attn.astype(BF))
    datt = dot_tn(out_w, low_attn).astype(BF)
    dq, dk, dv = attend_backward(q_t, k_t, v_t, None, lse, datt)
    (g_out,) = reduce_weights(low_attn, att, [feat])
    dkv = reduce_keys(jnp.concatenate([dk, dv], axis=0))
    dqkv = jnp.concatenate([dq, dkv], axis=0)
    g_q, g_k, g_v = reduce_weights(attn_full, dqkv, [feat, feat, feat])
    g_q_b = jnp.sum(dq.astype(F32), axis=1)
    g_v_b = jnp.sum(dkv[heads_w:].astype(F32), axis=1)
    back_a, g_shift_a, g_scale_a = norm_backward(
        reduce_pair(dot_nn(qkv_w, dqkv)), normed_a, inv_a, scale_a
    )
    grad_input = tokens_out(grad_res + back_a)

    model_g = jnp.stack(
        [g_shift_a, g_scale_a, g_gate_a, g_shift_m, g_scale_m, g_gate_m, g_out_b, g_cout_b, g_down_b], axis=1
    )
    model_g = to_natural(model_g).T.reshape(9, cols, feat).transpose(1, 0, 2)
    per_col = ups // feat
    col_g = jnp.concatenate(
        [g.reshape(half, 1, feat) for g in (g_q_b, g_v_b, g_cq_b, g_cv_b)] + [g_up_b.reshape(half, per_col, feat)],
        axis=1,
    )
    side = c & 1
    blocks = []
    for j in range(cols):
        part = lax.dynamic_index_in_dim(col_g, (j >> 1) ^ (c >> 1), 0, keepdims=False)
        blocks.append(jnp.where(side == (j & 1), part, 0.0))
    small_g = jnp.concatenate([model_g, jnp.stack(blocks)], axis=1)
    small_g = lax.all_to_all(small_g, "col", 0, 0, tiled=True)
    mod_g = small_g[:, :6].reshape(2, cols // 8, 2, 2, 6, feat).sum(axis=(1, 3))
    bias_g = small_g[:, 6:].sum(axis=0)
    step_rows = jnp.broadcast_to(time_index.astype(F32), (2, feat))
    small_g = lax.all_gather(jnp.concatenate([mod_g.reshape(24, feat), bias_g, step_rows], axis=0), "row")
    step_all = small_g[:, -2:, 0].T.reshape(2 * rows).astype(jnp.int32)
    mod_g = small_g[:, :24].reshape(rows // 2, 2, 2, 2, 6, feat).sum(axis=1)
    mod_g = mod_g.transpose(1, 0, 2, 3, 4).reshape(2 * rows, 6, feat)
    bias_g = small_g[:, 24:-2].sum(axis=0)
    g_shift = mod_g.sum(axis=0)
    onehot_all = (step_all[:, None] == step_ids[None, :]).astype(F32)
    g_time = lax.dot_general(
        mod_g.reshape(2 * rows, 6 * feat),
        onehot_all,
        (((0,), (0,)), ((), ())),
        precision=lax.Precision.HIGHEST,
        preferred_element_type=F32,
    ).reshape(6, feat, steps)
    g_out_b, g_cout_b, g_down_b, g_q_b, g_v_b, g_cq_b, g_cv_b = (bias_g[i] for i in range(7))
    g_up_b = bias_g[7:].reshape(ups)
    return (
        block_output,
        grad_input,
        grad_text,
        g_shift,
        g_time,
        g_q,
        g_k,
        g_v,
        g_q_b,
        g_v_b,
        g_out.T,
        g_out_b,
        g_cq,
        g_ck,
        g_cv,
        g_cq_b,
        g_cv_b,
        g_cout.T,
        g_cout_b,
        g_up,
        g_up_b,
        g_down.T,
        g_down_b,
    )


def solution(mesh):
    return jax.shard_map(
        shards,
        mesh=mesh,
        in_specs=(
            P(None, "col", "row"),
            P(None, "row", "col"),
            P(None, "row"),
            P(None, "row"),
            P(None, "col"),
            P(None, "col", None),
            P("row", "col"),
            P("row", "col"),
            P("row", "col"),
            P("col"),
            P("col"),
            P("col", "row"),
            P("col"),
            P("row", "col"),
            P("row", "col"),
            P("row", "col"),
            P("col"),
            P("col"),
            P("col", "row"),
            P("col"),
            P("row", "col"),
            P("col"),
            P("col", "row"),
            P("col"),
            P(None, "col", "row"),
        ),
        out_specs=(
            P(None, "col", "row"),
            P(None, "col", "row"),
            P(None, "row", "col"),
            P(None, "col"),
            P(None, "col", None),
            P("row", "col"),
            P("row", "col"),
            P("row", "col"),
            P("col"),
            P("col"),
            P("col", "row"),
            P("col"),
            P("row", "col"),
            P("row", "col"),
            P("row", "col"),
            P("col"),
            P("col"),
            P("col", "row"),
            P("col"),
            P("row", "col"),
            P("col"),
            P("col", "row"),
            P("col"),
        ),
        check_vma=False,
    )
```

```python
import functools

import jax
import jax.numpy as jnp
from jax import lax
from jax.experimental import pallas as pl
from jax.experimental.pallas import tpu as pltpu
from jax.sharding import PartitionSpec as P

D = 1152
HEADS = 16
HD = 72

NORM_EPS = 1e-06
MASK_FILL = -1e30
BF = jnp.bfloat16
F32 = jnp.float32
LOG_SCALE = HD ** -0.5 * 1.4426950408889634


def dot_nn(a, b):
    return lax.dot_general(a, b, (((1,), (0,)), ((), ())), preferred_element_type=F32)


def dot_tn(a, b):
    return lax.dot_general(a, b, (((0,), (0,)), ((), ())), preferred_element_type=F32)


def dot_nt(a, b):
    return lax.dot_general(a, b, (((1,), (1,)), ((), ())), preferred_element_type=F32)


def after(value, *deps):
    return lax.optimization_barrier((value,) + deps)[0]


def row_swap(value, rows, bit):
    return lax.ppermute(value, "row", [(i, i ^ bit) for i in range(rows)])


def col_swap(value, cols, mask):
    return lax.ppermute(value, "col", [(i, i ^ mask) for i in range(cols)])


def layer_norm(resid):
    mean = jnp.mean(resid, axis=0, keepdims=True)
    centered = resid - mean
    var = jnp.mean(centered * centered, axis=0, keepdims=True)
    inv = lax.rsqrt(var + NORM_EPS)
    return centered * inv, inv


def norm_backward(grad, normed, inv, scale):
    dn = grad * (1.0 + scale)
    first = jnp.mean(dn, axis=0, keepdims=True)
    second = jnp.mean(dn * normed, axis=0, keepdims=True)
    back = (dn - first - normed * second) * inv
    return back, jnp.sum(grad, axis=1), jnp.sum(grad * normed, axis=1)


def dot_at(a, b, a_dim, b_dim):
    return lax.dot_general(a, b, (((a_dim,), (b_dim,)), ((), ())), preferred_element_type=F32)


def masked_scores(scores, len_ref):
    if len_ref is None:
        return scores
    return jnp.where(lax.broadcasted_iota(jnp.int32, scores.shape, 1) < len_ref[0], scores, MASK_FILL)


def forward_kernel(*refs):
    len_ref = refs[0] if len(refs) == 6 else None
    q_ref, k_ref, v_ref, out_ref, lse_ref = refs[-5:]
    for h in range(q_ref.shape[0] // HD):
        head = slice(HD * h, HD * h + HD)
        scores = masked_scores(dot_at(q_ref[head, :], k_ref[head, :], 0, 0), len_ref)
        top = jnp.max(scores, axis=1, keepdims=True)
        probs = jnp.exp2((scores - top) * LOG_SCALE)
        total = jnp.sum(probs, axis=1, keepdims=True)
        out = dot_at(probs.astype(BF), v_ref[head, :], 1, 1) / total
        out_ref[head, :] = out.T.astype(BF)
        lse_ref[0, :, h : h + 1] = top * LOG_SCALE + jnp.log2(total)


def backward_kernel(*refs):
    len_ref = refs[0] if len(refs) == 9 else None
    q_ref, k_ref, v_ref, lse_ref, do_ref, dq_ref, dk_ref, dv_ref = refs[-8:]
    for h in range(q_ref.shape[0] // HD):
        head = slice(HD * h, HD * h + HD)
        q, k, v, do = q_ref[head, :], k_ref[head, :], v_ref[head, :], do_ref[head, :]
        scores = masked_scores(dot_at(q, k, 0, 0), len_ref)
        probs = jnp.exp2(scores * LOG_SCALE - lse_ref[0, :, h : h + 1])
        dv_ref[head, :] = dot_at(do, probs.astype(BF), 1, 0).astype(BF)
        dp = dot_at(do, v, 0, 0)
        ds = probs * (dp - jnp.sum(dp * probs, axis=1, keepdims=True)) * HD ** -0.5
        ds = ds.astype(BF)
        dq_ref[head, :] = dot_at(ds, k, 1, 1).T.astype(BF)
        dk_ref[head, :] = dot_at(q, ds, 1, 0).astype(BF)


def attend_call(kernel, args, length, outs, group):
    def spec(a):
        if len(a.shape) == 3:
            return pl.BlockSpec((1,) + a.shape[1:], lambda i: (i, 0, 0))
        return pl.BlockSpec((group, a.shape[1]), lambda i: (i, 0))

    specs = [spec(a) for a in args]
    if length is not None:
        specs, args = [pl.BlockSpec(memory_space=pltpu.SMEM)] + specs, [length] + args
    return pl.pallas_call(
        kernel,
        grid=(outs[0].shape[0] // group,),
        in_specs=specs,
        out_specs=[spec(o) for o in outs],
        out_shape=outs,
        compiler_params=pltpu.CompilerParams(vmem_limit_bytes=50 * 2**20),
    )(*args)


def attend_forward(q_t, k_t, v_t, length):
    group = HD * (2 if q_t.shape[0] % (2 * HD) == 0 else 1)
    outs = [
        jax.ShapeDtypeStruct(q_t.shape, BF),
        jax.ShapeDtypeStruct((q_t.shape[0] // group, q_t.shape[1], group // HD), F32),
    ]
    return attend_call(forward_kernel, [q_t, k_t, v_t], length, outs, group)


def attend_backward(q_t, k_t, v_t, length, lse, do_t):
    group = HD * lse.shape[2]
    outs = [jax.ShapeDtypeStruct(a.shape, BF) for a in (q_t, k_t, v_t)]
    return attend_call(backward_kernel, [q_t, k_t, v_t, lse, do_t], length, outs, group)


def outer_kernel(*refs):
    out_ref = refs[-1]
    rows, chunk = out_ref.shape[0], out_ref.shape[1]
    for r in range(rows):
        block = slice(r * chunk, r * chunk + chunk)
        start = 0
        for left_ref, right_ref in zip(refs[:-1:2], refs[1:-1:2]):
            end = start + right_ref.shape[0]
            out_ref[r, :, start:end] = dot_nt(left_ref[block, :], right_ref[...]).astype(BF)
            start = end


def outer_blocks(pairs, rows, half):
    chunk = D // rows
    sizes = [b.shape[0] // half for _, b in pairs]
    specs, args = [], []
    for (a, b), n in zip(pairs, sizes):
        specs.append(pl.BlockSpec(a.shape, lambda z: (0, 0)))
        specs.append(pl.BlockSpec((n, b.shape[1]), lambda z: (z, 0)))
        args += [a, b]
    return pl.pallas_call(
        outer_kernel,
        grid=(half,),
        in_specs=specs,
        out_specs=pl.BlockSpec((rows, chunk, sum(sizes)), lambda z: (z, 0, 0)),
        out_shape=jax.ShapeDtypeStruct((half * rows, chunk, sum(sizes)), BF),
        compiler_params=pltpu.CompilerParams(vmem_limit_bytes=50 * 2**20),
    )(*args), sizes


def shards(
    block_input,
    text_tokens,
    text_length,
    time_index,
    shift_table,
    time_table,
    query_weight,
    key_weight,
    value_weight,
    query_bias,
    value_bias,
    out_weight,
    out_bias,
    cross_query,
    cross_key,
    cross_value,
    cross_query_bias,
    cross_value_bias,
    cross_out,
    cross_out_bias,
    up_weight,
    up_bias,
    down_weight,
    down_bias,
    out_grad,
):
    rows, cols = lax.axis_size("row"), lax.axis_size("col")
    r, c = lax.axis_index("row"), lax.axis_index("col")
    half = cols // 2
    feat = block_input.shape[1]
    width = 2 * block_input.shape[2] // cols
    texts = text_tokens.shape[1]
    steps = time_table.shape[2]
    ups = up_bias.shape[0]
    core, low_z, micro = r & 1, (c >> 1) & 1, c // half
    at_home = core == low_z

    kv_masks = [1 << b for b in range(2, cols.bit_length() - 2)]
    swap_pairs = []
    for i in range(rows):
        for j in range(cols):
            swap_pairs.append(
                (i * cols + j, ((i & ~1) | ((j >> 1) & 1)) * cols + ((j & ~2) | ((i & 1) << 1)))
            )

    def place_swap(value):
        return lax.ppermute(value, ("row", "col"), swap_pairs)

    def tokens_in(value):
        blocks = value.reshape(2, feat, half, width).transpose(0, 2, 1, 3).reshape(cols, feat, width)
        blocks = lax.all_to_all(blocks, "col", 0, 0, tiled=True)
        return place_swap(blocks.reshape(D, width))

    def tokens_out(value):
        blocks = place_swap(value.astype(BF)).reshape(cols, feat, width)
        blocks = lax.all_to_all(blocks, "col", 0, 0, tiled=True)
        blocks = blocks.reshape(2, half, feat, width).transpose(0, 2, 1, 3)
        return blocks.reshape(2, feat, half * width).astype(F32)

    def gather_pair(value):
        return jnp.concatenate([value, col_swap(value, cols, 1)], axis=1)

    def reduce_pair(value):
        own, other = value[:, :width], value[:, width:]
        return own + col_swap(other.astype(BF), cols, 1).astype(F32)

    def gather_keys(value):
        parts = [value]
        parts = parts + [row_swap(p, rows, 1) for p in parts]
        for mask in kv_masks:
            parts = parts + [col_swap(p, cols, mask) for p in parts]
        return jnp.concatenate(parts, axis=1)

    def reduce_keys(value):
        for mask in reversed(kv_masks):
            h = value.shape[1] // 2
            value = (value[:, :h].astype(F32) + col_swap(value[:, h:], cols, mask).astype(F32)).astype(BF)
        h = value.shape[1] // 2
        return (value[:, :h].astype(F32) + row_swap(value[:, h:], rows, 1).astype(F32)).astype(BF)

    groups = [[i * cols + 2 * z + y for z in range(half) for i in range(rows)] for y in range(2)]

    def gather_weights(shards_w):
        flat = jnp.concatenate(shards_w, axis=1)
        full = lax.all_gather(flat, ("row", "col"), axis=0, tiled=True, axis_index_groups=groups)
        return full.reshape(half, D, flat.shape[1])

    def apply_in(weight, value):
        return jnp.concatenate([dot_tn(weight[z], value) for z in range(half)], axis=0)

    def apply_out(weight, value):
        n = weight.shape[2]
        total = dot_nn(weight[0], value[:n])
        for z in range(1, half):
            total = total + dot_nn(weight[z], value[z * n : z * n + n])
        return total

    def reduce_weights(pairs):
        blocks, sizes = outer_blocks(pairs, rows, half)
        flat = blocks.reshape(half * D, sum(sizes))
        own = lax.psum_scatter(flat, ("row", "col"), scatter_dimension=0, tiled=True, axis_index_groups=groups)
        out, start = [], 0
        for size in sizes:
            out.append(own[:, start : start + size].astype(F32))
            start += size
        return out

    def mix_heads(parts):
        t = parts[0].shape[1]
        return jnp.stack([p.reshape(half, feat, t) for p in parts], axis=1).reshape(half * 3 * feat, t)

    first_w = gather_weights(
        [query_weight, key_weight, value_weight, out_weight.T, cross_query, cross_key, cross_value, cross_out.T]
    )
    second_w = gather_weights([up_weight, down_weight.T])

    step_ids = jnp.arange(steps, dtype=jnp.int32)
    onehot = (time_index[:, 0][:, None] == step_ids[None, :]).astype(F32)
    modulation = lax.dot_general(
        onehot,
        time_table.reshape(6 * feat, steps),
        (((1,), (1,)), ((), ())),
        precision=lax.Precision.HIGHEST,
        preferred_element_type=F32,
    ).reshape(2, 6, feat) + shift_table[None]
    same = [
        jnp.broadcast_to(b.reshape(1, -1, feat), (2, b.shape[0] // feat, feat))
        for b in (out_bias, cross_out_bias, down_bias, query_bias, value_bias, cross_query_bias, cross_value_bias, up_bias)
    ]
    lengths = jnp.broadcast_to(text_length.astype(F32)[:, :, None], (2, 1, feat))
    small = jnp.concatenate([modulation, lengths] + same, axis=1).transpose(0, 2, 1)
    small_high = lax.reduce_precision(small, 8, 7)
    small_rest = small - small_high
    small_mid = lax.reduce_precision(small_rest, 8, 7)
    small_low = small_rest - small_mid
    extra = jnp.concatenate(
        [text_tokens.transpose(0, 2, 1)] + [p.astype(BF) for p in (small_high, small_mid, small_low)], axis=2
    )
    blocks = block_input.reshape(2, feat, half, width).transpose(0, 2, 1, 3).reshape(cols, feat, width)
    blocks = jnp.concatenate([blocks, jnp.repeat(extra, half, axis=0)], axis=2)
    blocks = lax.all_to_all(blocks, "col", 0, 0, tiled=True).reshape(D, -1)
    arrived = place_swap(blocks)
    small_n = small.shape[2]

    def small_of(value):
        parts = [value[:, width + texts + i * small_n : width + texts + (i + 1) * small_n].astype(F32) for i in range(3)]
        return parts[0] + parts[1] + parts[2]

    model_rows = small_of(arrived)
    shift_a, scale_a, gate_a, shift_m, scale_m, gate_m, length_row, out_b, cout_b, down_b = (
        model_rows[:, i : i + 1] for i in range(10)
    )
    length = length_row[0].astype(jnp.int32)
    col_rows = small_of(arrived).reshape(cols, feat, small_n)
    col_rows = jnp.concatenate(
        [
            lax.dynamic_index_in_dim(col_rows, 2 * e + (c & 1), 0, keepdims=False)[:, 10:].T.reshape(-1, 1, feat)
            for e in range(half)
        ],
        axis=1,
    )
    q_b, v_b, cq_b, cv_b = (col_rows[i].reshape(half * feat, 1) for i in range(4))
    up_b = col_rows[4:].transpose(1, 0, 2).reshape(half * ups, 1)
    text_t = arrived[:, width : width + texts]

    resid = arrived[:, :width].astype(F32)
    cot_low = tokens_in(after(out_grad, arrived))
    cot = cot_low.astype(F32)
    first_w = after(first_w, cot_low)
    qkv_w = first_w[:, :, : 3 * feat]
    out_w, cq_w, ck_w, cv_w, cout_w = (first_w[:, :, i * feat : (i + 1) * feat] for i in range(3, 8))
    up_w, down_w = second_w[:, :, :ups], second_w[:, :, ups:]
    normed_a, inv_a = layer_norm(resid)
    attn_full = gather_pair((normed_a * (1.0 + scale_a) + shift_a).astype(BF))
    heads_w = half * feat
    qkv_bias = mix_heads([q_b, jnp.zeros_like(q_b), v_b])
    qkv = (apply_in(qkv_w, attn_full) + qkv_bias).astype(BF).reshape(half, 3 * feat, 2 * width)
    q_t = qkv[:, :feat].reshape(heads_w, 2 * width)
    kv_t = gather_keys(jnp.concatenate([qkv[:, feat : 2 * feat], qkv[:, 2 * feat :]], axis=0).reshape(2 * heads_w, 2 * width))
    k_t, v_t = kv_t[:heads_w], kv_t[heads_w:]
    att, lse = attend_forward(q_t, k_t, v_t, None)
    branch_a = reduce_pair(apply_out(out_w, att)) + out_b
    after_attn = resid + gate_a * branch_a
    cross_full = gather_pair(after_attn.astype(BF))
    cq_t = (apply_in(cq_w, cross_full) + cq_b).astype(BF)
    ck_t = apply_in(ck_w, text_t).astype(BF)
    cv_t = (apply_in(cv_w, text_t) + cv_b).astype(BF)
    catt, clse = attend_forward(cq_t, ck_t, cv_t, length)
    after_cross = after_attn + reduce_pair(apply_out(cout_w, catt)) + cout_b
    normed_m, inv_m = layer_norm(after_cross)
    mlp_full = gather_pair((normed_m * (1.0 + scale_m) + shift_m).astype(BF))
    hidden_pre = apply_in(up_w, mlp_full) + up_b
    hidden_val, gelu_pull = jax.vjp(lambda v: jax.nn.gelu(v, approximate=True), hidden_pre)
    hidden = hidden_val.astype(BF)
    branch_m = reduce_pair(apply_out(down_w, hidden)) + down_b
    block_output = tokens_out(after_cross + gate_m * branch_m)

    grad_mlp = gate_m * cot
    low_full = gather_pair(grad_mlp.astype(BF))
    g_down_b = jnp.sum(grad_mlp, axis=1)
    g_gate_m = jnp.sum(cot * branch_m, axis=1)
    grad_pre = gelu_pull(apply_in(down_w, low_full))[0].astype(BF)
    g_up, g_down = reduce_weights([(mlp_full, grad_pre), (low_full, hidden)])
    back_in = reduce_pair(apply_out(up_w, grad_pre))
    g_up_b = jnp.sum(grad_pre.astype(F32), axis=1)
    back_m, g_shift_m, g_scale_m = norm_backward(back_in, normed_m, inv_m, scale_m)
    grad_cross = cot + back_m
    g_cout_b = jnp.sum(grad_cross, axis=1)
    low_cross = gather_pair(grad_cross.astype(BF))
    dcatt = apply_in(cout_w, low_cross).astype(BF)
    dcq, dck, dcv = attend_backward(cq_t, ck_t, cv_t, length, clse, dcatt)
    g_cq_b = jnp.sum(dcq.astype(F32), axis=1)
    g_cv_b = jnp.sum(dcv.astype(F32), axis=1)
    grad_res = grad_cross + reduce_pair(apply_out(cq_w, dcq))
    grad_text = (apply_out(ck_w, dck) + apply_out(cv_w, dcv)).astype(BF)
    grad_text = grad_text.astype(F32) + row_swap(grad_text, rows, 1).astype(F32)
    grad_text = jnp.where(at_home, grad_text, 0.0).astype(BF).reshape(cols, feat, texts)
    grad_text = lax.all_to_all(grad_text, "col", 0, 0, tiled=True)
    grad_text = jnp.sum(grad_text.reshape(2, half, feat, texts).astype(F32), axis=1).transpose(0, 2, 1)
    g_gate_a = jnp.sum(grad_res * branch_a, axis=1)
    grad_attn = gate_a * grad_res
    g_out_b = jnp.sum(grad_attn, axis=1)
    low_attn = gather_pair(grad_attn.astype(BF))
    datt = apply_in(out_w, low_attn).astype(BF)
    dq, dk, dv = attend_backward(q_t, k_t, v_t, None, lse, datt)
    dkv = reduce_keys(jnp.concatenate([dk, dv], axis=0))
    dqkv = mix_heads([dq, dkv[:heads_w], dkv[heads_w:]])
    g_qkv, g_out, g_cq, g_ck, g_cv, g_cout = reduce_weights(
        [(attn_full, dqkv), (low_attn, att), (cross_full, dcq), (text_t, dck), (text_t, dcv), (low_cross, catt)]
    )
    g_q, g_k, g_v = (g_qkv[:, i * feat : (i + 1) * feat] for i in range(3))
    g_q_b = jnp.sum(dq.astype(F32), axis=1)
    g_v_b = jnp.sum(dkv[heads_w:].astype(F32), axis=1)
    back_a, g_shift_a, g_scale_a = norm_backward(
        reduce_pair(apply_out(qkv_w, dqkv)), normed_a, inv_a, scale_a
    )
    grad_input = tokens_out(grad_res + back_a)

    model_g = jnp.stack(
        [g_shift_a, g_scale_a, g_gate_a, g_shift_m, g_scale_m, g_gate_m, g_out_b, g_cout_b, g_down_b], axis=1
    )
    model_g = model_g.T.reshape(9, cols, feat).transpose(1, 0, 2)
    per_col = ups // feat
    col_g = jnp.concatenate(
        [g.reshape(half, 1, feat) for g in (g_q_b, g_v_b, g_cq_b, g_cv_b)] + [g_up_b.reshape(half, per_col, feat)],
        axis=1,
    )
    side = c & 1
    blocks = []
    for j in range(cols):
        blocks.append(jnp.where(side == (j & 1), col_g[j >> 1], 0.0))
    small_g = jnp.concatenate([model_g, jnp.stack(blocks)], axis=1)
    small_g = lax.all_to_all(small_g, "col", 0, 0, tiled=True)
    mod_g = small_g[:, :6].reshape(2, cols // 8, 2, 2, 6, feat).sum(axis=(1, 3))
    bias_g = small_g[:, 6:].sum(axis=0)
    step_rows = jnp.broadcast_to(time_index.astype(F32), (2, feat))
    small_g = lax.all_gather(jnp.concatenate([mod_g.reshape(24, feat), bias_g, step_rows], axis=0), "row")
    step_all = small_g[:, -2:, 0].T.reshape(2 * rows).astype(jnp.int32)
    mod_g = small_g[:, :24].reshape(rows // 2, 2, 2, 2, 6, feat).sum(axis=1)
    mod_g = mod_g.transpose(1, 0, 2, 3, 4).reshape(2 * rows, 6, feat)
    bias_g = small_g[:, 24:-2].sum(axis=0)
    g_shift = mod_g.sum(axis=0)
    onehot_all = (step_all[:, None] == step_ids[None, :]).astype(F32)
    g_time = lax.dot_general(
        mod_g.reshape(2 * rows, 6 * feat),
        onehot_all,
        (((0,), (0,)), ((), ())),
        precision=lax.Precision.HIGHEST,
        preferred_element_type=F32,
    ).reshape(6, feat, steps)
    g_out_b, g_cout_b, g_down_b, g_q_b, g_v_b, g_cq_b, g_cv_b = (bias_g[i] for i in range(7))
    g_up_b = bias_g[7:].reshape(ups)
    return (
        block_output,
        grad_input,
        grad_text,
        g_shift,
        g_time,
        g_q,
        g_k,
        g_v,
        g_q_b,
        g_v_b,
        g_out.T,
        g_out_b,
        g_cq,
        g_ck,
        g_cv,
        g_cq_b,
        g_cv_b,
        g_cout.T,
        g_cout_b,
        g_up,
        g_up_b,
        g_down.T,
        g_down_b,
    )


def solution(mesh):
    return jax.shard_map(
        shards,
        mesh=mesh,
        in_specs=(
            P(None, "col", "row"),
            P(None, "row", "col"),
            P(None, "row"),
            P(None, "row"),
            P(None, "col"),
            P(None, "col", None),
            P("row", "col"),
            P("row", "col"),
            P("row", "col"),
            P("col"),
            P("col"),
            P("col", "row"),
            P("col"),
            P("row", "col"),
            P("row", "col"),
            P("row", "col"),
            P("col"),
            P("col"),
            P("col", "row"),
            P("col"),
            P("row", "col"),
            P("col"),
            P("col", "row"),
            P("col"),
            P(None, "col", "row"),
        ),
        out_specs=(
            P(None, "col", "row"),
            P(None, "col", "row"),
            P(None, "row", "col"),
            P(None, "col"),
            P(None, "col", None),
            P("row", "col"),
            P("row", "col"),
            P("row", "col"),
            P("col"),
            P("col"),
            P("col", "row"),
            P("col"),
            P("row", "col"),
            P("row", "col"),
            P("row", "col"),
            P("col"),
            P("col"),
            P("col", "row"),
            P("col"),
            P("row", "col"),
            P("col"),
            P("col", "row"),
            P("col"),
        ),
        check_vma=False,
    )
```

```python
import functools

import jax
import jax.numpy as jnp
from jax import lax
from jax.experimental import pallas as pl
from jax.experimental.pallas import tpu as pltpu
from jax.sharding import PartitionSpec as P

D = 1152
HEADS = 16
HD = 72

NORM_EPS = 1e-06
MASK_FILL = -1e30
BF = jnp.bfloat16
F32 = jnp.float32
LOG_SCALE = HD ** -0.5 * 1.4426950408889634


def dot_nn(a, b):
    return lax.dot_general(a, b, (((1,), (0,)), ((), ())), preferred_element_type=F32)


def dot_tn(a, b):
    return lax.dot_general(a, b, (((0,), (0,)), ((), ())), preferred_element_type=F32)


def dot_nt(a, b):
    return lax.dot_general(a, b, (((1,), (1,)), ((), ())), preferred_element_type=F32)


def after(value, *deps):
    return lax.optimization_barrier((value,) + deps)[0]


def row_swap(value, rows, bit):
    return lax.ppermute(value, "row", [(i, i ^ bit) for i in range(rows)])


def col_swap(value, cols, mask):
    return lax.ppermute(value, "col", [(i, i ^ mask) for i in range(cols)])


def layer_norm(resid):
    mean = jnp.mean(resid, axis=0, keepdims=True)
    centered = resid - mean
    var = jnp.mean(centered * centered, axis=0, keepdims=True)
    inv = lax.rsqrt(var + NORM_EPS)
    return centered * inv, inv


def norm_backward(grad, normed, inv, scale):
    dn = grad * (1.0 + scale)
    first = jnp.mean(dn, axis=0, keepdims=True)
    second = jnp.mean(dn * normed, axis=0, keepdims=True)
    back = (dn - first - normed * second) * inv
    return back, jnp.sum(grad, axis=1), jnp.sum(grad * normed, axis=1)


def dot_at(a, b, a_dim, b_dim):
    return lax.dot_general(a, b, (((a_dim,), (b_dim,)), ((), ())), preferred_element_type=F32)


def masked_scores(scores, len_ref):
    if len_ref is None:
        return scores
    return jnp.where(lax.broadcasted_iota(jnp.int32, scores.shape, 1) < len_ref[0], scores, MASK_FILL)


def join(refs, rows):
    return jnp.concatenate([ref[rows, :] for ref in refs], axis=1)


def put(refs, rows, value):
    start = 0
    for ref in refs:
        end = start + ref.shape[1]
        ref[rows, :] = value[:, start:end].astype(ref.dtype)
        start = end


def head_rows(h, first):
    return slice(first + HD * h, first + HD * h + HD)


def forward_kernel(n_q, n_kv, has_len, *refs):
    len_ref = refs[0] if has_len else None
    refs = refs[1:] if has_len else refs
    q_refs, kv_refs, out_refs, lse_ref = refs[:n_q], refs[n_q : n_q + n_kv], refs[n_q + n_kv : -1], refs[-1]
    feat = q_refs[0].shape[0]
    for h in range(feat // HD):
        head, value_rows = head_rows(h, 0), head_rows(h, feat)
        q, k, v = join(q_refs, head), join(kv_refs, head), join(kv_refs, value_rows)
        scores = masked_scores(dot_at(q, k, 0, 0), len_ref)
        top = jnp.max(scores, axis=1, keepdims=True)
        probs = jnp.exp2((scores - top) * LOG_SCALE)
        total = jnp.sum(probs, axis=1, keepdims=True)
        out = dot_at(probs.astype(BF), v, 1, 1) / total
        put(out_refs, head, out.T)
        lse_ref[0, :, h : h + 1] = top * LOG_SCALE + jnp.log2(total)


def backward_kernel(n_q, n_kv, has_len, *refs):
    len_ref = refs[0] if has_len else None
    refs = refs[1:] if has_len else refs
    q_refs, kv_refs, lse_ref = refs[:n_q], refs[n_q : n_q + n_kv], refs[n_q + n_kv]
    refs = refs[n_q + n_kv + 1 :]
    do_refs, dq_refs, dkv_refs = refs[:n_q], refs[n_q : 2 * n_q], refs[2 * n_q :]
    feat = q_refs[0].shape[0]
    for h in range(feat // HD):
        head, value_rows = head_rows(h, 0), head_rows(h, feat)
        q, k, v, do = join(q_refs, head), join(kv_refs, head), join(kv_refs, value_rows), join(do_refs, head)
        scores = masked_scores(dot_at(q, k, 0, 0), len_ref)
        probs = jnp.exp2(scores * LOG_SCALE - lse_ref[0, :, h : h + 1])
        put(dkv_refs, value_rows, dot_at(do, probs.astype(BF), 1, 0))
        dp = dot_at(do, v, 0, 0)
        ds = probs * (dp - jnp.sum(dp * probs, axis=1, keepdims=True)) * HD ** -0.5
        ds = ds.astype(BF)
        put(dq_refs, head, dot_at(ds, k, 1, 1).T)
        put(dkv_refs, head, dot_at(q, ds, 1, 0))


def part_spec(shape, steps):
    if len(shape) == 3:
        return pl.BlockSpec((1,) + tuple(shape[1:]), lambda z: (z, 0, 0))
    return pl.BlockSpec((shape[0] // steps, shape[1]), lambda z: (z, 0))


def whole_spec(shape):
    return pl.BlockSpec(tuple(shape), lambda z: (0,) * len(shape))


def call_parts(kernel, steps, args, arg_specs, outs, out_specs, scratch=()):
    return pl.pallas_call(
        kernel,
        grid=(steps,),
        in_specs=arg_specs,
        out_specs=out_specs,
        out_shape=outs,
        scratch_shapes=list(scratch),
        compiler_params=pltpu.CompilerParams(vmem_limit_bytes=50 * 2**20),
    )(*args)


def attend_forward(q_parts, kv_parts, length, half):
    rows, tokens = q_parts[0].shape[0], sum(q.shape[1] for q in q_parts)
    outs = [jax.ShapeDtypeStruct(q.shape, BF) for q in q_parts]
    outs.append(jax.ShapeDtypeStruct((half, tokens, rows // half // HD), F32))
    args = list(q_parts) + list(kv_parts)
    specs = [part_spec(a.shape, half) for a in args]
    if length is not None:
        args, specs = [length] + args, [pl.BlockSpec(memory_space=pltpu.SMEM)] + specs
    kernel = functools.partial(forward_kernel, len(q_parts), len(kv_parts), length is not None)
    res = call_parts(kernel, half, args, specs, outs, [part_spec(o.shape, half) for o in outs])
    return res[:-1], res[-1]


def attend_backward(q_parts, kv_parts, length, lse, do_parts, half):
    outs = [jax.ShapeDtypeStruct(a.shape, BF) for a in list(q_parts) + list(kv_parts)]
    args = list(q_parts) + list(kv_parts) + [lse] + list(do_parts)
    specs = [part_spec(a.shape, half) for a in args]
    if length is not None:
        args, specs = [length] + args, [pl.BlockSpec(memory_space=pltpu.SMEM)] + specs
    kernel = functools.partial(backward_kernel, len(q_parts), len(kv_parts), length is not None)
    res = call_parts(kernel, half, args, specs, outs, [part_spec(o.shape, half) for o in outs])
    return res[: len(q_parts)], res[len(q_parts) :]


def in_kernel(start, size, w_ref, x_ref, bias_ref, *out_refs):
    value = dot_tn(w_ref[0, :, start : start + size], x_ref[...]) + bias_ref[...]
    first = 0
    for ref in out_refs:
        ref[...] = value[first : first + ref.shape[0]].astype(ref.dtype)
        first += ref.shape[0]


def gelu_kernel(start, size, w_ref, x_ref, bias_ref, hidden_ref, slope_ref):
    v = dot_tn(w_ref[0, :, start : start + size], x_ref[...]) + bias_ref[...]
    square = v * v
    t = jnp.tanh(0.7978845608 * (v + 0.044715 * square * v))
    hidden_ref[...] = (0.5 * v * (1.0 + t)).astype(BF)
    slope_ref[...] = 0.5 * (1.0 + t) + 0.5 * v * (1.0 - t * t) * 0.7978845608 * (1.0 + 3.0 * 0.044715 * square)


def slope_kernel(start, size, w_ref, x_ref, slope_ref, grad_ref, sum_ref):
    grad = (dot_tn(w_ref[0, :, start : start + size], x_ref[...]) * slope_ref[...]).astype(BF)
    grad_ref[...] = grad
    sum_ref[...] = jnp.sum(grad.astype(F32), axis=1, keepdims=True)


def apply_in(kernel, weight, span, value, extra, outs):
    half = weight.shape[0]
    args = [weight, value, extra]
    specs = [part_spec(weight.shape, half), whole_spec(value.shape), part_spec(extra.shape, half)]
    outs = [jax.ShapeDtypeStruct((rows, cols), dtype) for rows, cols, dtype in outs]
    kernel = functools.partial(kernel, span[0], span[1])
    return call_parts(kernel, half, args, specs, outs, [part_spec(o.shape, half) for o in outs])


def out_kernel(start, w_ref, *refs):
    v_refs, out_ref, acc_ref = refs[:-2], refs[-2], refs[-1]
    z = pl.program_id(0)
    total = None
    for v_ref in v_refs:
        end = start + v_ref.shape[0]
        part = dot_nn(w_ref[0, :, start:end], v_ref[...])
        total = part if total is None else total + part
        start = end

    @pl.when(z == 0)
    def _():
        acc_ref[...] = total

    @pl.when(z > 0)
    def _():
        acc_ref[...] += total

    @pl.when(z == pl.num_programs(0) - 1)
    def _():
        out_ref[...] = acc_ref[...].astype(out_ref.dtype)


def apply_out(weight, start, values, dtype):
    half = weight.shape[0]
    tokens = values[0].shape[1]
    args = [weight] + list(values)
    out = jax.ShapeDtypeStruct((D, tokens), dtype)
    return call_parts(
        functools.partial(out_kernel, start),
        half,
        args,
        [part_spec(a.shape, half) for a in args],
        out,
        whole_spec(out.shape),
        [pltpu.VMEM((D, tokens), F32)],
    )


def outer_kernel(terms, *refs):
    out_ref = refs[-1]
    rows, chunk = out_ref.shape[0], out_ref.shape[1]
    for r in range(rows):
        block = slice(r * chunk, r * chunk + chunk)
        start, at = 0, 0
        for count in terms:
            total = None
            for i in range(count):
                part = dot_nt(refs[at + i][block, :], refs[at + count + i][...])
                total = part if total is None else total + part
            end = start + refs[at + count].shape[0]
            out_ref[r, :, start:end] = total.astype(BF)
            start, at = end, at + 2 * count


def outer_blocks(pairs, rows, half):
    chunk = D // rows
    sizes = [b[0].shape[0] // half for _, b in pairs]
    specs, args = [], []
    for a, b in pairs:
        specs += [whole_spec(p.shape) for p in a] + [part_spec(p.shape, half) for p in b]
        args += list(a) + list(b)
    out = jax.ShapeDtypeStruct((half * rows, chunk, sum(sizes)), BF)
    out_spec = pl.BlockSpec((rows, chunk, sum(sizes)), lambda z: (z, 0, 0))
    kernel = functools.partial(outer_kernel, [len(a) for a, _ in pairs])
    return call_parts(kernel, half, args, specs, out, out_spec), sizes


def shards(
    block_input,
    text_tokens,
    text_length,
    time_index,
    shift_table,
    time_table,
    query_weight,
    key_weight,
    value_weight,
    query_bias,
    value_bias,
    out_weight,
    out_bias,
    cross_query,
    cross_key,
    cross_value,
    cross_query_bias,
    cross_value_bias,
    cross_out,
    cross_out_bias,
    up_weight,
    up_bias,
    down_weight,
    down_bias,
    out_grad,
):
    rows, cols = lax.axis_size("row"), lax.axis_size("col")
    r, c = lax.axis_index("row"), lax.axis_index("col")
    half = cols // 2
    feat = block_input.shape[1]
    width = 2 * block_input.shape[2] // cols
    texts = text_tokens.shape[1]
    steps = time_table.shape[2]
    ups = up_bias.shape[0]
    core, low_z, micro = r & 1, (c >> 1) & 1, c // half
    at_home = core == low_z

    kv_masks = [1 << b for b in range(2, cols.bit_length() - 2)]
    swap_pairs = []
    for i in range(rows):
        for j in range(cols):
            swap_pairs.append(
                (i * cols + j, ((i & ~1) | ((j >> 1) & 1)) * cols + ((j & ~2) | ((i & 1) << 1)))
            )

    def place_swap(value):
        return lax.ppermute(value, ("row", "col"), swap_pairs)

    def token_blocks(value):
        return value.reshape(2, feat, half, width).transpose(0, 2, 1, 3).reshape(cols, feat, width)

    def tokens_out(value):
        blocks = place_swap(value.astype(BF)).reshape(cols, feat, width)
        blocks = lax.all_to_all(blocks, "col", 0, 0, tiled=True)
        blocks = blocks.reshape(2, half, feat, width).transpose(0, 2, 1, 3)
        return blocks.reshape(2, feat, half * width).astype(F32)

    def gather_pair(value):
        return [value, col_swap(value, cols, 1)]

    def reduce_pair(weight, start, *values):
        other = apply_out(weight, start, [v[1] for v in values], BF)
        received = col_swap(other, cols, 1)
        return apply_out(weight, start, [v[0] for v in values], F32) + received.astype(F32)

    def gather_keys(parts):
        parts = list(parts) + [row_swap(p, rows, 1) for p in parts]
        for mask in kv_masks:
            parts = parts + [col_swap(p, cols, mask) for p in parts]
        return parts

    def add_swapped(parts, swap):
        h = len(parts) // 2
        return [(a.astype(F32) + swap(b).astype(F32)).astype(BF) for a, b in zip(parts[:h], parts[h:])]

    def reduce_keys(parts):
        for mask in reversed(kv_masks):
            parts = add_swapped(parts, lambda p, mask=mask: col_swap(p, cols, mask))
        return add_swapped(parts, lambda p: row_swap(p, rows, 1))

    groups = [[i * cols + 2 * z + y for z in range(half) for i in range(rows)] for y in range(2)]

    def gather_weights(shards_w):
        flat = jnp.concatenate(shards_w, axis=1)
        full = lax.all_gather(flat, ("row", "col"), axis=0, tiled=True, axis_index_groups=groups)
        return full.reshape(half, D, flat.shape[1])

    def reduce_weights(pairs):
        blocks, sizes = outer_blocks(pairs, rows, half)
        flat = blocks.reshape(half * D, sum(sizes))
        own = lax.psum_scatter(flat, ("row", "col"), scatter_dimension=0, tiled=True, axis_index_groups=groups)
        out, start = [], 0
        for size in sizes:
            out.append(own[:, start : start + size].astype(F32))
            start += size
        return out

    first_w = gather_weights(
        [query_weight, key_weight, value_weight, out_weight.T, cross_query, cross_key, cross_value, cross_out.T]
    )
    second_w = gather_weights([up_weight, down_weight.T])

    step_ids = jnp.arange(steps, dtype=jnp.int32)
    onehot = (time_index[:, 0][:, None] == step_ids[None, :]).astype(F32)
    modulation = lax.dot_general(
        onehot,
        time_table.reshape(6 * feat, steps),
        (((1,), (1,)), ((), ())),
        precision=lax.Precision.HIGHEST,
        preferred_element_type=F32,
    ).reshape(2, 6, feat) + shift_table[None]
    same = [
        jnp.broadcast_to(b.reshape(1, -1, feat), (2, b.shape[0] // feat, feat))
        for b in (out_bias, cross_out_bias, down_bias, query_bias, value_bias, cross_query_bias, cross_value_bias, up_bias)
    ]
    lengths = jnp.broadcast_to(text_length.astype(F32)[:, :, None], (2, 1, feat))
    small = jnp.concatenate([modulation, lengths] + same, axis=1).transpose(0, 2, 1)
    small_high = lax.reduce_precision(small, 8, 7)
    small_rest = small - small_high
    small_mid = lax.reduce_precision(small_rest, 8, 7)
    small_low = small_rest - small_mid
    extra = jnp.concatenate(
        [text_tokens.transpose(0, 2, 1)] + [p.astype(BF) for p in (small_high, small_mid, small_low)], axis=2
    )
    blocks = jnp.concatenate([token_blocks(block_input), token_blocks(out_grad), jnp.repeat(extra, half, axis=0)], axis=2)
    blocks = lax.all_to_all(blocks, "col", 0, 0, tiled=True).reshape(D, -1)
    arrived = place_swap(blocks)
    small_n, head = small.shape[2], 2 * width

    def small_of(value):
        parts = [value[:, head + texts + i * small_n : head + texts + (i + 1) * small_n].astype(F32) for i in range(3)]
        return parts[0] + parts[1] + parts[2]

    model_rows = small_of(arrived)
    shift_a, scale_a, gate_a, shift_m, scale_m, gate_m, length_row, out_b, cout_b, down_b = (
        model_rows[:, i : i + 1] for i in range(10)
    )
    length = length_row[0].astype(jnp.int32)
    col_rows = small_of(arrived).reshape(cols, feat, small_n)
    col_rows = jnp.concatenate(
        [
            lax.dynamic_index_in_dim(col_rows, 2 * e + (c & 1), 0, keepdims=False)[:, 10:].T.reshape(-1, 1, feat)
            for e in range(half)
        ],
        axis=1,
    )
    q_b, v_b, cq_b, cv_b = (col_rows[i].reshape(half * feat, 1) for i in range(4))
    up_b = col_rows[4:].transpose(1, 0, 2).reshape(half * ups, 1)
    text_t = arrived[:, head : head + texts]

    resid = arrived[:, :width].astype(F32)
    cot = arrived[:, width:head].astype(F32)
    heads_w, hidden_w = half * feat, half * ups
    qkv_w, out_w, cq_w, ckv_w, cout_w = (
        first_w[:, :, i * feat : j * feat] for i, j in ((0, 3), (3, 4), (4, 5), (5, 7), (7, 8))
    )

    def columns(*parts):
        return jnp.stack([p.reshape(half, feat) for p in parts], axis=1).reshape(-1, 1)

    def heads_in(weight, value, *biases):
        sizes = [1] if len(biases) == 1 else [1, len(biases) - 1]
        outs = [(n * heads_w, value.shape[1], BF) for n in sizes]
        return apply_in(in_kernel, weight, (0, len(biases) * feat), value, columns(*biases), outs)

    none = jnp.zeros((heads_w,), F32)
    normed_a, inv_a = layer_norm(resid)
    attn_full = gather_pair((normed_a * (1.0 + scale_a) + shift_a).astype(BF))
    q_parts, kv_parts = zip(*(heads_in(qkv_w, p, q_b, none, v_b) for p in attn_full))
    kv_all = gather_keys(kv_parts)
    att, lse = attend_forward(q_parts, kv_all, None, half)
    branch_a = reduce_pair(out_w, 0, att) + out_b
    after_attn = resid + gate_a * branch_a
    cross_full = gather_pair(after_attn.astype(BF))
    cq_parts = [heads_in(cq_w, p, cq_b)[0] for p in cross_full]
    ckv = apply_in(in_kernel, ckv_w, (0, 2 * feat), text_t, columns(none, cv_b), [(2 * heads_w, texts, BF)])
    catt, clse = attend_forward(cq_parts, ckv, length, half)
    after_cross = after_attn + reduce_pair(cout_w, 0, catt) + cout_b
    normed_m, inv_m = layer_norm(after_cross)
    mlp_full = gather_pair((normed_m * (1.0 + scale_m) + shift_m).astype(BF))
    hidden_outs = [(hidden_w, width, BF), (hidden_w, width, F32)]
    hidden, slope = zip(*(apply_in(gelu_kernel, second_w, (0, ups), p, up_b, hidden_outs) for p in mlp_full))
    branch_m = reduce_pair(second_w, ups, hidden) + down_b
    block_output = tokens_out(after_cross + gate_m * branch_m)

    grad_mlp = gate_m * cot
    low_full = gather_pair(grad_mlp.astype(BF))
    g_down_b = jnp.sum(grad_mlp, axis=1)
    g_gate_m = jnp.sum(cot * branch_m, axis=1)
    pre_outs = [(hidden_w, width, BF), (hidden_w, 1, F32)]
    grad_pre, pre_sums = zip(
        *(apply_in(slope_kernel, second_w, (ups, ups), p, d, pre_outs) for p, d in zip(low_full, slope))
    )
    g_up_b = pre_sums[0] + pre_sums[1]
    back_in = reduce_pair(second_w, 0, grad_pre)
    g_up, g_down = reduce_weights([(mlp_full, grad_pre), (low_full, hidden)])
    back_m, g_shift_m, g_scale_m = norm_backward(back_in, normed_m, inv_m, scale_m)
    grad_cross = cot + back_m
    g_cout_b = jnp.sum(grad_cross, axis=1)
    low_cross = gather_pair(grad_cross.astype(BF))
    dcatt = [heads_in(cout_w, p, none)[0] for p in low_cross]
    dcq, dckv = attend_backward(cq_parts, ckv, length, clse, dcatt, half)
    grad_res = grad_cross + reduce_pair(cq_w, 0, dcq)
    g_cq, g_ckv, g_cout = reduce_weights([(cross_full, dcq), ([text_t], dckv), (low_cross, catt)])
    g_ck, g_cv = g_ckv[:, :feat], g_ckv[:, feat:]
    g_cq_b = jnp.sum(sum(p.astype(F32) for p in dcq), axis=1)
    g_cv_b = jnp.sum(dckv[0].astype(F32).reshape(half, 2, feat, texts)[:, 1], axis=2)
    g_gate_a = jnp.sum(grad_res * branch_a, axis=1)
    grad_attn = gate_a * grad_res
    g_out_b = jnp.sum(grad_attn, axis=1)
    low_attn = gather_pair(grad_attn.astype(BF))
    datt = [heads_in(out_w, p, none)[0] for p in low_attn]
    dq, dkv = attend_backward(q_parts, kv_all, None, lse, datt, half)
    dkv = reduce_keys(dkv)
    back_att = reduce_pair(qkv_w, 0, dq, dkv)
    g_q, g_kv, g_out = reduce_weights([(attn_full, dq), (attn_full, dkv), (low_attn, att)])
    g_k, g_v = g_kv[:, :feat], g_kv[:, feat:]
    g_q_b = jnp.sum(sum(p.astype(F32) for p in dq), axis=1)
    g_v_b = jnp.sum(sum(p.astype(F32) for p in dkv).reshape(half, 2, feat, width)[:, 1], axis=2)
    back_a, g_shift_a, g_scale_a = norm_backward(back_att, normed_a, inv_a, scale_a)
    grad_input = tokens_out(grad_res + back_a)
    grad_text = apply_out(ckv_w, 0, dckv, BF)
    grad_text = grad_text.astype(F32) + row_swap(grad_text, rows, 1).astype(F32)
    grad_text = jnp.where(at_home, grad_text, 0.0).astype(BF).reshape(cols, feat, texts)
    grad_text = lax.all_to_all(grad_text, "col", 0, 0, tiled=True)
    grad_text = jnp.sum(grad_text.reshape(2, half, feat, texts).astype(F32), axis=1).transpose(0, 2, 1)

    model_g = jnp.stack(
        [g_shift_a, g_scale_a, g_gate_a, g_shift_m, g_scale_m, g_gate_m, g_out_b, g_cout_b, g_down_b], axis=1
    )
    model_g = model_g.T.reshape(9, cols, feat).transpose(1, 0, 2)
    per_col = ups // feat
    col_g = jnp.concatenate(
        [g.reshape(half, 1, feat) for g in (g_q_b, g_v_b, g_cq_b, g_cv_b)] + [g_up_b.reshape(half, per_col, feat)],
        axis=1,
    )
    side = c & 1
    blocks = []
    for j in range(cols):
        blocks.append(jnp.where(side == (j & 1), col_g[j >> 1], 0.0))
    small_g = jnp.concatenate([model_g, jnp.stack(blocks)], axis=1)
    small_g = lax.all_to_all(small_g, "col", 0, 0, tiled=True)
    mod_g = small_g[:, :6].reshape(2, cols // 8, 2, 2, 6, feat).sum(axis=(1, 3))
    bias_g = small_g[:, 6:].sum(axis=0)
    step_rows = jnp.broadcast_to(time_index.astype(F32), (2, feat))
    small_g = lax.all_gather(jnp.concatenate([mod_g.reshape(24, feat), bias_g, step_rows], axis=0), "row")
    step_all = small_g[:, -2:, 0].T.reshape(2 * rows).astype(jnp.int32)
    mod_g = small_g[:, :24].reshape(rows // 2, 2, 2, 2, 6, feat).sum(axis=1)
    mod_g = mod_g.transpose(1, 0, 2, 3, 4).reshape(2 * rows, 6, feat)
    bias_g = small_g[:, 24:-2].sum(axis=0)
    g_shift = mod_g.sum(axis=0)
    onehot_all = (step_all[:, None] == step_ids[None, :]).astype(F32)
    g_time = lax.dot_general(
        mod_g.reshape(2 * rows, 6 * feat),
        onehot_all,
        (((0,), (0,)), ((), ())),
        precision=lax.Precision.HIGHEST,
        preferred_element_type=F32,
    ).reshape(6, feat, steps)
    g_out_b, g_cout_b, g_down_b, g_q_b, g_v_b, g_cq_b, g_cv_b = (bias_g[i] for i in range(7))
    g_up_b = bias_g[7:].reshape(ups)
    return (
        block_output,
        grad_input,
        grad_text,
        g_shift,
        g_time,
        g_q,
        g_k,
        g_v,
        g_q_b,
        g_v_b,
        g_out.T,
        g_out_b,
        g_cq,
        g_ck,
        g_cv,
        g_cq_b,
        g_cv_b,
        g_cout.T,
        g_cout_b,
        g_up,
        g_up_b,
        g_down.T,
        g_down_b,
    )


def solution(mesh):
    return jax.shard_map(
        shards,
        mesh=mesh,
        in_specs=(
            P(None, "col", "row"),
            P(None, "row", "col"),
            P(None, "row"),
            P(None, "row"),
            P(None, "col"),
            P(None, "col", None),
            P("row", "col"),
            P("row", "col"),
            P("row", "col"),
            P("col"),
            P("col"),
            P("col", "row"),
            P("col"),
            P("row", "col"),
            P("row", "col"),
            P("row", "col"),
            P("col"),
            P("col"),
            P("col", "row"),
            P("col"),
            P("row", "col"),
            P("col"),
            P("col", "row"),
            P("col"),
            P(None, "col", "row"),
        ),
        out_specs=(
            P(None, "col", "row"),
            P(None, "col", "row"),
            P(None, "row", "col"),
            P(None, "col"),
            P(None, "col", None),
            P("row", "col"),
            P("row", "col"),
            P("row", "col"),
            P("col"),
            P("col"),
            P("col", "row"),
            P("col"),
            P("row", "col"),
            P("row", "col"),
            P("row", "col"),
            P("col"),
            P("col"),
            P("col", "row"),
            P("col"),
            P("row", "col"),
            P("col"),
            P("col", "row"),
            P("col"),
        ),
        check_vma=False,
    )
```

```python
import functools

import jax
import jax.numpy as jnp
from jax import lax
from jax.experimental import pallas as pl
from jax.experimental.pallas import tpu as pltpu
from jax.sharding import PartitionSpec as P

D = 1152
HEADS = 16
HD = 72

NORM_EPS = 1e-06
MASK_FILL = -1e30
BF = jnp.bfloat16
F32 = jnp.float32
LOG_SCALE = HD ** -0.5 * 1.4426950408889634


def dot_nn(a, b):
    return lax.dot_general(a, b, (((1,), (0,)), ((), ())), preferred_element_type=F32)


def dot_tn(a, b):
    return lax.dot_general(a, b, (((0,), (0,)), ((), ())), preferred_element_type=F32)


def dot_nt(a, b):
    return lax.dot_general(a, b, (((1,), (1,)), ((), ())), preferred_element_type=F32)


def after(value, *deps):
    return lax.optimization_barrier((value,) + deps)[0]


def row_swap(value, rows, bit):
    return lax.ppermute(value, "row", [(i, i ^ bit) for i in range(rows)])


def col_swap(value, cols, mask):
    return lax.ppermute(value, "col", [(i, i ^ mask) for i in range(cols)])


def layer_norm(resid):
    mean = jnp.mean(resid, axis=0, keepdims=True)
    centered = resid - mean
    var = jnp.mean(centered * centered, axis=0, keepdims=True)
    inv = lax.rsqrt(var + NORM_EPS)
    return centered * inv, inv


def norm_backward(grad, normed, inv, scale):
    dn = grad * (1.0 + scale)
    first = jnp.mean(dn, axis=0, keepdims=True)
    second = jnp.mean(dn * normed, axis=0, keepdims=True)
    back = (dn - first - normed * second) * inv
    return back, jnp.sum(grad, axis=1), jnp.sum(grad * normed, axis=1)


def dot_at(a, b, a_dim, b_dim):
    return lax.dot_general(a, b, (((a_dim,), (b_dim,)), ((), ())), preferred_element_type=F32)


def masked_scores(scores, len_ref):
    if len_ref is None:
        return scores
    return jnp.where(lax.broadcasted_iota(jnp.int32, scores.shape, 1) < len_ref[0], scores, MASK_FILL)


def join(refs, rows):
    return jnp.concatenate([ref[rows, :] for ref in refs], axis=1)


def put(refs, rows, value):
    start = 0
    for ref in refs:
        end = start + ref.shape[1]
        ref[rows, :] = value[:, start:end].astype(ref.dtype)
        start = end


def head_rows(h, first):
    return slice(first + HD * h, first + HD * h + HD)


def forward_kernel(n_q, n_kv, has_len, *refs):
    len_ref = refs[0] if has_len else None
    refs = refs[1:] if has_len else refs
    q_refs, kv_refs, out_refs, lse_ref = refs[:n_q], refs[n_q : n_q + n_kv], refs[n_q + n_kv : -1], refs[-1]
    feat = q_refs[0].shape[0]
    for h in range(feat // HD):
        head, value_rows = head_rows(h, 0), head_rows(h, feat)
        q, k, v = join(q_refs, head), join(kv_refs, head), join(kv_refs, value_rows)
        scores = masked_scores(dot_at(q, k, 0, 0), len_ref)
        top = jnp.max(scores, axis=1, keepdims=True)
        probs = jnp.exp2((scores - top) * LOG_SCALE)
        total = jnp.sum(probs, axis=1, keepdims=True)
        out = dot_at(probs.astype(BF), v, 1, 1) / total
        put(out_refs, head, out.T)
        lse_ref[0, :, h : h + 1] = top * LOG_SCALE + jnp.log2(total)


def backward_kernel(n_q, n_kv, has_len, *refs):
    len_ref = refs[0] if has_len else None
    refs = refs[1:] if has_len else refs
    q_refs, kv_refs, lse_ref = refs[:n_q], refs[n_q : n_q + n_kv], refs[n_q + n_kv]
    refs = refs[n_q + n_kv + 1 :]
    do_refs, dq_refs, dkv_refs = refs[:n_q], refs[n_q : 2 * n_q], refs[2 * n_q :]
    feat = q_refs[0].shape[0]
    for h in range(feat // HD):
        head, value_rows = head_rows(h, 0), head_rows(h, feat)
        q, k, v, do = join(q_refs, head), join(kv_refs, head), join(kv_refs, value_rows), join(do_refs, head)
        scores = masked_scores(dot_at(q, k, 0, 0), len_ref)
        probs = jnp.exp2(scores * LOG_SCALE - lse_ref[0, :, h : h + 1])
        put(dkv_refs, value_rows, dot_at(do, probs.astype(BF), 1, 0))
        dp = dot_at(do, v, 0, 0)
        ds = probs * (dp - jnp.sum(dp * probs, axis=1, keepdims=True)) * HD ** -0.5
        ds = ds.astype(BF)
        put(dq_refs, head, dot_at(ds, k, 1, 1).T)
        put(dkv_refs, head, dot_at(q, ds, 1, 0))


def part_spec(shape, steps):
    if len(shape) == 3:
        return pl.BlockSpec((1,) + tuple(shape[1:]), lambda z: (z, 0, 0))
    return pl.BlockSpec((shape[0] // steps, shape[1]), lambda z: (z, 0))


def whole_spec(shape):
    return pl.BlockSpec(tuple(shape), lambda z: (0,) * len(shape))


def call_parts(kernel, steps, args, arg_specs, outs, out_specs, scratch=()):
    return pl.pallas_call(
        kernel,
        grid=(steps,),
        in_specs=arg_specs,
        out_specs=out_specs,
        out_shape=outs,
        scratch_shapes=list(scratch),
        compiler_params=pltpu.CompilerParams(vmem_limit_bytes=50 * 2**20),
    )(*args)


def attend_forward(q_parts, kv_parts, length, half):
    rows, tokens = q_parts[0].shape[0], sum(q.shape[1] for q in q_parts)
    outs = [jax.ShapeDtypeStruct(q.shape, BF) for q in q_parts]
    outs.append(jax.ShapeDtypeStruct((half, tokens, rows // half // HD), F32))
    args = list(q_parts) + list(kv_parts)
    specs = [part_spec(a.shape, half) for a in args]
    if length is not None:
        args, specs = [length] + args, [pl.BlockSpec(memory_space=pltpu.SMEM)] + specs
    kernel = functools.partial(forward_kernel, len(q_parts), len(kv_parts), length is not None)
    res = call_parts(kernel, half, args, specs, outs, [part_spec(o.shape, half) for o in outs])
    return res[:-1], res[-1]


def attend_backward(q_parts, kv_parts, length, lse, do_parts, half):
    outs = [jax.ShapeDtypeStruct(a.shape, BF) for a in list(q_parts) + list(kv_parts)]
    args = list(q_parts) + list(kv_parts) + [lse] + list(do_parts)
    specs = [part_spec(a.shape, half) for a in args]
    if length is not None:
        args, specs = [length] + args, [pl.BlockSpec(memory_space=pltpu.SMEM)] + specs
    kernel = functools.partial(backward_kernel, len(q_parts), len(kv_parts), length is not None)
    res = call_parts(kernel, half, args, specs, outs, [part_spec(o.shape, half) for o in outs])
    return res[: len(q_parts)], res[len(q_parts) :]


class View:
    def __init__(self, weight, block, indices, start, size):
        self.weight, self.block, self.indices, self.start, self.size = weight, block, indices, start, size

    def args(self):
        return [self.weight] * len(self.indices)

    def specs(self):
        return [pl.BlockSpec((1, D, self.block), lambda z, i=i: (z, 0, i)) for i in self.indices]

    def load(self, refs):
        if len(refs) == 1:
            return refs[0][0, :, self.start : self.start + self.size]
        value = jnp.concatenate([ref[0] for ref in refs], axis=1)
        return value[:, self.start : self.start + self.size]


def view_of(weight, start, size):
    lanes = weight.shape[2]
    best = None
    for block in range(128, lanes, 128):
        first, last = start // block, (start + size - 1) // block
        if (last + 1) * block > lanes and block * (last + 1) - lanes >= 128:
            continue
        cost = (block * (last - first + 1), last - first)
        if last - first < 2 and (best is None or cost < best[0]):
            best = (cost, block, list(range(first, last + 1)), start - first * block)
    if best is None:
        return View(weight, lanes, [0], start, size)
    return View(weight, best[1], best[2], best[3], size)


def store_rows(value, refs):
    first = 0
    for ref in refs:
        ref[...] = value[first : first + ref.shape[0]].astype(ref.dtype)
        first += ref.shape[0]


def in_kernel(view, n_x, *refs):
    n = len(view.indices)
    w, x_refs, bias_ref, out_refs = view.load(refs[:n]), refs[n : n + n_x], refs[n + n_x], refs[n + n_x + 1 :]
    store_rows(dot_tn(w, x_refs[0][...]) + bias_ref[...], out_refs)


def gelu_kernel(view, n_x, *refs):
    n = len(view.indices)
    w, x_refs, bias_ref, out_refs = view.load(refs[:n]), refs[n : n + n_x], refs[n + n_x], refs[n + n_x + 1 :]
    x = jnp.concatenate([ref[...] for ref in x_refs], axis=1)
    v = dot_tn(w, x) + bias_ref[...]
    square = v * v
    t = jnp.tanh(0.7978845608 * (v + 0.044715 * square * v))
    hidden = 0.5 * v * (1.0 + t)
    slope = 0.5 * (1.0 + t) + 0.5 * v * (1.0 - t * t) * 0.7978845608 * (1.0 + 3.0 * 0.044715 * square)
    put(out_refs[:n_x], slice(None), hidden)
    out_refs[n_x][...] = slope


def slope_kernel(view, n_x, *refs):
    n = len(view.indices)
    w, x_refs, slope_ref, out_refs = view.load(refs[:n]), refs[n : n + n_x], refs[n + n_x], refs[n + n_x + 1 :]
    x = jnp.concatenate([ref[...] for ref in x_refs], axis=1)
    grad = (dot_tn(w, x) * slope_ref[...]).astype(BF)
    put(out_refs[:n_x], slice(None), grad)
    out_refs[n_x][...] = jnp.sum(grad.astype(F32), axis=1, keepdims=True)


def apply_in(kernel, view, values, extra, outs):
    half = view.weight.shape[0]
    args = view.args() + list(values) + [extra]
    specs = view.specs() + [whole_spec(v.shape) for v in values] + [part_spec(extra.shape, half)]
    outs = [jax.ShapeDtypeStruct((rows, cols), dtype) for rows, cols, dtype in outs]
    kernel = functools.partial(kernel, view, len(values))
    return call_parts(kernel, half, args, specs, outs, [part_spec(o.shape, half) for o in outs])


def out_kernel(view, *refs):
    n = len(view.indices)
    w, v_refs, out_ref, acc_ref = view.load(refs[:n]), refs[n:-2], refs[-2], refs[-1]
    z = pl.program_id(0)
    total, start = None, 0
    for v_ref in v_refs:
        end = start + v_ref.shape[0]
        part = dot_nn(w[:, start:end], v_ref[...])
        total = part if total is None else total + part
        start = end

    @pl.when(z == 0)
    def _():
        acc_ref[...] = total

    @pl.when(z > 0)
    def _():
        acc_ref[...] += total

    @pl.when(z == pl.num_programs(0) - 1)
    def _():
        out_ref[...] = acc_ref[...].astype(out_ref.dtype)


def apply_out(view, values, dtype):
    half = view.weight.shape[0]
    tokens = values[0].shape[1]
    out = jax.ShapeDtypeStruct((D, tokens), dtype)
    return call_parts(
        functools.partial(out_kernel, view),
        half,
        view.args() + list(values),
        view.specs() + [part_spec(v.shape, half) for v in values],
        out,
        whole_spec(out.shape),
        [pltpu.VMEM((D, tokens), F32)],
    )


def pack_kernel(*refs):
    out_ref, start = refs[-1], 0
    for ref in refs[:-1]:
        end = start + ref.shape[0]
        out_ref[:, start:end] = ref[...].T
        start = end


def unpack_kernel(in_ref, *out_refs):
    start = 0
    for ref in out_refs:
        end = start + ref.shape[0]
        ref[...] = in_ref[:, start:end].astype(F32).T
        start = end


def pack(parts):
    out = jax.ShapeDtypeStruct((parts[0].shape[1], sum(p.shape[0] for p in parts)), BF)
    specs = [whole_spec(p.shape) for p in parts]
    return call_parts(pack_kernel, 1, parts, specs, out, whole_spec(out.shape))


def unpack(value, sizes):
    outs = [jax.ShapeDtypeStruct((n, value.shape[0]), F32) for n in sizes]
    return call_parts(unpack_kernel, 1, [value], [whole_spec(value.shape)], outs, [whole_spec(o.shape) for o in outs])


def outer_kernel(terms, *refs):
    out_ref = refs[-1]
    rows, chunk = out_ref.shape[0], out_ref.shape[1]
    for r in range(rows):
        block = slice(r * chunk, r * chunk + chunk)
        start, at = 0, 0
        for count in terms:
            total = None
            for i in range(count):
                part = dot_nt(refs[at + i][block, :], refs[at + count + i][...])
                total = part if total is None else total + part
            end = start + refs[at + count].shape[0]
            out_ref[r, :, start:end] = total.astype(BF)
            start, at = end, at + 2 * count


def outer_blocks(pairs, rows, half):
    chunk = D // rows
    sizes = [b[0].shape[0] // half for _, b in pairs]
    specs, args = [], []
    for a, b in pairs:
        specs += [whole_spec(p.shape) for p in a] + [part_spec(p.shape, half) for p in b]
        args += list(a) + list(b)
    out = jax.ShapeDtypeStruct((half * rows, chunk, sum(sizes)), BF)
    out_spec = pl.BlockSpec((rows, chunk, sum(sizes)), lambda z: (z, 0, 0))
    kernel = functools.partial(outer_kernel, [len(a) for a, _ in pairs])
    return call_parts(kernel, half, args, specs, out, out_spec)


def shards(
    block_input,
    text_tokens,
    text_length,
    time_index,
    shift_table,
    time_table,
    query_weight,
    key_weight,
    value_weight,
    query_bias,
    value_bias,
    out_weight,
    out_bias,
    cross_query,
    cross_key,
    cross_value,
    cross_query_bias,
    cross_value_bias,
    cross_out,
    cross_out_bias,
    up_weight,
    up_bias,
    down_weight,
    down_bias,
    out_grad,
):
    rows, cols = lax.axis_size("row"), lax.axis_size("col")
    r, c = lax.axis_index("row"), lax.axis_index("col")
    half = cols // 2
    feat = block_input.shape[1]
    width = 2 * block_input.shape[2] // cols
    texts = text_tokens.shape[1]
    steps = time_table.shape[2]
    ups = up_bias.shape[0]
    core, low_z, micro = r & 1, (c >> 1) & 1, c // half
    at_home = core == low_z

    kv_masks = [1 << b for b in range(2, cols.bit_length() - 2)]
    swap_pairs = []
    for i in range(rows):
        for j in range(cols):
            swap_pairs.append(
                (i * cols + j, ((i & ~1) | ((j >> 1) & 1)) * cols + ((j & ~2) | ((i & 1) << 1)))
            )

    def place_swap(value):
        return lax.ppermute(value, ("row", "col"), swap_pairs)

    def token_blocks(value):
        return value.reshape(2, feat, half, width).transpose(0, 2, 1, 3).reshape(cols, feat, width)

    def tokens_out(value):
        blocks = place_swap(value.astype(BF)).reshape(cols, feat, width)
        blocks = lax.all_to_all(blocks, "col", 0, 0, tiled=True)
        blocks = blocks.reshape(2, half, feat, width).transpose(0, 2, 1, 3)
        return blocks.reshape(2, feat, half * width).astype(F32)

    def gather_pair(value):
        return [value, col_swap(value, cols, 1)]

    def reduce_pair(view, *values, cover=None):
        other = apply_out(view, [v[1] for v in values], BF)
        received = col_swap(other, cols, 1)
        own = [v[0] for v in values]
        covered = None
        if cover is not None:
            covered = cover(other)
            own[0] = after(own[0], covered)
        return apply_out(view, own, F32) + received.astype(F32), covered

    def gather_keys(parts):
        parts = list(parts) + [row_swap(p, rows, 1) for p in parts]
        for mask in kv_masks:
            parts = parts + [col_swap(p, cols, mask) for p in parts]
        return parts

    def add_swapped(parts, swap):
        h = len(parts) // 2
        return [(a.astype(F32) + swap(b).astype(F32)).astype(BF) for a, b in zip(parts[:h], parts[h:])]

    def reduce_keys(parts):
        for mask in reversed(kv_masks):
            parts = add_swapped(parts, lambda p, mask=mask: col_swap(p, cols, mask))
        return add_swapped(parts, lambda p: row_swap(p, rows, 1))

    groups = [[i * cols + 2 * z + y for z in range(half) for i in range(rows)] for y in range(2)]

    def gather_weights(flat):
        full = lax.all_gather(flat, ("row", "col"), axis=0, tiled=True, axis_index_groups=groups)
        return full.reshape(half, D, flat.shape[1])

    def scatter(blocks):
        flat = blocks.reshape(half * D, blocks.shape[2])
        return lax.psum_scatter(flat, ("row", "col"), scatter_dimension=0, tiled=True, axis_index_groups=groups)

    first_w = gather_weights(
        pack([query_weight.T, key_weight.T, value_weight.T, out_weight, cross_query.T, cross_key.T, cross_value.T, cross_out])
    )
    second_w = gather_weights(jnp.concatenate([up_weight, down_weight.T], axis=1))

    step_ids = jnp.arange(steps, dtype=jnp.int32)
    onehot = (time_index[:, 0][:, None] == step_ids[None, :]).astype(F32)
    modulation = lax.dot_general(
        onehot,
        time_table.reshape(6 * feat, steps),
        (((1,), (1,)), ((), ())),
        precision=lax.Precision.HIGHEST,
        preferred_element_type=F32,
    ).reshape(2, 6, feat) + shift_table[None]
    same = [
        jnp.broadcast_to(b.reshape(1, -1, feat), (2, b.shape[0] // feat, feat))
        for b in (out_bias, cross_out_bias, down_bias, query_bias, value_bias, cross_query_bias, cross_value_bias, up_bias)
    ]
    lengths = jnp.broadcast_to(text_length.astype(F32)[:, :, None], (2, 1, feat))
    small = jnp.concatenate([modulation, lengths] + same, axis=1).transpose(0, 2, 1)
    small_high = lax.reduce_precision(small, 8, 7)
    small_rest = small - small_high
    small_mid = lax.reduce_precision(small_rest, 8, 7)
    small_low = small_rest - small_mid
    extra = jnp.concatenate(
        [text_tokens.transpose(0, 2, 1)] + [p.astype(BF) for p in (small_high, small_mid, small_low)], axis=2
    )
    blocks = jnp.concatenate([token_blocks(block_input), token_blocks(out_grad), jnp.repeat(extra, half, axis=0)], axis=2)
    blocks = lax.all_to_all(blocks, "col", 0, 0, tiled=True).reshape(D, -1)
    arrived = place_swap(blocks)
    small_n, head = small.shape[2], 2 * width

    def small_of(value):
        parts = [value[:, head + texts + i * small_n : head + texts + (i + 1) * small_n].astype(F32) for i in range(3)]
        return parts[0] + parts[1] + parts[2]

    model_rows = small_of(arrived)
    shift_a, scale_a, gate_a, shift_m, scale_m, gate_m, length_row, out_b, cout_b, down_b = (
        model_rows[:, i : i + 1] for i in range(10)
    )
    length = length_row[0].astype(jnp.int32)
    col_rows = small_of(arrived).reshape(cols, feat, small_n)
    col_rows = jnp.concatenate(
        [
            lax.dynamic_index_in_dim(col_rows, 2 * e + (c & 1), 0, keepdims=False)[:, 10:].T.reshape(-1, 1, feat)
            for e in range(half)
        ],
        axis=1,
    )
    q_b, v_b, cq_b, cv_b = (col_rows[i].reshape(half * feat, 1) for i in range(4))
    up_b = col_rows[4:].transpose(1, 0, 2).reshape(half * ups, 1)
    text_t = arrived[:, head : head + texts]

    resid = arrived[:, :width].astype(F32)
    cot = arrived[:, width:head].astype(F32)
    heads_w, hidden_w = half * feat, half * ups
    qkv_w, out_w, cq_w, ckv_w, cout_w = (
        view_of(first_w, i * feat, (j - i) * feat) for i, j in ((0, 3), (3, 4), (4, 5), (5, 7), (7, 8))
    )
    up_w, down_w = view_of(second_w, 0, ups), view_of(second_w, ups, ups)

    def columns(*parts):
        return jnp.stack([p.reshape(half, feat) for p in parts], axis=1).reshape(-1, 1)

    def heads_in(weight, value, *biases):
        sizes = [1] if len(biases) == 1 else [1, len(biases) - 1]
        outs = [(n * heads_w, value.shape[1], BF) for n in sizes]
        return apply_in(in_kernel, weight, [value], columns(*biases), outs)

    none = jnp.zeros((heads_w,), F32)
    normed_a, inv_a = layer_norm(resid)
    attn_full = gather_pair((normed_a * (1.0 + scale_a) + shift_a).astype(BF))
    q_parts, kv_parts = zip(*(heads_in(qkv_w, p, q_b, none, v_b) for p in attn_full))
    kv_all = gather_keys(kv_parts)
    att, lse = attend_forward(q_parts, kv_all, None, half)
    branch_a = reduce_pair(out_w, att)[0] + out_b
    after_attn = resid + gate_a * branch_a
    cross_full = gather_pair(after_attn.astype(BF))
    cq_parts = [heads_in(cq_w, p, cq_b)[0] for p in cross_full]
    ckv = apply_in(in_kernel, ckv_w, [text_t], columns(none, cv_b), [(2 * heads_w, texts, BF)])
    catt, clse = attend_forward(cq_parts, ckv, length, half)
    after_cross = after_attn + reduce_pair(cout_w, catt)[0] + cout_b
    normed_m, inv_m = layer_norm(after_cross)
    mlp_full = gather_pair((normed_m * (1.0 + scale_m) + shift_m).astype(BF))
    hidden_outs = [(hidden_w, width, BF)] * 2
    *hidden, slope = apply_in(gelu_kernel, up_w, mlp_full, up_b, hidden_outs + [(hidden_w, 2 * width, F32)])
    branch_m = reduce_pair(down_w, hidden)[0] + down_b
    block_output = tokens_out(after_cross + gate_m * branch_m)

    grad_mlp = gate_m * cot
    low_full = gather_pair(grad_mlp.astype(BF))
    g_down_b = jnp.sum(grad_mlp, axis=1)
    g_gate_m = jnp.sum(cot * branch_m, axis=1)
    *grad_pre, g_up_b = apply_in(slope_kernel, down_w, low_full, slope, hidden_outs + [(hidden_w, 1, F32)])

    def mlp_cover(other):
        return outer_blocks([(mlp_full, grad_pre), (low_full, [after(hidden[0], other), hidden[1]])], rows, half)

    back_in, mlp_blocks = reduce_pair(up_w, grad_pre, cover=mlp_cover)
    mlp_grads = scatter(mlp_blocks)
    back_m, g_shift_m, g_scale_m = norm_backward(back_in, normed_m, inv_m, scale_m)
    grad_cross = cot + back_m
    g_cout_b = jnp.sum(grad_cross, axis=1)
    low_cross = gather_pair(grad_cross.astype(BF))
    dcatt = [heads_in(cout_w, p, none)[0] for p in low_cross]
    dcq, dckv = attend_backward(cq_parts, ckv, length, clse, dcatt, half)
    grad_res = grad_cross + reduce_pair(cq_w, dcq)[0]
    g_cq_b = jnp.sum(sum(p.astype(F32) for p in dcq), axis=1)
    g_cv_b = jnp.sum(dckv[0].astype(F32).reshape(half, 2, feat, texts)[:, 1], axis=2)
    g_gate_a = jnp.sum(grad_res * branch_a, axis=1)
    grad_attn = gate_a * grad_res
    g_out_b = jnp.sum(grad_attn, axis=1)
    low_attn = gather_pair(grad_attn.astype(BF))
    datt = [heads_in(out_w, p, none)[0] for p in low_attn]
    dq, dkv = attend_backward(q_parts, kv_all, None, lse, datt, half)
    dkv = reduce_keys(dkv)

    def attention_cover(other):
        pairs = [(attn_full, dq), (attn_full, dkv), (low_attn, att), (cross_full, dcq), ([text_t], dckv), (low_cross, catt)]
        return outer_blocks([(pairs[0][0], [after(dq[0], other), dq[1]])] + pairs[1:], rows, half)

    back_att, att_blocks = reduce_pair(qkv_w, dq, dkv, cover=attention_cover)
    att_grads = scatter(att_blocks)
    g_q, g_k, g_v, g_out, g_cq, g_ck, g_cv, g_cout = unpack(att_grads, [feat] * 8)
    g_up, g_down = mlp_grads[:, :ups].astype(F32), mlp_grads[:, ups:].astype(F32)
    g_q_b = jnp.sum(sum(p.astype(F32) for p in dq), axis=1)
    g_v_b = jnp.sum(sum(p.astype(F32) for p in dkv).reshape(half, 2, feat, width)[:, 1], axis=2)
    back_a, g_shift_a, g_scale_a = norm_backward(back_att, normed_a, inv_a, scale_a)
    grad_input = tokens_out(grad_res + back_a)
    grad_text = apply_out(ckv_w, dckv, BF)
    grad_text = grad_text.astype(F32) + row_swap(grad_text, rows, 1).astype(F32)
    grad_text = jnp.where(at_home, grad_text, 0.0).astype(BF).reshape(cols, feat, texts)
    grad_text = lax.all_to_all(grad_text, "col", 0, 0, tiled=True)
    grad_text = jnp.sum(grad_text.reshape(2, half, feat, texts).astype(F32), axis=1).transpose(0, 2, 1)

    model_g = jnp.stack(
        [g_shift_a, g_scale_a, g_gate_a, g_shift_m, g_scale_m, g_gate_m, g_out_b, g_cout_b, g_down_b], axis=1
    )
    model_g = model_g.T.reshape(9, cols, feat).transpose(1, 0, 2)
    per_col = ups // feat
    col_g = jnp.concatenate(
        [g.reshape(half, 1, feat) for g in (g_q_b, g_v_b, g_cq_b, g_cv_b)] + [g_up_b.reshape(half, per_col, feat)],
        axis=1,
    )
    side = c & 1
    blocks = []
    for j in range(cols):
        blocks.append(jnp.where(side == (j & 1), col_g[j >> 1], 0.0))
    small_g = jnp.concatenate([model_g, jnp.stack(blocks)], axis=1)
    small_g = lax.all_to_all(small_g, "col", 0, 0, tiled=True)
    mod_g = small_g[:, :6].reshape(2, cols // 8, 2, 2, 6, feat).sum(axis=(1, 3))
    bias_g = small_g[:, 6:].sum(axis=0)
    step_rows = jnp.broadcast_to(time_index.astype(F32), (2, feat))
    small_g = lax.all_gather(jnp.concatenate([mod_g.reshape(24, feat), bias_g, step_rows], axis=0), "row")
    step_all = small_g[:, -2:, 0].T.reshape(2 * rows).astype(jnp.int32)
    mod_g = small_g[:, :24].reshape(rows // 2, 2, 2, 2, 6, feat).sum(axis=1)
    mod_g = mod_g.transpose(1, 0, 2, 3, 4).reshape(2 * rows, 6, feat)
    bias_g = small_g[:, 24:-2].sum(axis=0)
    g_shift = mod_g.sum(axis=0)
    onehot_all = (step_all[:, None] == step_ids[None, :]).astype(F32)
    g_time = lax.dot_general(
        mod_g.reshape(2 * rows, 6 * feat),
        onehot_all,
        (((0,), (0,)), ((), ())),
        precision=lax.Precision.HIGHEST,
        preferred_element_type=F32,
    ).reshape(6, feat, steps)
    g_out_b, g_cout_b, g_down_b, g_q_b, g_v_b, g_cq_b, g_cv_b = (bias_g[i] for i in range(7))
    g_up_b = bias_g[7:].reshape(ups)
    return (
        block_output,
        grad_input,
        grad_text,
        g_shift,
        g_time,
        g_q.T,
        g_k.T,
        g_v.T,
        g_q_b,
        g_v_b,
        g_out,
        g_out_b,
        g_cq.T,
        g_ck.T,
        g_cv.T,
        g_cq_b,
        g_cv_b,
        g_cout,
        g_cout_b,
        g_up,
        g_up_b,
        g_down.T,
        g_down_b,
    )


def solution(mesh):
    return jax.shard_map(
        shards,
        mesh=mesh,
        in_specs=(
            P(None, "col", "row"),
            P(None, "row", "col"),
            P(None, "row"),
            P(None, "row"),
            P(None, "col"),
            P(None, "col", None),
            P("row", "col"),
            P("row", "col"),
            P("row", "col"),
            P("col"),
            P("col"),
            P("col", "row"),
            P("col"),
            P("row", "col"),
            P("row", "col"),
            P("row", "col"),
            P("col"),
            P("col"),
            P("col", "row"),
            P("col"),
            P("row", "col"),
            P("col"),
            P("col", "row"),
            P("col"),
            P(None, "col", "row"),
        ),
        out_specs=(
            P(None, "col", "row"),
            P(None, "col", "row"),
            P(None, "row", "col"),
            P(None, "col"),
            P(None, "col", None),
            P("row", "col"),
            P("row", "col"),
            P("row", "col"),
            P("col"),
            P("col"),
            P("col", "row"),
            P("col"),
            P("row", "col"),
            P("row", "col"),
            P("row", "col"),
            P("col"),
            P("col"),
            P("col", "row"),
            P("col"),
            P("row", "col"),
            P("col"),
            P("col", "row"),
            P("col"),
        ),
        check_vma=False,
    )
```

```python
import functools

import jax
import jax.numpy as jnp
from jax import lax
from jax.experimental import pallas as pl
from jax.experimental.pallas import tpu as pltpu
from jax.sharding import PartitionSpec as P

D = 1152
HEADS = 16
HD = 72

NORM_EPS = 1e-06
MASK_FILL = -1e30
BF = jnp.bfloat16
F32 = jnp.float32
LOG_SCALE = HD ** -0.5 * 1.4426950408889634


def dot_nn(a, b):
    return lax.dot_general(a, b, (((1,), (0,)), ((), ())), preferred_element_type=F32)


def dot_tn(a, b):
    return lax.dot_general(a, b, (((0,), (0,)), ((), ())), preferred_element_type=F32)


def dot_nt(a, b):
    return lax.dot_general(a, b, (((1,), (1,)), ((), ())), preferred_element_type=F32)


def after(value, *deps):
    return lax.optimization_barrier((value,) + deps)[0]


def row_swap(value, rows, bit):
    return lax.ppermute(value, "row", [(i, i ^ bit) for i in range(rows)])


def col_swap(value, cols, mask):
    return lax.ppermute(value, "col", [(i, i ^ mask) for i in range(cols)])


def layer_norm(resid):
    mean = jnp.mean(resid, axis=0, keepdims=True)
    centered = resid - mean
    var = jnp.mean(centered * centered, axis=0, keepdims=True)
    inv = lax.rsqrt(var + NORM_EPS)
    return centered * inv, inv


def norm_backward(grad, normed, inv, scale):
    dn = grad * (1.0 + scale)
    first = jnp.mean(dn, axis=0, keepdims=True)
    second = jnp.mean(dn * normed, axis=0, keepdims=True)
    back = (dn - first - normed * second) * inv
    return back, jnp.sum(grad, axis=1), jnp.sum(grad * normed, axis=1)


def dot_at(a, b, a_dim, b_dim):
    return lax.dot_general(a, b, (((a_dim,), (b_dim,)), ((), ())), preferred_element_type=F32)


def masked_scores(scores, len_ref):
    if len_ref is None:
        return scores
    return jnp.where(lax.broadcasted_iota(jnp.int32, scores.shape, 1) < len_ref[0], scores, MASK_FILL)


def join(refs, rows):
    return jnp.concatenate([ref[rows, :] for ref in refs], axis=1)


def put(refs, rows, value):
    start = 0
    for ref in refs:
        end = start + ref.shape[1]
        ref[rows, :] = value[:, start:end].astype(ref.dtype)
        start = end


def head_rows(h, first):
    return slice(first + HD * h, first + HD * h + HD)


def forward_kernel(n_q, n_kv, has_len, *refs):
    len_ref = refs[0] if has_len else None
    refs = refs[1:] if has_len else refs
    q_refs, kv_refs, out_refs, lse_ref = refs[:n_q], refs[n_q : n_q + n_kv], refs[n_q + n_kv : -1], refs[-1]
    feat = q_refs[0].shape[0]
    for h in range(feat // HD):
        head, value_rows = head_rows(h, 0), head_rows(h, feat)
        q, k, v = join(q_refs, head), join(kv_refs, head), join(kv_refs, value_rows)
        scores = masked_scores(dot_at(q, k, 0, 0), len_ref)
        top = jnp.max(scores, axis=1, keepdims=True)
        probs = jnp.exp2((scores - top) * LOG_SCALE)
        total = jnp.sum(probs, axis=1, keepdims=True)
        out = dot_at(probs.astype(BF), v, 1, 1) / total
        put(out_refs, head, out.T)
        lse_ref[0, :, h : h + 1] = top * LOG_SCALE + jnp.log2(total)


def backward_kernel(n_q, n_kv, has_len, *refs):
    len_ref = refs[0] if has_len else None
    refs = refs[1:] if has_len else refs
    q_refs, kv_refs, lse_ref = refs[:n_q], refs[n_q : n_q + n_kv], refs[n_q + n_kv]
    refs = refs[n_q + n_kv + 1 :]
    do_refs, dq_refs, dkv_refs = refs[:n_q], refs[n_q : 2 * n_q], refs[2 * n_q :]
    feat = q_refs[0].shape[0]
    for h in range(feat // HD):
        head, value_rows = head_rows(h, 0), head_rows(h, feat)
        q, k, v, do = join(q_refs, head), join(kv_refs, head), join(kv_refs, value_rows), join(do_refs, head)
        scores = masked_scores(dot_at(q, k, 0, 0), len_ref)
        probs = jnp.exp2(scores * LOG_SCALE - lse_ref[0, :, h : h + 1])
        put(dkv_refs, value_rows, dot_at(do, probs.astype(BF), 1, 0))
        dp = dot_at(do, v, 0, 0)
        ds = probs * (dp - jnp.sum(dp * probs, axis=1, keepdims=True)) * HD ** -0.5
        ds = ds.astype(BF)
        put(dq_refs, head, dot_at(ds, k, 1, 1).T)
        put(dkv_refs, head, dot_at(q, ds, 1, 0))


def part_spec(shape, steps):
    if len(shape) == 3:
        return pl.BlockSpec((1,) + tuple(shape[1:]), lambda z: (z, 0, 0))
    return pl.BlockSpec((shape[0] // steps, shape[1]), lambda z: (z, 0))


def whole_spec(shape):
    return pl.BlockSpec(tuple(shape), lambda z: (0,) * len(shape))


def call_parts(kernel, steps, args, arg_specs, outs, out_specs, scratch=()):
    return pl.pallas_call(
        kernel,
        grid=(steps,),
        in_specs=arg_specs,
        out_specs=out_specs,
        out_shape=outs,
        scratch_shapes=list(scratch),
        compiler_params=pltpu.CompilerParams(vmem_limit_bytes=50 * 2**20),
    )(*args)


def attend_forward(q_parts, kv_parts, length, half):
    rows, tokens = q_parts[0].shape[0], sum(q.shape[1] for q in q_parts)
    outs = [jax.ShapeDtypeStruct(q.shape, BF) for q in q_parts]
    outs.append(jax.ShapeDtypeStruct((half, tokens, rows // half // HD), F32))
    args = list(q_parts) + list(kv_parts)
    specs = [part_spec(a.shape, half) for a in args]
    if length is not None:
        args, specs = [length] + args, [pl.BlockSpec(memory_space=pltpu.SMEM)] + specs
    kernel = functools.partial(forward_kernel, len(q_parts), len(kv_parts), length is not None)
    res = call_parts(kernel, half, args, specs, outs, [part_spec(o.shape, half) for o in outs])
    return res[:-1], res[-1]


def attend_backward(q_parts, kv_parts, length, lse, do_parts, half):
    outs = [jax.ShapeDtypeStruct(a.shape, BF) for a in list(q_parts) + list(kv_parts)]
    args = list(q_parts) + list(kv_parts) + [lse] + list(do_parts)
    specs = [part_spec(a.shape, half) for a in args]
    if length is not None:
        args, specs = [length] + args, [pl.BlockSpec(memory_space=pltpu.SMEM)] + specs
    kernel = functools.partial(backward_kernel, len(q_parts), len(kv_parts), length is not None)
    res = call_parts(kernel, half, args, specs, outs, [part_spec(o.shape, half) for o in outs])
    return res[: len(q_parts)], res[len(q_parts) :]


class View:
    def __init__(self, weight, block, indices, start, size):
        self.weight, self.block, self.indices, self.start, self.size = weight, block, indices, start, size

    def args(self):
        return [self.weight] * len(self.indices)

    def specs(self):
        return [pl.BlockSpec((1, D, self.block), lambda z, i=i: (z, 0, i)) for i in self.indices]

    def load(self, refs):
        if len(refs) == 1:
            return refs[0][0, :, self.start : self.start + self.size]
        value = jnp.concatenate([ref[0] for ref in refs], axis=1)
        return value[:, self.start : self.start + self.size]


def view_of(weight, start, size):
    lanes = weight.shape[2]
    best = None
    for block in range(128, lanes, 128):
        first, last = start // block, (start + size - 1) // block
        if (last + 1) * block > lanes and block * (last + 1) - lanes >= 128:
            continue
        cost = (block * (last - first + 1), last - first)
        if last - first < 2 and (best is None or cost < best[0]):
            best = (cost, block, list(range(first, last + 1)), start - first * block)
    if best is None:
        return View(weight, lanes, [0], start, size)
    return View(weight, best[1], best[2], best[3], size)


def store_rows(value, refs):
    first = 0
    for ref in refs:
        ref[...] = value[first : first + ref.shape[0]].astype(ref.dtype)
        first += ref.shape[0]


def in_kernel(view, n_x, *refs):
    n = len(view.indices)
    w, x_refs, bias_ref, out_refs = view.load(refs[:n]), refs[n : n + n_x], refs[n + n_x], refs[n + n_x + 1 :]
    store_rows(dot_tn(w, x_refs[0][...]) + bias_ref[...], out_refs)


def gelu_kernel(view, n_x, *refs):
    n = len(view.indices)
    w, x_refs, bias_ref, out_refs = view.load(refs[:n]), refs[n : n + n_x], refs[n + n_x], refs[n + n_x + 1 :]
    x = jnp.concatenate([ref[...] for ref in x_refs], axis=1)
    v = dot_tn(w, x) + bias_ref[...]
    square = v * v
    t = jnp.tanh(0.7978845608 * (v + 0.044715 * square * v))
    hidden = 0.5 * v * (1.0 + t)
    slope = 0.5 * (1.0 + t) + 0.5 * v * (1.0 - t * t) * 0.7978845608 * (1.0 + 3.0 * 0.044715 * square)
    put(out_refs[:n_x], slice(None), hidden)
    out_refs[n_x][...] = slope


def slope_kernel(view, n_x, *refs):
    n = len(view.indices)
    w, x_refs, slope_ref, out_refs = view.load(refs[:n]), refs[n : n + n_x], refs[n + n_x], refs[n + n_x + 1 :]
    x = jnp.concatenate([ref[...] for ref in x_refs], axis=1)
    grad = (dot_tn(w, x) * slope_ref[...]).astype(BF)
    put(out_refs[:n_x], slice(None), grad)
    out_refs[n_x][...] = jnp.sum(grad.astype(F32), axis=1, keepdims=True)


def apply_in(kernel, view, values, extra, outs):
    half = view.weight.shape[0]
    args = view.args() + list(values) + [extra]
    specs = view.specs() + [whole_spec(v.shape) for v in values] + [part_spec(extra.shape, half)]
    outs = [jax.ShapeDtypeStruct((rows, cols), dtype) for rows, cols, dtype in outs]
    kernel = functools.partial(kernel, view, len(values))
    return call_parts(kernel, half, args, specs, outs, [part_spec(o.shape, half) for o in outs])


def out_kernel(view, *refs):
    n = len(view.indices)
    w, v_refs, out_ref, acc_ref = view.load(refs[:n]), refs[n:-2], refs[-2], refs[-1]
    z = pl.program_id(0)
    total, start = None, 0
    for v_ref in v_refs:
        end = start + v_ref.shape[0]
        part = dot_nn(w[:, start:end], v_ref[...])
        total = part if total is None else total + part
        start = end

    @pl.when(z == 0)
    def _():
        acc_ref[...] = total

    @pl.when(z > 0)
    def _():
        acc_ref[...] += total

    @pl.when(z == pl.num_programs(0) - 1)
    def _():
        out_ref[...] = acc_ref[...].astype(out_ref.dtype)


def apply_out(view, values, dtype):
    half = view.weight.shape[0]
    tokens = values[0].shape[1]
    out = jax.ShapeDtypeStruct((D, tokens), dtype)
    return call_parts(
        functools.partial(out_kernel, view),
        half,
        view.args() + list(values),
        view.specs() + [part_spec(v.shape, half) for v in values],
        out,
        whole_spec(out.shape),
        [pltpu.VMEM((D, tokens), F32)],
    )


def pack_kernel(*refs):
    out_ref, start = refs[-1], 0
    for ref in refs[:-1]:
        end = start + ref.shape[0]
        out_ref[:, start:end] = ref[...].T
        start = end


def unpack_kernel(in_ref, *out_refs):
    start = 0
    for ref in out_refs:
        end = start + ref.shape[0]
        ref[...] = in_ref[:, start:end].astype(F32).T
        start = end


def pack(parts):
    out = jax.ShapeDtypeStruct((parts[0].shape[1], sum(p.shape[0] for p in parts)), BF)
    specs = [whole_spec(p.shape) for p in parts]
    return call_parts(pack_kernel, 1, parts, specs, out, whole_spec(out.shape))


def unpack(value, sizes):
    outs = [jax.ShapeDtypeStruct((n, value.shape[0]), F32) for n in sizes]
    return call_parts(unpack_kernel, 1, [value], [whole_spec(value.shape)], outs, [whole_spec(o.shape) for o in outs])


def outer_kernel(terms, *refs):
    out_ref = refs[-1]
    rows, chunk = out_ref.shape[0], out_ref.shape[1]
    for r in range(rows):
        block = slice(r * chunk, r * chunk + chunk)
        start, at = 0, 0
        for count in terms:
            total = None
            for i in range(count):
                part = dot_nt(refs[at + i][block, :], refs[at + count + i][...])
                total = part if total is None else total + part
            end = start + refs[at + count].shape[0]
            out_ref[r, :, start:end] = total.astype(BF)
            start, at = end, at + 2 * count


def outer_blocks(pairs, rows, half):
    chunk = D // rows
    sizes = [b[0].shape[0] // half for _, b in pairs]
    specs, args = [], []
    for a, b in pairs:
        specs += [whole_spec(p.shape) for p in a] + [part_spec(p.shape, half) for p in b]
        args += list(a) + list(b)
    out = jax.ShapeDtypeStruct((half * rows, chunk, sum(sizes)), BF)
    out_spec = pl.BlockSpec((rows, chunk, sum(sizes)), lambda z: (z, 0, 0))
    kernel = functools.partial(outer_kernel, [len(a) for a, _ in pairs])
    return call_parts(kernel, half, args, specs, out, out_spec)


def shards(
    block_input,
    text_tokens,
    text_length,
    time_index,
    shift_table,
    time_table,
    query_weight,
    key_weight,
    value_weight,
    query_bias,
    value_bias,
    out_weight,
    out_bias,
    cross_query,
    cross_key,
    cross_value,
    cross_query_bias,
    cross_value_bias,
    cross_out,
    cross_out_bias,
    up_weight,
    up_bias,
    down_weight,
    down_bias,
    out_grad,
):
    rows, cols = lax.axis_size("row"), lax.axis_size("col")
    r, c = lax.axis_index("row"), lax.axis_index("col")
    half = cols // 2
    feat = block_input.shape[1]
    width = 2 * block_input.shape[2] // cols
    texts = text_tokens.shape[1]
    steps = time_table.shape[2]
    ups = up_bias.shape[0]
    core, low_z, micro = r & 1, (c >> 1) & 1, c // half
    at_home = core == low_z

    kv_masks = [1 << b for b in range(2, cols.bit_length() - 2)]
    def home_of(i, j):
        return (i & ~1) | ((j >> 1) & 1), (j & ~2) | ((i & 1) << 1)

    home_r, home_c = home_of(r, c)

    def place_swap(value):
        pairs = []
        for i in range(rows):
            for j in range(cols):
                to_r, to_c = home_of(i, j)
                pairs.append((i * cols + j, to_r * cols + to_c))
        return lax.ppermute(value, ("row", "col"), pairs)

    def send_tokens(blocks):
        full = jnp.zeros_like(blocks)
        for e in range(cols):
            pairs = []
            for i in range(rows):
                for j in range(cols):
                    to_r, to_c = home_of(i, j ^ e)
                    pairs.append((i * cols + j, to_r * cols + to_c))
            part = lax.dynamic_slice_in_dim(blocks, c ^ e, 1, 0)
            part = lax.ppermute(part, ("row", "col"), pairs)
            full = lax.dynamic_update_slice_in_dim(full, part, home_c ^ e, 0)
        return full.reshape(D, blocks.shape[2])

    def token_blocks(value):
        return value.reshape(2, feat, half, width).transpose(0, 2, 1, 3).reshape(cols, feat, width)

    def tokens_out(value):
        blocks = place_swap(value.astype(BF)).reshape(cols, feat, width)
        blocks = lax.all_to_all(blocks, "col", 0, 0, tiled=True)
        blocks = blocks.reshape(2, half, feat, width).transpose(0, 2, 1, 3)
        return blocks.reshape(2, feat, half * width).astype(F32)

    def gather_pair(value):
        return [value, col_swap(value, cols, 1)]

    def reduce_pair(view, *values, cover=None):
        other = apply_out(view, [v[1] for v in values], BF)
        received = col_swap(other, cols, 1)
        own = [v[0] for v in values]
        covered = None
        if cover is not None:
            covered = cover(other)
            own[0] = after(own[0], covered)
        return apply_out(view, own, F32) + received.astype(F32), covered

    def gather_keys(parts):
        parts = list(parts) + [row_swap(p, rows, 1) for p in parts]
        for mask in kv_masks:
            parts = parts + [col_swap(p, cols, mask) for p in parts]
        return parts

    def add_swapped(parts, swap):
        h = len(parts) // 2
        return [(a.astype(F32) + swap(b).astype(F32)).astype(BF) for a, b in zip(parts[:h], parts[h:])]

    def reduce_keys(parts):
        for mask in reversed(kv_masks):
            parts = add_swapped(parts, lambda p, mask=mask: col_swap(p, cols, mask))
        return add_swapped(parts, lambda p: row_swap(p, rows, 1))

    groups = [[i * cols + 2 * z + y for z in range(half) for i in range(rows)] for y in range(2)]

    def gather_weights(flat):
        full = lax.all_gather(flat, ("row", "col"), axis=0, tiled=True, axis_index_groups=groups)
        return full.reshape(half, D, flat.shape[1])

    def scatter(blocks):
        flat = blocks.reshape(half * D, blocks.shape[2])
        return lax.psum_scatter(flat, ("row", "col"), scatter_dimension=0, tiled=True, axis_index_groups=groups)

    first_w = gather_weights(
        pack([query_weight.T, key_weight.T, value_weight.T, out_weight, cross_query.T, cross_key.T, cross_value.T, cross_out])
    )
    second_w = gather_weights(jnp.concatenate([up_weight, down_weight.T], axis=1))

    step_ids = jnp.arange(steps, dtype=jnp.int32)
    onehot = (time_index[:, 0][:, None] == step_ids[None, :]).astype(F32)
    modulation = lax.dot_general(
        onehot,
        time_table.reshape(6 * feat, steps),
        (((1,), (1,)), ((), ())),
        precision=lax.Precision.HIGHEST,
        preferred_element_type=F32,
    ).reshape(2, 6, feat) + shift_table[None]
    same = [
        jnp.broadcast_to(b.reshape(1, -1, feat), (2, b.shape[0] // feat, feat))
        for b in (out_bias, cross_out_bias, down_bias, query_bias, value_bias, cross_query_bias, cross_value_bias, up_bias)
    ]
    lengths = jnp.broadcast_to(text_length.astype(F32)[:, :, None], (2, 1, feat))
    small = jnp.concatenate([modulation, lengths] + same, axis=1).transpose(0, 2, 1)
    small_high = lax.reduce_precision(small, 8, 7)
    small_rest = small - small_high
    small_mid = lax.reduce_precision(small_rest, 8, 7)
    small_low = small_rest - small_mid
    extra = jnp.concatenate(
        [text_tokens.transpose(0, 2, 1)] + [p.astype(BF) for p in (small_high, small_mid, small_low)], axis=2
    )
    arrived = send_tokens(jnp.concatenate([token_blocks(block_input), jnp.repeat(extra, half, axis=0)], axis=2))
    cot_low = send_tokens(token_blocks(after(out_grad, arrived)))
    small_n, head = small.shape[2], width

    def small_of(value):
        parts = [value[:, head + texts + i * small_n : head + texts + (i + 1) * small_n].astype(F32) for i in range(3)]
        return parts[0] + parts[1] + parts[2]

    model_rows = small_of(arrived)
    shift_a, scale_a, gate_a, shift_m, scale_m, gate_m, length_row, out_b, cout_b, down_b = (
        model_rows[:, i : i + 1] for i in range(10)
    )
    length = length_row[0].astype(jnp.int32)
    col_rows = small_of(arrived).reshape(cols, feat, small_n)
    col_rows = jnp.concatenate(
        [
            lax.dynamic_index_in_dim(col_rows, 2 * e + (c & 1), 0, keepdims=False)[:, 10:].T.reshape(-1, 1, feat)
            for e in range(half)
        ],
        axis=1,
    )
    q_b, v_b, cq_b, cv_b = (col_rows[i].reshape(half * feat, 1) for i in range(4))
    up_b = col_rows[4:].transpose(1, 0, 2).reshape(half * ups, 1)
    text_t = arrived[:, head : head + texts]

    resid = arrived[:, :width].astype(F32)
    cot = cot_low.astype(F32)
    heads_w, hidden_w = half * feat, half * ups
    qkv_w, out_w, cq_w, ckv_w, cout_w = (
        view_of(first_w, i * feat, (j - i) * feat) for i, j in ((0, 3), (3, 4), (4, 5), (5, 7), (7, 8))
    )
    up_w, down_w = view_of(second_w, 0, ups), view_of(second_w, ups, ups)

    def columns(*parts):
        return jnp.stack([p.reshape(half, feat) for p in parts], axis=1).reshape(-1, 1)

    def heads_in(weight, value, *biases):
        sizes = [1] if len(biases) == 1 else [1, len(biases) - 1]
        outs = [(n * heads_w, value.shape[1], BF) for n in sizes]
        return apply_in(in_kernel, weight, [value], columns(*biases), outs)

    none = jnp.zeros((heads_w,), F32)
    normed_a, inv_a = layer_norm(resid)
    attn_full = gather_pair((normed_a * (1.0 + scale_a) + shift_a).astype(BF))
    q_parts, kv_parts = zip(*(heads_in(qkv_w, p, q_b, none, v_b) for p in attn_full))
    kv_all = gather_keys(kv_parts)
    att, lse = attend_forward(q_parts, kv_all, None, half)
    branch_a = reduce_pair(out_w, att)[0] + out_b
    after_attn = resid + gate_a * branch_a
    cross_full = gather_pair(after_attn.astype(BF))
    cq_parts = [heads_in(cq_w, p, cq_b)[0] for p in cross_full]
    ckv = apply_in(in_kernel, ckv_w, [text_t], columns(none, cv_b), [(2 * heads_w, texts, BF)])
    catt, clse = attend_forward(cq_parts, ckv, length, half)
    after_cross = after_attn + reduce_pair(cout_w, catt)[0] + cout_b
    normed_m, inv_m = layer_norm(after_cross)
    mlp_full = gather_pair((normed_m * (1.0 + scale_m) + shift_m).astype(BF))
    hidden_outs = [(hidden_w, width, BF)] * 2
    *hidden, slope = apply_in(gelu_kernel, up_w, mlp_full, up_b, hidden_outs + [(hidden_w, 2 * width, F32)])
    branch_m = reduce_pair(down_w, hidden)[0] + down_b
    block_output = tokens_out(after_cross + gate_m * branch_m)

    grad_mlp = gate_m * cot
    low_full = gather_pair(grad_mlp.astype(BF))
    g_down_b = jnp.sum(grad_mlp, axis=1)
    g_gate_m = jnp.sum(cot * branch_m, axis=1)
    *grad_pre, g_up_b = apply_in(slope_kernel, down_w, low_full, slope, hidden_outs + [(hidden_w, 1, F32)])

    def mlp_cover(other):
        return outer_blocks([(mlp_full, grad_pre), (low_full, [after(hidden[0], other), hidden[1]])], rows, half)

    back_in, mlp_blocks = reduce_pair(up_w, grad_pre, cover=mlp_cover)
    mlp_grads = scatter(mlp_blocks)
    back_m, g_shift_m, g_scale_m = norm_backward(back_in, normed_m, inv_m, scale_m)
    grad_cross = cot + back_m
    g_cout_b = jnp.sum(grad_cross, axis=1)
    low_cross = gather_pair(grad_cross.astype(BF))
    dcatt = [heads_in(cout_w, p, none)[0] for p in low_cross]
    dcq, dckv = attend_backward(cq_parts, ckv, length, clse, dcatt, half)
    grad_res = grad_cross + reduce_pair(cq_w, dcq)[0]
    g_cq_b = jnp.sum(sum(p.astype(F32) for p in dcq), axis=1)
    g_cv_b = jnp.sum(dckv[0].astype(F32).reshape(half, 2, feat, texts)[:, 1], axis=2)
    g_gate_a = jnp.sum(grad_res * branch_a, axis=1)
    grad_attn = gate_a * grad_res
    g_out_b = jnp.sum(grad_attn, axis=1)
    low_attn = gather_pair(grad_attn.astype(BF))
    datt = [heads_in(out_w, p, none)[0] for p in low_attn]
    dq, dkv = attend_backward(q_parts, kv_all, None, lse, datt, half)
    dkv = reduce_keys(dkv)

    def attention_cover(other):
        pairs = [(attn_full, dq), (attn_full, dkv), (low_attn, att), (cross_full, dcq), ([text_t], dckv), (low_cross, catt)]
        return outer_blocks([(pairs[0][0], [after(dq[0], other), dq[1]])] + pairs[1:], rows, half)

    back_att, att_blocks = reduce_pair(qkv_w, dq, dkv, cover=attention_cover)
    att_grads = scatter(att_blocks)
    g_q, g_k, g_v, g_out, g_cq, g_ck, g_cv, g_cout = unpack(att_grads, [feat] * 8)
    g_up, g_down = mlp_grads[:, :ups].astype(F32), mlp_grads[:, ups:].astype(F32)
    g_q_b = jnp.sum(sum(p.astype(F32) for p in dq), axis=1)
    g_v_b = jnp.sum(sum(p.astype(F32) for p in dkv).reshape(half, 2, feat, width)[:, 1], axis=2)
    back_a, g_shift_a, g_scale_a = norm_backward(back_att, normed_a, inv_a, scale_a)
    grad_input = tokens_out(grad_res + back_a)
    grad_text = apply_out(ckv_w, dckv, BF)
    grad_text = grad_text.astype(F32) + row_swap(grad_text, rows, 1).astype(F32)
    grad_text = jnp.where(at_home, grad_text, 0.0).astype(BF).reshape(cols, feat, texts)
    grad_text = lax.all_to_all(grad_text, "col", 0, 0, tiled=True)
    grad_text = jnp.sum(grad_text.reshape(2, half, feat, texts).astype(F32), axis=1).transpose(0, 2, 1)

    model_g = jnp.stack(
        [g_shift_a, g_scale_a, g_gate_a, g_shift_m, g_scale_m, g_gate_m, g_out_b, g_cout_b, g_down_b], axis=1
    )
    model_g = model_g.T.reshape(9, cols, feat).transpose(1, 0, 2)
    per_col = ups // feat
    col_g = jnp.concatenate(
        [g.reshape(half, 1, feat) for g in (g_q_b, g_v_b, g_cq_b, g_cv_b)] + [g_up_b.reshape(half, per_col, feat)],
        axis=1,
    )
    side = c & 1
    blocks = []
    for j in range(cols):
        blocks.append(jnp.where(side == (j & 1), col_g[j >> 1], 0.0))
    small_g = jnp.concatenate([model_g, jnp.stack(blocks)], axis=1)
    small_g = lax.all_to_all(small_g, "col", 0, 0, tiled=True)
    mod_g = small_g[:, :6].reshape(2, cols // 8, 2, 2, 6, feat).sum(axis=(1, 3))
    bias_g = small_g[:, 6:].sum(axis=0)
    step_rows = jnp.broadcast_to(time_index.astype(F32), (2, feat))
    small_g = lax.all_gather(jnp.concatenate([mod_g.reshape(24, feat), bias_g, step_rows], axis=0), "row")
    step_all = small_g[:, -2:, 0].T.reshape(2 * rows).astype(jnp.int32)
    mod_g = small_g[:, :24].reshape(rows // 2, 2, 2, 2, 6, feat).sum(axis=1)
    mod_g = mod_g.transpose(1, 0, 2, 3, 4).reshape(2 * rows, 6, feat)
    bias_g = small_g[:, 24:-2].sum(axis=0)
    g_shift = mod_g.sum(axis=0)
    onehot_all = (step_all[:, None] == step_ids[None, :]).astype(F32)
    g_time = lax.dot_general(
        mod_g.reshape(2 * rows, 6 * feat),
        onehot_all,
        (((0,), (0,)), ((), ())),
        precision=lax.Precision.HIGHEST,
        preferred_element_type=F32,
    ).reshape(6, feat, steps)
    g_out_b, g_cout_b, g_down_b, g_q_b, g_v_b, g_cq_b, g_cv_b = (bias_g[i] for i in range(7))
    g_up_b = bias_g[7:].reshape(ups)
    return (
        block_output,
        grad_input,
        grad_text,
        g_shift,
        g_time,
        g_q.T,
        g_k.T,
        g_v.T,
        g_q_b,
        g_v_b,
        g_out,
        g_out_b,
        g_cq.T,
        g_ck.T,
        g_cv.T,
        g_cq_b,
        g_cv_b,
        g_cout,
        g_cout_b,
        g_up,
        g_up_b,
        g_down.T,
        g_down_b,
    )


def solution(mesh):
    return jax.shard_map(
        shards,
        mesh=mesh,
        in_specs=(
            P(None, "col", "row"),
            P(None, "row", "col"),
            P(None, "row"),
            P(None, "row"),
            P(None, "col"),
            P(None, "col", None),
            P("row", "col"),
            P("row", "col"),
            P("row", "col"),
            P("col"),
            P("col"),
            P("col", "row"),
            P("col"),
            P("row", "col"),
            P("row", "col"),
            P("row", "col"),
            P("col"),
            P("col"),
            P("col", "row"),
            P("col"),
            P("row", "col"),
            P("col"),
            P("col", "row"),
            P("col"),
            P(None, "col", "row"),
        ),
        out_specs=(
            P(None, "col", "row"),
            P(None, "col", "row"),
            P(None, "row", "col"),
            P(None, "col"),
            P(None, "col", None),
            P("row", "col"),
            P("row", "col"),
            P("row", "col"),
            P("col"),
            P("col"),
            P("col", "row"),
            P("col"),
            P("row", "col"),
            P("row", "col"),
            P("row", "col"),
            P("col"),
            P("col"),
            P("col", "row"),
            P("col"),
            P("row", "col"),
            P("col"),
            P("col", "row"),
            P("col"),
        ),
        check_vma=False,
    )
```

```python
import functools

import jax
import jax.numpy as jnp
from jax import lax
from jax.experimental import pallas as pl
from jax.experimental.pallas import tpu as pltpu
from jax.sharding import PartitionSpec as P

D = 1152
HEADS = 16
HD = 72

NORM_EPS = 1e-06
MASK_FILL = -1e30
BF = jnp.bfloat16
F32 = jnp.float32
LOG_SCALE = HD ** -0.5 * 1.4426950408889634


def dot_nn(a, b):
    return lax.dot_general(a, b, (((1,), (0,)), ((), ())), preferred_element_type=F32)


def dot_tn(a, b):
    return lax.dot_general(a, b, (((0,), (0,)), ((), ())), preferred_element_type=F32)


def dot_nt(a, b):
    return lax.dot_general(a, b, (((1,), (1,)), ((), ())), preferred_element_type=F32)


def after(value, *deps):
    return lax.optimization_barrier((value,) + deps)[0]


def row_swap(value, rows, bit):
    return lax.ppermute(value, "row", [(i, i ^ bit) for i in range(rows)])


def col_swap(value, cols, mask):
    return lax.ppermute(value, "col", [(i, i ^ mask) for i in range(cols)])


def layer_norm(resid):
    mean = jnp.mean(resid, axis=0, keepdims=True)
    centered = resid - mean
    var = jnp.mean(centered * centered, axis=0, keepdims=True)
    inv = lax.rsqrt(var + NORM_EPS)
    return centered * inv, inv


def norm_backward(grad, normed, inv, scale):
    dn = grad * (1.0 + scale)
    first = jnp.mean(dn, axis=0, keepdims=True)
    second = jnp.mean(dn * normed, axis=0, keepdims=True)
    back = (dn - first - normed * second) * inv
    return back, jnp.sum(grad, axis=1), jnp.sum(grad * normed, axis=1)


def dot_at(a, b, a_dim, b_dim):
    return lax.dot_general(a, b, (((a_dim,), (b_dim,)), ((), ())), preferred_element_type=F32)


def masked_scores(scores, len_ref):
    if len_ref is None:
        return scores
    return jnp.where(lax.broadcasted_iota(jnp.int32, scores.shape, 1) < len_ref[0], scores, MASK_FILL)


def join(refs, rows):
    return jnp.concatenate([ref[rows, :] for ref in refs], axis=1)


def put(refs, rows, value):
    start = 0
    for ref in refs:
        end = start + ref.shape[1]
        ref[rows, :] = value[:, start:end].astype(ref.dtype)
        start = end


def head_rows(h, first):
    return slice(first + HD * h, first + HD * h + HD)


def forward_kernel(n_q, n_kv, has_len, *refs):
    len_ref = refs[0] if has_len else None
    refs = refs[1:] if has_len else refs
    q_refs, kv_refs, out_refs, lse_ref = refs[:n_q], refs[n_q : n_q + n_kv], refs[n_q + n_kv : -1], refs[-1]
    feat = q_refs[0].shape[0]
    for h in range(feat // HD):
        head, value_rows = head_rows(h, 0), head_rows(h, feat)
        q, k, v = join(q_refs, head), join(kv_refs, head), join(kv_refs, value_rows)
        scores = masked_scores(dot_at(q, k, 0, 0), len_ref)
        top = jnp.max(scores, axis=1, keepdims=True)
        probs = jnp.exp2((scores - top) * LOG_SCALE)
        total = jnp.sum(probs, axis=1, keepdims=True)
        out = dot_at(probs.astype(BF), v, 1, 1) / total
        put(out_refs, head, out.T)
        lse_ref[0, :, h : h + 1] = top * LOG_SCALE + jnp.log2(total)


def backward_kernel(n_q, n_kv, has_len, *refs):
    len_ref = refs[0] if has_len else None
    refs = refs[1:] if has_len else refs
    q_refs, kv_refs, lse_ref = refs[:n_q], refs[n_q : n_q + n_kv], refs[n_q + n_kv]
    refs = refs[n_q + n_kv + 1 :]
    do_refs, dq_refs, dkv_refs = refs[:n_q], refs[n_q : 2 * n_q], refs[2 * n_q :]
    feat = q_refs[0].shape[0]
    for h in range(feat // HD):
        head, value_rows = head_rows(h, 0), head_rows(h, feat)
        q, k, v, do = join(q_refs, head), join(kv_refs, head), join(kv_refs, value_rows), join(do_refs, head)
        scores = masked_scores(dot_at(q, k, 0, 0), len_ref)
        probs = jnp.exp2(scores * LOG_SCALE - lse_ref[0, :, h : h + 1])
        put(dkv_refs, value_rows, dot_at(do, probs.astype(BF), 1, 0))
        dp = dot_at(do, v, 0, 0)
        ds = probs * (dp - jnp.sum(dp * probs, axis=1, keepdims=True)) * HD ** -0.5
        ds = ds.astype(BF)
        put(dq_refs, head, dot_at(ds, k, 1, 1).T)
        put(dkv_refs, head, dot_at(q, ds, 1, 0))


def part_spec(shape, steps):
    if len(shape) == 3:
        return pl.BlockSpec((1,) + tuple(shape[1:]), lambda z: (z, 0, 0))
    return pl.BlockSpec((shape[0] // steps, shape[1]), lambda z: (z, 0))


def whole_spec(shape):
    return pl.BlockSpec(tuple(shape), lambda z: (0,) * len(shape))


def call_parts(kernel, steps, args, arg_specs, outs, out_specs, scratch=()):
    return pl.pallas_call(
        kernel,
        grid=(steps,),
        in_specs=arg_specs,
        out_specs=out_specs,
        out_shape=outs,
        scratch_shapes=list(scratch),
        compiler_params=pltpu.CompilerParams(vmem_limit_bytes=50 * 2**20),
    )(*args)


def attend_forward(q_parts, kv_parts, length, half):
    rows, tokens = q_parts[0].shape[0], sum(q.shape[1] for q in q_parts)
    outs = [jax.ShapeDtypeStruct(q.shape, BF) for q in q_parts]
    outs.append(jax.ShapeDtypeStruct((half, tokens, rows // half // HD), F32))
    args = list(q_parts) + list(kv_parts)
    specs = [part_spec(a.shape, half) for a in args]
    if length is not None:
        args, specs = [length] + args, [pl.BlockSpec(memory_space=pltpu.SMEM)] + specs
    kernel = functools.partial(forward_kernel, len(q_parts), len(kv_parts), length is not None)
    res = call_parts(kernel, half, args, specs, outs, [part_spec(o.shape, half) for o in outs])
    return res[:-1], res[-1]


def attend_backward(q_parts, kv_parts, length, lse, do_parts, half):
    outs = [jax.ShapeDtypeStruct(a.shape, BF) for a in list(q_parts) + list(kv_parts)]
    args = list(q_parts) + list(kv_parts) + [lse] + list(do_parts)
    specs = [part_spec(a.shape, half) for a in args]
    if length is not None:
        args, specs = [length] + args, [pl.BlockSpec(memory_space=pltpu.SMEM)] + specs
    kernel = functools.partial(backward_kernel, len(q_parts), len(kv_parts), length is not None)
    res = call_parts(kernel, half, args, specs, outs, [part_spec(o.shape, half) for o in outs])
    return res[: len(q_parts)], res[len(q_parts) :]


class View:
    def __init__(self, weight, block, indices, start, size):
        self.weight, self.block, self.indices, self.start, self.size = weight, block, indices, start, size

    def args(self):
        return [self.weight] * len(self.indices)

    def specs(self):
        return [pl.BlockSpec((1, D, self.block), lambda z, i=i: (z, 0, i)) for i in self.indices]

    def load(self, refs):
        if len(refs) == 1:
            return refs[0][0, :, self.start : self.start + self.size]
        value = jnp.concatenate([ref[0] for ref in refs], axis=1)
        return value[:, self.start : self.start + self.size]


def view_of(weight, start, size):
    lanes = weight.shape[2]
    best = None
    for block in range(128, lanes, 128):
        first, last = start // block, (start + size - 1) // block
        if (last + 1) * block > lanes and block * (last + 1) - lanes >= 128:
            continue
        cost = (block * (last - first + 1), last - first)
        if last - first < 2 and (best is None or cost < best[0]):
            best = (cost, block, list(range(first, last + 1)), start - first * block)
    if best is None:
        return View(weight, lanes, [0], start, size)
    return View(weight, best[1], best[2], best[3], size)


def store_rows(value, refs):
    first = 0
    for ref in refs:
        ref[...] = value[first : first + ref.shape[0]].astype(ref.dtype)
        first += ref.shape[0]


def in_kernel(view, n_x, *refs):
    n = len(view.indices)
    w, x_refs, bias_ref, out_refs = view.load(refs[:n]), refs[n : n + n_x], refs[n + n_x], refs[n + n_x + 1 :]
    store_rows(dot_tn(w, x_refs[0][...]) + bias_ref[...], out_refs)


def gelu_kernel(view, n_x, *refs):
    n = len(view.indices)
    w, x_refs, bias_ref, out_refs = view.load(refs[:n]), refs[n : n + n_x], refs[n + n_x], refs[n + n_x + 1 :]
    x = jnp.concatenate([ref[...] for ref in x_refs], axis=1)
    v = dot_tn(w, x) + bias_ref[...]
    square = v * v
    t = jnp.tanh(0.7978845608 * (v + 0.044715 * square * v))
    hidden = 0.5 * v * (1.0 + t)
    slope = 0.5 * (1.0 + t) + 0.5 * v * (1.0 - t * t) * 0.7978845608 * (1.0 + 3.0 * 0.044715 * square)
    put(out_refs[:n_x], slice(None), hidden)
    out_refs[n_x][...] = slope


def slope_kernel(view, n_x, *refs):
    n = len(view.indices)
    w, x_refs, slope_ref, out_refs = view.load(refs[:n]), refs[n : n + n_x], refs[n + n_x], refs[n + n_x + 1 :]
    x = jnp.concatenate([ref[...] for ref in x_refs], axis=1)
    grad = (dot_tn(w, x) * slope_ref[...]).astype(BF)
    put(out_refs[:n_x], slice(None), grad)
    out_refs[n_x][...] = jnp.sum(grad.astype(F32), axis=1, keepdims=True)


def apply_in(kernel, view, values, extra, outs):
    half = view.weight.shape[0]
    args = view.args() + list(values) + [extra]
    specs = view.specs() + [whole_spec(v.shape) for v in values] + [part_spec(extra.shape, half)]
    outs = [jax.ShapeDtypeStruct((rows, cols), dtype) for rows, cols, dtype in outs]
    kernel = functools.partial(kernel, view, len(values))
    return call_parts(kernel, half, args, specs, outs, [part_spec(o.shape, half) for o in outs])


def out_kernel(view, *refs):
    n = len(view.indices)
    w, v_refs, out_ref, acc_ref = view.load(refs[:n]), refs[n:-2], refs[-2], refs[-1]
    z = pl.program_id(0)
    total, start = None, 0
    for v_ref in v_refs:
        end = start + v_ref.shape[0]
        part = dot_nn(w[:, start:end], v_ref[...])
        total = part if total is None else total + part
        start = end

    @pl.when(z == 0)
    def _():
        acc_ref[...] = total

    @pl.when(z > 0)
    def _():
        acc_ref[...] += total

    @pl.when(z == pl.num_programs(0) - 1)
    def _():
        out_ref[...] = acc_ref[...].astype(out_ref.dtype)


def apply_out(view, values, dtype):
    half = view.weight.shape[0]
    tokens = values[0].shape[1]
    out = jax.ShapeDtypeStruct((D, tokens), dtype)
    return call_parts(
        functools.partial(out_kernel, view),
        half,
        view.args() + list(values),
        view.specs() + [part_spec(v.shape, half) for v in values],
        out,
        whole_spec(out.shape),
        [pltpu.VMEM((D, tokens), F32)],
    )


def pack_kernel(*refs):
    out_ref, start = refs[-1], 0
    for ref in refs[:-1]:
        end = start + ref.shape[0]
        out_ref[:, start:end] = ref[...].T
        start = end


def unpack_kernel(in_ref, *out_refs):
    start = 0
    for ref in out_refs:
        end = start + ref.shape[0]
        ref[...] = in_ref[:, start:end].astype(F32).T
        start = end


def pack(parts):
    out = jax.ShapeDtypeStruct((parts[0].shape[1], sum(p.shape[0] for p in parts)), BF)
    specs = [whole_spec(p.shape) for p in parts]
    return call_parts(pack_kernel, 1, parts, specs, out, whole_spec(out.shape))


def unpack(value, sizes):
    outs = [jax.ShapeDtypeStruct((n, value.shape[0]), F32) for n in sizes]
    return call_parts(unpack_kernel, 1, [value], [whole_spec(value.shape)], outs, [whole_spec(o.shape) for o in outs])


def outer_kernel(terms, *refs):
    out_ref = refs[-1]
    rows, chunk = out_ref.shape[0], out_ref.shape[1]
    for r in range(rows):
        block = slice(r * chunk, r * chunk + chunk)
        start, at = 0, 0
        for count in terms:
            total = None
            for i in range(count):
                part = dot_nt(refs[at + i][block, :], refs[at + count + i][...])
                total = part if total is None else total + part
            end = start + refs[at + count].shape[0]
            out_ref[r, :, start:end] = total.astype(BF)
            start, at = end, at + 2 * count


def outer_blocks(pairs, rows, half):
    chunk = D // rows
    sizes = [b[0].shape[0] // half for _, b in pairs]
    specs, args = [], []
    for a, b in pairs:
        specs += [whole_spec(p.shape) for p in a] + [part_spec(p.shape, half) for p in b]
        args += list(a) + list(b)
    out = jax.ShapeDtypeStruct((half * rows, chunk, sum(sizes)), BF)
    out_spec = pl.BlockSpec((rows, chunk, sum(sizes)), lambda z: (z, 0, 0))
    kernel = functools.partial(outer_kernel, [len(a) for a, _ in pairs])
    return call_parts(kernel, half, args, specs, out, out_spec)


def tree_kernel(terms, order_ref, *refs):
    out_ref, start, at = refs[-1], 0, 0
    for count in terms:
        total = None
        for i in range(count):
            part = dot_nt(refs[at + i][...], refs[at + count + i][...])
            total = part if total is None else total + part
        end = start + refs[at + count].shape[0]
        out_ref[0, 0, :, start:end] = total.astype(BF)
        start, at = end, at + 2 * count


def tree_blocks(pairs, rows, half, row_order, col_order):
    chunk = D // rows
    sizes = [b[0].shape[0] // half for _, b in pairs]
    specs, args = [], []
    for (a, b), n in zip(pairs, sizes):
        specs += [pl.BlockSpec((chunk, p.shape[1]), lambda i, e, order: (order[i], 0)) for p in a]
        specs += [pl.BlockSpec((n, p.shape[1]), lambda i, e, order: (order[rows + e], 0)) for p in b]
        args += list(a) + list(b)
    return pl.pallas_call(
        functools.partial(tree_kernel, [len(a) for a, _ in pairs]),
        grid_spec=pltpu.PrefetchScalarGridSpec(
            num_scalar_prefetch=1,
            grid=(rows, half),
            in_specs=specs,
            out_specs=pl.BlockSpec((1, 1, chunk, sum(sizes)), lambda i, e, order: (i, e, 0, 0)),
        ),
        out_shape=jax.ShapeDtypeStruct((rows, half, chunk, sum(sizes)), BF),
        compiler_params=pltpu.CompilerParams(vmem_limit_bytes=50 * 2**20),
    )(jnp.stack(row_order + col_order), *args)


def shards(
    block_input,
    text_tokens,
    text_length,
    time_index,
    shift_table,
    time_table,
    query_weight,
    key_weight,
    value_weight,
    query_bias,
    value_bias,
    out_weight,
    out_bias,
    cross_query,
    cross_key,
    cross_value,
    cross_query_bias,
    cross_value_bias,
    cross_out,
    cross_out_bias,
    up_weight,
    up_bias,
    down_weight,
    down_bias,
    out_grad,
):
    rows, cols = lax.axis_size("row"), lax.axis_size("col")
    r, c = lax.axis_index("row"), lax.axis_index("col")
    half = cols // 2
    feat = block_input.shape[1]
    width = 2 * block_input.shape[2] // cols
    texts = text_tokens.shape[1]
    steps = time_table.shape[2]
    ups = up_bias.shape[0]
    core, low_z, micro = r & 1, (c >> 1) & 1, c // half
    at_home = core == low_z

    kv_masks = [1 << b for b in range(2, cols.bit_length() - 2)]
    def home_of(i, j):
        return (i & ~1) | ((j >> 1) & 1), (j & ~2) | ((i & 1) << 1)

    home_r, home_c = home_of(r, c)

    def place_swap(value):
        pairs = []
        for i in range(rows):
            for j in range(cols):
                to_r, to_c = home_of(i, j)
                pairs.append((i * cols + j, to_r * cols + to_c))
        return lax.ppermute(value, ("row", "col"), pairs)

    def send_tokens(blocks):
        full = jnp.zeros_like(blocks)
        for e in range(cols):
            pairs = []
            for i in range(rows):
                for j in range(cols):
                    to_r, to_c = home_of(i, j ^ e)
                    pairs.append((i * cols + j, to_r * cols + to_c))
            part = lax.dynamic_slice_in_dim(blocks, c ^ e, 1, 0)
            part = lax.ppermute(part, ("row", "col"), pairs)
            full = lax.dynamic_update_slice_in_dim(full, part, home_c ^ e, 0)
        return full.reshape(D, blocks.shape[2])

    def token_blocks(value):
        return value.reshape(2, feat, half, width).transpose(0, 2, 1, 3).reshape(cols, feat, width)

    def tokens_out(value):
        blocks = place_swap(value).reshape(cols, feat, width)
        blocks = lax.all_to_all(blocks, "col", 0, 0, tiled=True)
        blocks = blocks.reshape(2, half, feat, width).transpose(0, 2, 1, 3)
        return blocks.reshape(2, feat, half * width).astype(F32)

    def gather_pair(value):
        return [value, col_swap(value, cols, 1)]

    def reduce_pair(view, *values, cover=None):
        other = apply_out(view, [v[1] for v in values], BF)
        received = col_swap(other, cols, 1)
        own = [v[0] for v in values]
        covered = None
        if cover is not None:
            covered = cover(other)
            own[0] = after(own[0], covered)
        return apply_out(view, own, F32) + received.astype(F32), covered

    def gather_keys(parts):
        parts = list(parts) + [row_swap(p, rows, 1) for p in parts]
        for mask in kv_masks:
            parts = parts + [col_swap(p, cols, mask) for p in parts]
        return parts

    def add_swapped(parts, swap):
        h = len(parts) // 2
        return [(a.astype(F32) + swap(b).astype(F32)).astype(BF) for a, b in zip(parts[:h], parts[h:])]

    def reduce_keys(parts):
        for mask in reversed(kv_masks):
            parts = add_swapped(parts, lambda p, mask=mask: col_swap(p, cols, mask))
        return add_swapped(parts, lambda p: row_swap(p, rows, 1))

    groups = [[i * cols + 2 * z + y for z in range(half) for i in range(rows)] for y in range(2)]

    def gather_weights(flat):
        full = lax.all_gather(flat, ("row", "col"), axis=0, tiled=True, axis_index_groups=groups)
        return full.reshape(half, D, flat.shape[1])

    def scatter(blocks):
        flat = blocks.reshape(half * D, blocks.shape[2])
        return lax.psum_scatter(flat, ("row", "col"), scatter_dimension=0, tiled=True, axis_index_groups=groups)

    row_bits = rows.bit_length() - 1
    order = [0]
    for b in range(row_bits):
        order = [i for j in order for i in (j, j | (1 << (row_bits - 1 - b)))]
    order = sorted(order, key=lambda i: int(format(i, f"0{row_bits}b")[::-1], 2))

    def tree_outer(pairs):
        return tree_blocks(pairs, rows, half, [r ^ i for i in order], [(c >> 1) ^ e for e in range(half)])

    def tree_reduce(blocks):
        for b in range(row_bits):
            h = blocks.shape[0] // 2
            received = row_swap(blocks[h:], rows, 1 << b)
            blocks = (blocks[:h].astype(F32) + received.astype(F32)).astype(BF)
        total = blocks[0, 0].astype(F32)
        for e in range(1, half):
            total = total + col_swap(blocks[0, e], cols, e << 1).astype(F32)
        return total

    first_w = gather_weights(
        pack([query_weight.T, key_weight.T, value_weight.T, out_weight, cross_query.T, cross_key.T, cross_value.T, cross_out])
    )
    second_w = gather_weights(jnp.concatenate([up_weight, down_weight.T], axis=1))

    step_ids = jnp.arange(steps, dtype=jnp.int32)
    onehot = (time_index[:, 0][:, None] == step_ids[None, :]).astype(F32)
    modulation = lax.dot_general(
        onehot,
        time_table.reshape(6 * feat, steps),
        (((1,), (1,)), ((), ())),
        precision=lax.Precision.HIGHEST,
        preferred_element_type=F32,
    ).reshape(2, 6, feat) + shift_table[None]
    same = [
        jnp.broadcast_to(b.reshape(1, -1, feat), (2, b.shape[0] // feat, feat))
        for b in (out_bias, cross_out_bias, down_bias, query_bias, value_bias, cross_query_bias, cross_value_bias, up_bias)
    ]
    lengths = jnp.broadcast_to(text_length.astype(F32)[:, :, None], (2, 1, feat))
    small = jnp.concatenate([modulation, lengths] + same, axis=1).transpose(0, 2, 1)
    small_high = lax.reduce_precision(small, 8, 7)
    small_rest = small - small_high
    small_mid = lax.reduce_precision(small_rest, 8, 7)
    small_low = small_rest - small_mid
    extra = jnp.concatenate(
        [text_tokens.transpose(0, 2, 1)] + [p.astype(BF) for p in (small_high, small_mid, small_low)], axis=2
    )
    arrived = send_tokens(
        jnp.concatenate([token_blocks(block_input), token_blocks(out_grad), jnp.repeat(extra, half, axis=0)], axis=2)
    )
    small_n, head = small.shape[2], 2 * width

    def small_of(value):
        parts = [value[:, head + texts + i * small_n : head + texts + (i + 1) * small_n].astype(F32) for i in range(3)]
        return parts[0] + parts[1] + parts[2]

    model_rows = small_of(arrived)
    shift_a, scale_a, gate_a, shift_m, scale_m, gate_m, length_row, out_b, cout_b, down_b = (
        model_rows[:, i : i + 1] for i in range(10)
    )
    length = length_row[0].astype(jnp.int32)
    col_rows = small_of(arrived).reshape(cols, feat, small_n)
    col_rows = jnp.concatenate(
        [
            lax.dynamic_index_in_dim(col_rows, 2 * e + (c & 1), 0, keepdims=False)[:, 10:].T.reshape(-1, 1, feat)
            for e in range(half)
        ],
        axis=1,
    )
    q_b, v_b, cq_b, cv_b = (col_rows[i].reshape(half * feat, 1) for i in range(4))
    up_b = col_rows[4:].transpose(1, 0, 2).reshape(half * ups, 1)
    text_t = arrived[:, head : head + texts]

    resid = arrived[:, :width].astype(F32)
    cot = arrived[:, width:head].astype(F32)
    heads_w, hidden_w = half * feat, half * ups
    qkv_w, out_w, cq_w, ckv_w, cout_w = (
        view_of(first_w, i * feat, (j - i) * feat) for i, j in ((0, 3), (3, 4), (4, 5), (5, 7), (7, 8))
    )
    up_w, down_w = view_of(second_w, 0, ups), view_of(second_w, ups, ups)

    def columns(*parts):
        return jnp.stack([p.reshape(half, feat) for p in parts], axis=1).reshape(-1, 1)

    def heads_in(weight, value, *biases):
        sizes = [1] if len(biases) == 1 else [1, len(biases) - 1]
        outs = [(n * heads_w, value.shape[1], BF) for n in sizes]
        return apply_in(in_kernel, weight, [value], columns(*biases), outs)

    none = jnp.zeros((heads_w,), F32)
    normed_a, inv_a = layer_norm(resid)
    attn_full = gather_pair((normed_a * (1.0 + scale_a) + shift_a).astype(BF))
    q_parts, kv_parts = zip(*(heads_in(qkv_w, p, q_b, none, v_b) for p in attn_full))
    kv_all = gather_keys(kv_parts)
    att, lse = attend_forward(q_parts, kv_all, None, half)
    branch_a = reduce_pair(out_w, att)[0] + out_b
    after_attn = resid + gate_a * branch_a
    cross_full = gather_pair(after_attn.astype(BF))
    cq_parts = [heads_in(cq_w, p, cq_b)[0] for p in cross_full]
    ckv = apply_in(in_kernel, ckv_w, [text_t], columns(none, cv_b), [(2 * heads_w, texts, BF)])
    catt, clse = attend_forward(cq_parts, ckv, length, half)
    after_cross = after_attn + reduce_pair(cout_w, catt)[0] + cout_b
    normed_m, inv_m = layer_norm(after_cross)
    mlp_full = gather_pair((normed_m * (1.0 + scale_m) + shift_m).astype(BF))
    hidden_outs = [(hidden_w, width, BF)] * 2
    *hidden, slope = apply_in(gelu_kernel, up_w, mlp_full, up_b, hidden_outs + [(hidden_w, 2 * width, F32)])
    branch_m = reduce_pair(down_w, hidden)[0] + down_b
    block_out = (after_cross + gate_m * branch_m).astype(BF)

    grad_mlp = gate_m * cot
    low_full = gather_pair(grad_mlp.astype(BF))
    g_down_b = jnp.sum(grad_mlp, axis=1)
    g_gate_m = jnp.sum(cot * branch_m, axis=1)
    *grad_pre, g_up_b = apply_in(slope_kernel, down_w, low_full, slope, hidden_outs + [(hidden_w, 1, F32)])

    def mlp_cover(other):
        return outer_blocks([(mlp_full, grad_pre), (low_full, [after(hidden[0], other), hidden[1]])], rows, half)

    back_in, mlp_blocks = reduce_pair(up_w, grad_pre, cover=mlp_cover)
    mlp_grads = scatter(mlp_blocks)
    back_m, g_shift_m, g_scale_m = norm_backward(back_in, normed_m, inv_m, scale_m)
    grad_cross = cot + back_m
    g_cout_b = jnp.sum(grad_cross, axis=1)
    low_cross = gather_pair(grad_cross.astype(BF))
    dcatt = [heads_in(cout_w, p, none)[0] for p in low_cross]
    dcq, dckv = attend_backward(cq_parts, ckv, length, clse, dcatt, half)

    def cross_cover(other):
        pairs = [(cross_full, dcq), ([text_t], dckv), (low_cross, [after(catt[0], other), catt[1]])]
        return outer_blocks(pairs, rows, half)

    back_cross, cross_blocks = reduce_pair(cq_w, dcq, cover=cross_cover)
    grad_res = grad_cross + back_cross
    g_cq_b = jnp.sum(sum(p.astype(F32) for p in dcq), axis=1)
    g_cv_b = jnp.sum(dckv[0].astype(F32).reshape(half, 2, feat, texts)[:, 1], axis=2)
    g_gate_a = jnp.sum(grad_res * branch_a, axis=1)
    grad_attn = gate_a * grad_res
    g_out_b = jnp.sum(grad_attn, axis=1)
    low_attn = gather_pair(grad_attn.astype(BF))
    datt = [heads_in(out_w, p, none)[0] for p in low_attn]
    dq, dkv = attend_backward(q_parts, kv_all, None, lse, datt, half)
    dkv = reduce_keys(dkv)

    def attention_cover(other):
        return tree_outer([(attn_full, [after(dq[0], other), dq[1]]), (attn_full, dkv), (low_attn, att)])

    back_att, att_blocks = reduce_pair(qkv_w, dq, dkv, cover=attention_cover)
    cross_grads = scatter(after(cross_blocks, mlp_grads, dq[0]))
    att_grads = tree_reduce(att_blocks)
    g_cq, g_ck, g_cv, g_cout = unpack(cross_grads, [feat] * 4)
    g_q, g_k, g_v, g_out = unpack(att_grads, [feat] * 4)
    g_up, g_down = mlp_grads[:, :ups].astype(F32), mlp_grads[:, ups:].astype(F32)
    g_q_b = jnp.sum(sum(p.astype(F32) for p in dq), axis=1)
    g_v_b = jnp.sum(sum(p.astype(F32) for p in dkv).reshape(half, 2, feat, width)[:, 1], axis=2)
    back_a, g_shift_a, g_scale_a = norm_backward(back_att, normed_a, inv_a, scale_a)
    block_output = tokens_out(after(block_out, back_att))
    grad_input = tokens_out((grad_res + back_a).astype(BF))
    grad_text = apply_out(ckv_w, dckv, BF)
    grad_text = grad_text.astype(F32) + row_swap(grad_text, rows, 1).astype(F32)
    grad_text = jnp.where(at_home, grad_text, 0.0).astype(BF).reshape(cols, feat, texts)
    grad_text = lax.all_to_all(grad_text, "col", 0, 0, tiled=True)
    grad_text = jnp.sum(grad_text.reshape(2, half, feat, texts).astype(F32), axis=1).transpose(0, 2, 1)

    model_g = jnp.stack(
        [g_shift_a, g_scale_a, g_gate_a, g_shift_m, g_scale_m, g_gate_m, g_out_b, g_cout_b, g_down_b], axis=1
    )
    model_g = model_g.T.reshape(9, cols, feat).transpose(1, 0, 2)
    per_col = ups // feat
    col_g = jnp.concatenate(
        [g.reshape(half, 1, feat) for g in (g_q_b, g_v_b, g_cq_b, g_cv_b)] + [g_up_b.reshape(half, per_col, feat)],
        axis=1,
    )
    side = c & 1
    blocks = []
    for j in range(cols):
        blocks.append(jnp.where(side == (j & 1), col_g[j >> 1], 0.0))
    small_g = jnp.concatenate([model_g, jnp.stack(blocks)], axis=1)
    small_g = lax.all_to_all(small_g, "col", 0, 0, tiled=True)
    mod_g = small_g[:, :6].reshape(2, cols // 8, 2, 2, 6, feat).sum(axis=(1, 3))
    bias_g = small_g[:, 6:].sum(axis=0)
    step_rows = jnp.broadcast_to(time_index.astype(F32), (2, feat))
    small_g = lax.all_gather(jnp.concatenate([mod_g.reshape(24, feat), bias_g, step_rows], axis=0), "row")
    step_all = small_g[:, -2:, 0].T.reshape(2 * rows).astype(jnp.int32)
    mod_g = small_g[:, :24].reshape(rows // 2, 2, 2, 2, 6, feat).sum(axis=1)
    mod_g = mod_g.transpose(1, 0, 2, 3, 4).reshape(2 * rows, 6, feat)
    bias_g = small_g[:, 24:-2].sum(axis=0)
    g_shift = mod_g.sum(axis=0)
    onehot_all = (step_all[:, None] == step_ids[None, :]).astype(F32)
    g_time = lax.dot_general(
        mod_g.reshape(2 * rows, 6 * feat),
        onehot_all,
        (((0,), (0,)), ((), ())),
        precision=lax.Precision.HIGHEST,
        preferred_element_type=F32,
    ).reshape(6, feat, steps)
    g_out_b, g_cout_b, g_down_b, g_q_b, g_v_b, g_cq_b, g_cv_b = (bias_g[i] for i in range(7))
    g_up_b = bias_g[7:].reshape(ups)
    return (
        block_output,
        grad_input,
        grad_text,
        g_shift,
        g_time,
        g_q.T,
        g_k.T,
        g_v.T,
        g_q_b,
        g_v_b,
        g_out,
        g_out_b,
        g_cq.T,
        g_ck.T,
        g_cv.T,
        g_cq_b,
        g_cv_b,
        g_cout,
        g_cout_b,
        g_up,
        g_up_b,
        g_down.T,
        g_down_b,
    )


def solution(mesh):
    return jax.shard_map(
        shards,
        mesh=mesh,
        in_specs=(
            P(None, "col", "row"),
            P(None, "row", "col"),
            P(None, "row"),
            P(None, "row"),
            P(None, "col"),
            P(None, "col", None),
            P("row", "col"),
            P("row", "col"),
            P("row", "col"),
            P("col"),
            P("col"),
            P("col", "row"),
            P("col"),
            P("row", "col"),
            P("row", "col"),
            P("row", "col"),
            P("col"),
            P("col"),
            P("col", "row"),
            P("col"),
            P("row", "col"),
            P("col"),
            P("col", "row"),
            P("col"),
            P(None, "col", "row"),
        ),
        out_specs=(
            P(None, "col", "row"),
            P(None, "col", "row"),
            P(None, "row", "col"),
            P(None, "col"),
            P(None, "col", None),
            P("row", "col"),
            P("row", "col"),
            P("row", "col"),
            P("col"),
            P("col"),
            P("col", "row"),
            P("col"),
            P("row", "col"),
            P("row", "col"),
            P("row", "col"),
            P("col"),
            P("col"),
            P("col", "row"),
            P("col"),
            P("row", "col"),
            P("col"),
            P("col", "row"),
            P("col"),
        ),
        check_vma=False,
    )
```

```python
import functools

import jax
import jax.numpy as jnp
from jax import lax
from jax.experimental import pallas as pl
from jax.experimental.pallas import tpu as pltpu
from jax.sharding import PartitionSpec as P

D = 1152
HEADS = 16
HD = 72

NORM_EPS = 1e-06
MASK_FILL = -1e30
COST_SCALE = 3
BF = jnp.bfloat16
F32 = jnp.float32
LOG_SCALE = HD ** -0.5 * 1.4426950408889634


def dot_nn(a, b):
    return lax.dot_general(a, b, (((1,), (0,)), ((), ())), preferred_element_type=F32)


def dot_tn(a, b):
    return lax.dot_general(a, b, (((0,), (0,)), ((), ())), preferred_element_type=F32)


def dot_nt(a, b):
    return lax.dot_general(a, b, (((1,), (1,)), ((), ())), preferred_element_type=F32)


def after(value, *deps):
    return lax.optimization_barrier((value,) + deps)[0]


def row_swap(value, rows, bit):
    return lax.ppermute(value, "row", [(i, i ^ bit) for i in range(rows)])


def col_swap(value, cols, mask):
    return lax.ppermute(value, "col", [(i, i ^ mask) for i in range(cols)])


def layer_norm(resid):
    mean = jnp.mean(resid, axis=0, keepdims=True)
    centered = resid - mean
    var = jnp.mean(centered * centered, axis=0, keepdims=True)
    inv = lax.rsqrt(var + NORM_EPS)
    return centered * inv, inv


def norm_backward(grad, normed, inv, scale):
    dn = grad * (1.0 + scale)
    first = jnp.mean(dn, axis=0, keepdims=True)
    second = jnp.mean(dn * normed, axis=0, keepdims=True)
    back = (dn - first - normed * second) * inv
    return back, jnp.sum(grad, axis=1), jnp.sum(grad * normed, axis=1)


def dot_at(a, b, a_dim, b_dim):
    return lax.dot_general(a, b, (((a_dim,), (b_dim,)), ((), ())), preferred_element_type=F32)


def masked_scores(scores, len_ref):
    if len_ref is None:
        return scores
    return jnp.where(lax.broadcasted_iota(jnp.int32, scores.shape, 1) < len_ref[0], scores, MASK_FILL)


def join(refs, rows):
    return jnp.concatenate([ref[rows, :] for ref in refs], axis=1)


def put(refs, rows, value):
    start = 0
    for ref in refs:
        end = start + ref.shape[1]
        ref[rows, :] = value[:, start:end].astype(ref.dtype)
        start = end


def head_rows(h, first):
    return slice(first + HD * h, first + HD * h + HD)


def forward_kernel(n_q, n_kv, has_len, *refs):
    len_ref = refs[0] if has_len else None
    refs = refs[1:] if has_len else refs
    q_refs, kv_refs, out_refs, lse_ref = refs[:n_q], refs[n_q : n_q + n_kv], refs[n_q + n_kv : -1], refs[-1]
    feat = q_refs[0].shape[0]
    for h in range(feat // HD):
        head, value_rows = head_rows(h, 0), head_rows(h, feat)
        q, k, v = join(q_refs, head), join(kv_refs, head), join(kv_refs, value_rows)
        scores = masked_scores(dot_at(q, k, 0, 0), len_ref)
        top = jnp.max(scores, axis=1, keepdims=True)
        probs = jnp.exp2((scores - top) * LOG_SCALE)
        total = jnp.sum(probs, axis=1, keepdims=True)
        out = dot_at(probs.astype(BF), v, 1, 1) / total
        put(out_refs, head, out.T)
        lse_ref[0, :, h : h + 1] = top * LOG_SCALE + jnp.log2(total)


def backward_kernel(n_q, n_kv, has_len, *refs):
    len_ref = refs[0] if has_len else None
    refs = refs[1:] if has_len else refs
    q_refs, kv_refs, lse_ref = refs[:n_q], refs[n_q : n_q + n_kv], refs[n_q + n_kv]
    refs = refs[n_q + n_kv + 1 :]
    do_refs, dq_refs, dkv_refs = refs[:n_q], refs[n_q : 2 * n_q], refs[2 * n_q :]
    feat = q_refs[0].shape[0]
    for h in range(feat // HD):
        head, value_rows = head_rows(h, 0), head_rows(h, feat)
        q, k, v, do = join(q_refs, head), join(kv_refs, head), join(kv_refs, value_rows), join(do_refs, head)
        scores = masked_scores(dot_at(q, k, 0, 0), len_ref)
        probs = jnp.exp2(scores * LOG_SCALE - lse_ref[0, :, h : h + 1])
        put(dkv_refs, value_rows, dot_at(do, probs.astype(BF), 1, 0))
        dp = dot_at(do, v, 0, 0)
        ds = probs * (dp - jnp.sum(dp * probs, axis=1, keepdims=True)) * HD ** -0.5
        ds = ds.astype(BF)
        put(dq_refs, head, dot_at(ds, k, 1, 1).T)
        put(dkv_refs, head, dot_at(q, ds, 1, 0))


def part_spec(shape, steps):
    if len(shape) == 3:
        return pl.BlockSpec((1,) + tuple(shape[1:]), lambda z: (z, 0, 0))
    return pl.BlockSpec((shape[0] // steps, shape[1]), lambda z: (z, 0))


def whole_spec(shape):
    return pl.BlockSpec(tuple(shape), lambda z: (0,) * len(shape))


def cost_of(args, outs, flops):
    total = sum(a.size * a.dtype.itemsize for a in args)
    for out in jax.tree.leaves(outs):
        size = 1
        for n in out.shape:
            size *= n
        total += size * jnp.dtype(out.dtype).itemsize
    return pl.CostEstimate(flops=int(flops), bytes_accessed=int(total), transcendentals=0)


def call_parts(kernel, steps, args, arg_specs, outs, out_specs, scratch=(), flops=0):
    return pl.pallas_call(
        kernel,
        cost_estimate=cost_of(args, outs, COST_SCALE * flops),
        grid=(steps,),
        in_specs=arg_specs,
        out_specs=out_specs,
        out_shape=outs,
        scratch_shapes=list(scratch),
        compiler_params=pltpu.CompilerParams(vmem_limit_bytes=50 * 2**20),
    )(*args)


def attend_forward(q_parts, kv_parts, length, half):
    rows, tokens = q_parts[0].shape[0], sum(q.shape[1] for q in q_parts)
    outs = [jax.ShapeDtypeStruct(q.shape, BF) for q in q_parts]
    outs.append(jax.ShapeDtypeStruct((half, tokens, rows // half // HD), F32))
    args = list(q_parts) + list(kv_parts)
    specs = [part_spec(a.shape, half) for a in args]
    if length is not None:
        args, specs = [length] + args, [pl.BlockSpec(memory_space=pltpu.SMEM)] + specs
    kernel = functools.partial(forward_kernel, len(q_parts), len(kv_parts), length is not None)
    flops = 4 * sum(q.size for q in q_parts) * sum(k.shape[1] for k in kv_parts)
    res = call_parts(kernel, half, args, specs, outs, [part_spec(o.shape, half) for o in outs], flops=4 * flops)
    return res[:-1], res[-1]


def attend_backward(q_parts, kv_parts, length, lse, do_parts, half):
    outs = [jax.ShapeDtypeStruct(a.shape, BF) for a in list(q_parts) + list(kv_parts)]
    args = list(q_parts) + list(kv_parts) + [lse] + list(do_parts)
    specs = [part_spec(a.shape, half) for a in args]
    if length is not None:
        args, specs = [length] + args, [pl.BlockSpec(memory_space=pltpu.SMEM)] + specs
    kernel = functools.partial(backward_kernel, len(q_parts), len(kv_parts), length is not None)
    flops = 10 * sum(q.size for q in q_parts) * sum(k.shape[1] for k in kv_parts)
    res = call_parts(kernel, half, args, specs, outs, [part_spec(o.shape, half) for o in outs], flops=3 * flops)
    return res[: len(q_parts)], res[len(q_parts) :]


class View:
    def __init__(self, weight, block, indices, start, size):
        self.weight, self.block, self.indices, self.start, self.size = weight, block, indices, start, size

    def args(self):
        return [self.weight] * len(self.indices)

    def specs(self):
        return [pl.BlockSpec((1, D, self.block), lambda z, i=i: (z, 0, i)) for i in self.indices]

    def load(self, refs):
        if len(refs) == 1:
            return refs[0][0, :, self.start : self.start + self.size]
        value = jnp.concatenate([ref[0] for ref in refs], axis=1)
        return value[:, self.start : self.start + self.size]


def view_of(weight, start, size):
    lanes = weight.shape[2]
    best = None
    for block in range(128, lanes, 128):
        first, last = start // block, (start + size - 1) // block
        if (last + 1) * block > lanes and block * (last + 1) - lanes >= 128:
            continue
        cost = (block * (last - first + 1), last - first)
        if last - first < 2 and (best is None or cost < best[0]):
            best = (cost, block, list(range(first, last + 1)), start - first * block)
    if best is None:
        return View(weight, lanes, [0], start, size)
    return View(weight, best[1], best[2], best[3], size)


def store_rows(value, refs):
    first = 0
    for ref in refs:
        ref[...] = value[first : first + ref.shape[0]].astype(ref.dtype)
        first += ref.shape[0]


def in_kernel(view, n_x, *refs):
    n = len(view.indices)
    w, x_refs, bias_ref, out_refs = view.load(refs[:n]), refs[n : n + n_x], refs[n + n_x], refs[n + n_x + 1 :]
    store_rows(dot_tn(w, x_refs[0][...]) + bias_ref[...], out_refs)


def gelu_kernel(view, n_x, *refs):
    n = len(view.indices)
    w, x_refs, bias_ref, out_refs = view.load(refs[:n]), refs[n : n + n_x], refs[n + n_x], refs[n + n_x + 1 :]
    x = jnp.concatenate([ref[...] for ref in x_refs], axis=1)
    v = dot_tn(w, x) + bias_ref[...]
    square = v * v
    t = jnp.tanh(0.7978845608 * (v + 0.044715 * square * v))
    hidden = 0.5 * v * (1.0 + t)
    slope = 0.5 * (1.0 + t) + 0.5 * v * (1.0 - t * t) * 0.7978845608 * (1.0 + 3.0 * 0.044715 * square)
    put(out_refs[:n_x], slice(None), hidden)
    out_refs[n_x][...] = slope


def slope_kernel(view, n_x, *refs):
    n = len(view.indices)
    w, x_refs, slope_ref, out_refs = view.load(refs[:n]), refs[n : n + n_x], refs[n + n_x], refs[n + n_x + 1 :]
    x = jnp.concatenate([ref[...] for ref in x_refs], axis=1)
    grad = (dot_tn(w, x) * slope_ref[...]).astype(BF)
    put(out_refs[:n_x], slice(None), grad)
    out_refs[n_x][...] = jnp.sum(grad.astype(F32), axis=1, keepdims=True)


def apply_in(kernel, view, values, extra, outs):
    half = view.weight.shape[0]
    args = view.args() + list(values) + [extra]
    specs = view.specs() + [whole_spec(v.shape) for v in values] + [part_spec(extra.shape, half)]
    outs = [jax.ShapeDtypeStruct((rows, cols), dtype) for rows, cols, dtype in outs]
    kernel = functools.partial(kernel, view, len(values))
    flops = 2 * half * view.size * sum(v.size for v in values)
    return call_parts(kernel, half, args, specs, outs, [part_spec(o.shape, half) for o in outs], flops=flops)


def out_kernel(view, *refs):
    n = len(view.indices)
    w, v_refs, out_ref, acc_ref = view.load(refs[:n]), refs[n:-2], refs[-2], refs[-1]
    z = pl.program_id(0)
    total, start = None, 0
    for v_ref in v_refs:
        end = start + v_ref.shape[0]
        part = dot_nn(w[:, start:end], v_ref[...])
        total = part if total is None else total + part
        start = end

    @pl.when(z == 0)
    def _():
        acc_ref[...] = total

    @pl.when(z > 0)
    def _():
        acc_ref[...] += total

    @pl.when(z == pl.num_programs(0) - 1)
    def _():
        out_ref[...] = acc_ref[...].astype(out_ref.dtype)


def apply_out(view, values, dtype):
    half = view.weight.shape[0]
    tokens = values[0].shape[1]
    out = jax.ShapeDtypeStruct((D, tokens), dtype)
    return call_parts(
        functools.partial(out_kernel, view),
        half,
        view.args() + list(values),
        view.specs() + [part_spec(v.shape, half) for v in values],
        out,
        whole_spec(out.shape),
        [pltpu.VMEM((D, tokens), F32)],
        flops=2 * D * sum(v.size for v in values),
    )


def pack_kernel(*refs):
    out_ref, start = refs[-1], 0
    for ref in refs[:-1]:
        end = start + ref.shape[0]
        out_ref[:, start:end] = ref[...].T
        start = end


def unpack_kernel(in_ref, *out_refs):
    start = 0
    for ref in out_refs:
        end = start + ref.shape[0]
        ref[...] = in_ref[:, start:end].astype(F32).T
        start = end


def pack(parts):
    out = jax.ShapeDtypeStruct((parts[0].shape[1], sum(p.shape[0] for p in parts)), BF)
    specs = [whole_spec(p.shape) for p in parts]
    return call_parts(pack_kernel, 1, parts, specs, out, whole_spec(out.shape))


def unpack(value, sizes):
    outs = [jax.ShapeDtypeStruct((n, value.shape[0]), F32) for n in sizes]
    return call_parts(unpack_kernel, 1, [value], [whole_spec(value.shape)], outs, [whole_spec(o.shape) for o in outs])


def outer_kernel(terms, *refs):
    out_ref = refs[-1]
    rows, chunk = out_ref.shape[0], out_ref.shape[1]
    for r in range(rows):
        block = slice(r * chunk, r * chunk + chunk)
        start, at = 0, 0
        for count in terms:
            total = None
            for i in range(count):
                part = dot_nt(refs[at + i][block, :], refs[at + count + i][...])
                total = part if total is None else total + part
            end = start + refs[at + count].shape[0]
            out_ref[r, :, start:end] = total.astype(BF)
            start, at = end, at + 2 * count


def outer_blocks(pairs, rows, half):
    chunk = D // rows
    sizes = [b[0].shape[0] // half for _, b in pairs]
    specs, args = [], []
    for a, b in pairs:
        specs += [whole_spec(p.shape) for p in a] + [part_spec(p.shape, half) for p in b]
        args += list(a) + list(b)
    out = jax.ShapeDtypeStruct((half * rows, chunk, sum(sizes)), BF)
    out_spec = pl.BlockSpec((rows, chunk, sum(sizes)), lambda z: (z, 0, 0))
    kernel = functools.partial(outer_kernel, [len(a) for a, _ in pairs])
    flops = sum(2 * p.size * D for _, b in pairs for p in b)
    return call_parts(kernel, half, args, specs, out, out_spec, flops=flops)


def tree_kernel(terms, order_ref, *refs):
    out_ref, start, at = refs[-1], 0, 0
    for count in terms:
        total = None
        for i in range(count):
            part = dot_nt(refs[at + i][...], refs[at + count + i][...])
            total = part if total is None else total + part
        end = start + refs[at + count].shape[0]
        out_ref[0, 0, :, start:end] = total.astype(BF)
        start, at = end, at + 2 * count


def tree_blocks(pairs, chunk, half, row_order, col_order):
    rows = len(row_order)
    sizes = [b[0].shape[0] // half for _, b in pairs]
    specs, args = [], []
    for (a, b), n in zip(pairs, sizes):
        specs += [pl.BlockSpec((chunk, p.shape[1]), lambda i, e, order: (order[i], 0)) for p in a]
        specs += [pl.BlockSpec((n, p.shape[1]), lambda i, e, order: (order[rows + e], 0)) for p in b]
        args += list(a) + list(b)
    return pl.pallas_call(
        functools.partial(tree_kernel, [len(a) for a, _ in pairs]),
        cost_estimate=cost_of(args, [], COST_SCALE * sum(2 * p.size * D for _, b in pairs for p in b) * rows * chunk // D),
        grid_spec=pltpu.PrefetchScalarGridSpec(
            num_scalar_prefetch=1,
            grid=(rows, half),
            in_specs=specs,
            out_specs=pl.BlockSpec((1, 1, chunk, sum(sizes)), lambda i, e, order: (i, e, 0, 0)),
        ),
        out_shape=jax.ShapeDtypeStruct((rows, half, chunk, sum(sizes)), BF),
        compiler_params=pltpu.CompilerParams(vmem_limit_bytes=50 * 2**20),
    )(jnp.stack(row_order + col_order), *args)


def shards(
    block_input,
    text_tokens,
    text_length,
    time_index,
    shift_table,
    time_table,
    query_weight,
    key_weight,
    value_weight,
    query_bias,
    value_bias,
    out_weight,
    out_bias,
    cross_query,
    cross_key,
    cross_value,
    cross_query_bias,
    cross_value_bias,
    cross_out,
    cross_out_bias,
    up_weight,
    up_bias,
    down_weight,
    down_bias,
    out_grad,
):
    rows, cols = lax.axis_size("row"), lax.axis_size("col")
    r, c = lax.axis_index("row"), lax.axis_index("col")
    half = cols // 2
    feat = block_input.shape[1]
    width = 2 * block_input.shape[2] // cols
    texts = text_tokens.shape[1]
    steps = time_table.shape[2]
    ups = up_bias.shape[0]
    core, low_z, micro = r & 1, (c >> 1) & 1, c // half
    at_home = core == low_z

    kv_masks = [1 << b for b in range(2, cols.bit_length() - 2)]
    def home_of(i, j):
        return (i & ~1) | ((j >> 1) & 1), (j & ~2) | ((i & 1) << 1)

    home_r, home_c = home_of(r, c)

    def place_swap(value):
        pairs = []
        for i in range(rows):
            for j in range(cols):
                to_r, to_c = home_of(i, j)
                pairs.append((i * cols + j, to_r * cols + to_c))
        return lax.ppermute(value, ("row", "col"), pairs)

    def send_tokens(blocks):
        full = jnp.zeros_like(blocks)
        for e in range(cols):
            pairs = []
            for i in range(rows):
                for j in range(cols):
                    to_r, to_c = home_of(i, j ^ e)
                    pairs.append((i * cols + j, to_r * cols + to_c))
            part = lax.dynamic_slice_in_dim(blocks, c ^ e, 1, 0)
            part = lax.ppermute(part, ("row", "col"), pairs)
            full = lax.dynamic_update_slice_in_dim(full, part, home_c ^ e, 0)
        return full.reshape(D, blocks.shape[2])

    def token_blocks(value):
        return value.reshape(2, feat, half, width).transpose(0, 2, 1, 3).reshape(cols, feat, width)

    def tokens_out(value):
        blocks = place_swap(value).reshape(cols, feat, width)
        blocks = lax.all_to_all(blocks, "col", 0, 0, tiled=True)
        blocks = blocks.reshape(2, half, feat, width).transpose(0, 2, 1, 3)
        return blocks.reshape(2, feat, half * width).astype(F32)

    def gather_pair(value):
        return [value, col_swap(value, cols, 1)]

    def reduce_pair(view, *values, cover=None):
        other = apply_out(view, [v[1] for v in values], BF)
        received = col_swap(other, cols, 1)
        own = [v[0] for v in values]
        covered = None
        if cover is not None:
            covered = cover(other)
            own[0] = after(own[0], covered)
        return apply_out(view, own, F32) + received.astype(F32), covered

    def gather_keys(parts):
        parts = list(parts) + [row_swap(p, rows, 1) for p in parts]
        for mask in kv_masks:
            parts = parts + [col_swap(p, cols, mask) for p in parts]
        return parts

    def add_swapped(parts, swap):
        h = len(parts) // 2
        return [(a.astype(F32) + swap(b).astype(F32)).astype(BF) for a, b in zip(parts[:h], parts[h:])]

    def reduce_keys(parts):
        for mask in reversed(kv_masks):
            parts = add_swapped(parts, lambda p, mask=mask: col_swap(p, cols, mask))
        return add_swapped(parts, lambda p: row_swap(p, rows, 1))

    groups = [[i * cols + 2 * z + y for z in range(half) for i in range(rows)] for y in range(2)]

    def gather_weights(flat):
        full = lax.all_gather(flat, ("row", "col"), axis=0, tiled=True, axis_index_groups=groups)
        return full.reshape(half, D, flat.shape[1])

    def scatter(blocks):
        flat = blocks.reshape(half * D, blocks.shape[2])
        return lax.psum_scatter(flat, ("row", "col"), scatter_dimension=0, tiled=True, axis_index_groups=groups)

    row_bits = rows.bit_length() - 1
    order = [0]
    for b in range(row_bits):
        order = [i for j in order for i in (j, j | (1 << (row_bits - 1 - b)))]
    order = sorted(order, key=lambda i: int(format(i, f"0{row_bits}b")[::-1], 2))

    def tree_outer(pairs, part):
        return tree_blocks(pairs, D // rows, half, [r ^ i for i in part], [(c >> 1) ^ e for e in range(half)])

    def tree_add(kept, sent, bit):
        return (kept.astype(F32) + row_swap(sent, rows, bit).astype(F32)).astype(BF)

    def tree_columns(blocks):
        total = blocks[0, 0].astype(F32)
        for e in range(1, half):
            total = total + col_swap(blocks[0, e], cols, e << 1).astype(F32)
        return total

    first_w = gather_weights(
        pack([query_weight.T, key_weight.T, value_weight.T, out_weight, cross_query.T, cross_key.T, cross_value.T, cross_out])
    )
    second_w = gather_weights(jnp.concatenate([up_weight, down_weight.T], axis=1))

    step_ids = jnp.arange(steps, dtype=jnp.int32)
    onehot = (time_index[:, 0][:, None] == step_ids[None, :]).astype(F32)
    modulation = lax.dot_general(
        onehot,
        time_table.reshape(6 * feat, steps),
        (((1,), (1,)), ((), ())),
        precision=lax.Precision.HIGHEST,
        preferred_element_type=F32,
    ).reshape(2, 6, feat) + shift_table[None]
    same = [
        jnp.broadcast_to(b.reshape(1, -1, feat), (2, b.shape[0] // feat, feat))
        for b in (out_bias, cross_out_bias, down_bias, query_bias, value_bias, cross_query_bias, cross_value_bias, up_bias)
    ]
    lengths = jnp.broadcast_to(text_length.astype(F32)[:, :, None], (2, 1, feat))
    small = jnp.concatenate([modulation, lengths] + same, axis=1).transpose(0, 2, 1)
    small_high = lax.reduce_precision(small, 8, 7)
    small_rest = small - small_high
    small_mid = lax.reduce_precision(small_rest, 8, 7)
    small_low = small_rest - small_mid
    extra = jnp.concatenate(
        [text_tokens.transpose(0, 2, 1)] + [p.astype(BF) for p in (small_high, small_mid, small_low)], axis=2
    )
    arrived = send_tokens(
        jnp.concatenate([token_blocks(block_input), token_blocks(out_grad), jnp.repeat(extra, half, axis=0)], axis=2)
    )
    small_n, head = small.shape[2], 2 * width

    def small_of(value):
        parts = [value[:, head + texts + i * small_n : head + texts + (i + 1) * small_n].astype(F32) for i in range(3)]
        return parts[0] + parts[1] + parts[2]

    model_rows = small_of(arrived)
    shift_a, scale_a, gate_a, shift_m, scale_m, gate_m, length_row, out_b, cout_b, down_b = (
        model_rows[:, i : i + 1] for i in range(10)
    )
    length = length_row[0].astype(jnp.int32)
    col_rows = small_of(arrived).reshape(cols, feat, small_n)
    col_rows = jnp.concatenate(
        [
            lax.dynamic_index_in_dim(col_rows, 2 * e + (c & 1), 0, keepdims=False)[:, 10:].T.reshape(-1, 1, feat)
            for e in range(half)
        ],
        axis=1,
    )
    q_b, v_b, cq_b, cv_b = (col_rows[i].reshape(half * feat, 1) for i in range(4))
    up_b = col_rows[4:].transpose(1, 0, 2).reshape(half * ups, 1)
    text_t = arrived[:, head : head + texts]

    resid = arrived[:, :width].astype(F32)
    cot = arrived[:, width:head].astype(F32)
    heads_w, hidden_w = half * feat, half * ups
    qkv_w, out_w, cq_w, ckv_w, cout_w = (
        view_of(first_w, i * feat, (j - i) * feat) for i, j in ((0, 3), (3, 4), (4, 5), (5, 7), (7, 8))
    )
    up_w, down_w = view_of(second_w, 0, ups), view_of(second_w, ups, ups)

    def columns(*parts):
        return jnp.stack([p.reshape(half, feat) for p in parts], axis=1).reshape(-1, 1)

    def heads_in(weight, value, *biases):
        sizes = [1] if len(biases) == 1 else [1, len(biases) - 1]
        outs = [(n * heads_w, value.shape[1], BF) for n in sizes]
        return apply_in(in_kernel, weight, [value], columns(*biases), outs)

    none = jnp.zeros((heads_w,), F32)
    normed_a, inv_a = layer_norm(resid)
    attn_full = gather_pair((normed_a * (1.0 + scale_a) + shift_a).astype(BF))
    q_parts, kv_parts = zip(*(heads_in(qkv_w, p, q_b, none, v_b) for p in attn_full))
    kv_all = gather_keys(kv_parts)
    att, lse = attend_forward(q_parts, kv_all, None, half)
    branch_a = reduce_pair(out_w, att)[0] + out_b
    after_attn = resid + gate_a * branch_a
    cross_full = gather_pair(after_attn.astype(BF))
    cq_parts = [heads_in(cq_w, p, cq_b)[0] for p in cross_full]
    ckv = apply_in(in_kernel, ckv_w, [text_t], columns(none, cv_b), [(2 * heads_w, texts, BF)])
    catt, clse = attend_forward(cq_parts, ckv, length, half)
    after_cross = after_attn + reduce_pair(cout_w, catt)[0] + cout_b
    normed_m, inv_m = layer_norm(after_cross)
    mlp_full = gather_pair((normed_m * (1.0 + scale_m) + shift_m).astype(BF))
    hidden_outs = [(hidden_w, width, BF)] * 2
    *hidden, slope = apply_in(gelu_kernel, up_w, mlp_full, up_b, hidden_outs + [(hidden_w, 2 * width, F32)])

    grad_mlp = gate_m * cot
    low_full = gather_pair(grad_mlp.astype(BF))
    g_down_b = jnp.sum(grad_mlp, axis=1)
    *grad_pre, g_up_b = apply_in(slope_kernel, down_w, low_full, slope, hidden_outs + [(hidden_w, 1, F32)])

    def mlp_cover(other):
        return outer_blocks([(mlp_full, grad_pre), (low_full, [after(hidden[0], other), hidden[1]])], rows, half)

    back_in, mlp_blocks = reduce_pair(up_w, grad_pre, cover=mlp_cover)
    mlp_grads = scatter(mlp_blocks)
    back_m, g_shift_m, g_scale_m = norm_backward(back_in, normed_m, inv_m, scale_m)
    grad_cross = cot + back_m
    g_cout_b = jnp.sum(grad_cross, axis=1)
    low_cross = gather_pair(grad_cross.astype(BF))
    dcatt = [heads_in(cout_w, p, none)[0] for p in low_cross]
    dcq, dckv = attend_backward(cq_parts, ckv, length, clse, dcatt, half)

    def cross_cover(other):
        pairs = [(cross_full, dcq), ([text_t], dckv), (low_cross, [after(catt[0], other), catt[1]])]
        return outer_blocks(pairs, rows, half)

    back_cross, cross_blocks = reduce_pair(cq_w, dcq, cover=cross_cover)
    grad_res = grad_cross + back_cross
    g_cq_b = jnp.sum(sum(p.astype(F32) for p in dcq), axis=1)
    g_cv_b = jnp.sum(dckv[0].astype(F32).reshape(half, 2, feat, texts)[:, 1], axis=2)
    g_gate_a = jnp.sum(grad_res * branch_a, axis=1)
    grad_attn = gate_a * grad_res
    g_out_b = jnp.sum(grad_attn, axis=1)
    low_attn = gather_pair(grad_attn.astype(BF))
    datt = [heads_in(out_w, p, none)[0] for p in low_attn]
    dq, dkv = attend_backward(q_parts, kv_all, None, lse, datt, half)
    dkv = reduce_keys(dkv)

    def attention_pairs(tie):
        return [(attn_full, [after(dq[0], tie), dq[1]]), (attn_full, dkv), (low_attn, att)]

    def attention_cover(other):
        return tree_outer(attention_pairs(other), order[rows // 2 :])

    back_att, sent = reduce_pair(qkv_w, dq, dkv, cover=attention_cover)
    cross_grads = scatter(after(cross_blocks, mlp_grads, sent))
    tree = tree_add(tree_outer(attention_pairs(sent), order[: rows // 2]), sent, 1)
    branch_m = reduce_pair(down_w, [after(hidden[0], tree), hidden[1]])[0] + down_b
    g_gate_m = jnp.sum(cot * branch_m, axis=1)
    for b in range(1, row_bits):
        h = tree.shape[0] // 2
        tree = tree_add(tree[:h], tree[h:], 1 << b)
    att_grads = tree_columns(tree)
    g_cq, g_ck, g_cv, g_cout = unpack(cross_grads, [feat] * 4)
    g_q, g_k, g_v, g_out = unpack(att_grads, [feat] * 4)
    g_up, g_down = mlp_grads[:, :ups].astype(F32), mlp_grads[:, ups:].astype(F32)
    g_q_b = jnp.sum(sum(p.astype(F32) for p in dq), axis=1)
    g_v_b = jnp.sum(sum(p.astype(F32) for p in dkv).reshape(half, 2, feat, width)[:, 1], axis=2)
    back_a, g_shift_a, g_scale_a = norm_backward(back_att, normed_a, inv_a, scale_a)
    block_out = (after_cross + gate_m * branch_m).astype(BF)
    block_output = tokens_out(block_out)
    grad_input = tokens_out((grad_res + back_a).astype(BF))
    grad_text = apply_out(ckv_w, dckv, BF)
    grad_text = grad_text.astype(F32) + row_swap(grad_text, rows, 1).astype(F32)
    grad_text = jnp.where(at_home, grad_text, 0.0).astype(BF).reshape(cols, feat, texts)
    grad_text = lax.all_to_all(grad_text, "col", 0, 0, tiled=True)
    grad_text = jnp.sum(grad_text.reshape(2, half, feat, texts).astype(F32), axis=1).transpose(0, 2, 1)

    model_g = jnp.stack(
        [g_shift_a, g_scale_a, g_gate_a, g_shift_m, g_scale_m, g_gate_m, g_out_b, g_cout_b, g_down_b], axis=1
    )
    model_g = model_g.T.reshape(9, cols, feat).transpose(1, 0, 2)
    per_col = ups // feat
    col_g = jnp.concatenate(
        [g.reshape(half, 1, feat) for g in (g_q_b, g_v_b, g_cq_b, g_cv_b)] + [g_up_b.reshape(half, per_col, feat)],
        axis=1,
    )
    side = c & 1
    blocks = []
    for j in range(cols):
        blocks.append(jnp.where(side == (j & 1), col_g[j >> 1], 0.0))
    small_g = after(jnp.concatenate([model_g, jnp.stack(blocks)], axis=1), tree)
    small_g = lax.all_to_all(small_g, "col", 0, 0, tiled=True)
    mod_g = small_g[:, :6].reshape(2, cols // 8, 2, 2, 6, feat).sum(axis=(1, 3))
    bias_g = small_g[:, 6:].sum(axis=0)
    step_rows = jnp.broadcast_to(time_index.astype(F32), (2, feat))
    small_g = lax.all_gather(jnp.concatenate([mod_g.reshape(24, feat), bias_g, step_rows], axis=0), "row")
    step_all = small_g[:, -2:, 0].T.reshape(2 * rows).astype(jnp.int32)
    mod_g = small_g[:, :24].reshape(rows // 2, 2, 2, 2, 6, feat).sum(axis=1)
    mod_g = mod_g.transpose(1, 0, 2, 3, 4).reshape(2 * rows, 6, feat)
    bias_g = small_g[:, 24:-2].sum(axis=0)
    g_shift = mod_g.sum(axis=0)
    onehot_all = (step_all[:, None] == step_ids[None, :]).astype(F32)
    g_time = lax.dot_general(
        mod_g.reshape(2 * rows, 6 * feat),
        onehot_all,
        (((0,), (0,)), ((), ())),
        precision=lax.Precision.HIGHEST,
        preferred_element_type=F32,
    ).reshape(6, feat, steps)
    g_out_b, g_cout_b, g_down_b, g_q_b, g_v_b, g_cq_b, g_cv_b = (bias_g[i] for i in range(7))
    g_up_b = bias_g[7:].reshape(ups)
    return (
        block_output,
        grad_input,
        grad_text,
        g_shift,
        g_time,
        g_q.T,
        g_k.T,
        g_v.T,
        g_q_b,
        g_v_b,
        g_out,
        g_out_b,
        g_cq.T,
        g_ck.T,
        g_cv.T,
        g_cq_b,
        g_cv_b,
        g_cout,
        g_cout_b,
        g_up,
        g_up_b,
        g_down.T,
        g_down_b,
    )


def solution(mesh):
    return jax.shard_map(
        shards,
        mesh=mesh,
        in_specs=(
            P(None, "col", "row"),
            P(None, "row", "col"),
            P(None, "row"),
            P(None, "row"),
            P(None, "col"),
            P(None, "col", None),
            P("row", "col"),
            P("row", "col"),
            P("row", "col"),
            P("col"),
            P("col"),
            P("col", "row"),
            P("col"),
            P("row", "col"),
            P("row", "col"),
            P("row", "col"),
            P("col"),
            P("col"),
            P("col", "row"),
            P("col"),
            P("row", "col"),
            P("col"),
            P("col", "row"),
            P("col"),
            P(None, "col", "row"),
        ),
        out_specs=(
            P(None, "col", "row"),
            P(None, "col", "row"),
            P(None, "row", "col"),
            P(None, "col"),
            P(None, "col", None),
            P("row", "col"),
            P("row", "col"),
            P("row", "col"),
            P("col"),
            P("col"),
            P("col", "row"),
            P("col"),
            P("row", "col"),
            P("row", "col"),
            P("row", "col"),
            P("col"),
            P("col"),
            P("col", "row"),
            P("col"),
            P("row", "col"),
            P("col"),
            P("col", "row"),
            P("col"),
        ),
        check_vma=False,
    )
```
